32 devices in a mesh: blk: 4 (over y, x), dp: 8 (over z, core).
Axes of the slice: x: 2, y: 2, z: 4, core: 2. Of those that a mesh axis runs over, the one named last changes fastest.
Arguments:
- patches: bfloat16 [4096, 64, 256], P(('blk', 'dp')), may hold values from -6 to 6
- w_mix: bfloat16 [256, 128], replicated, may hold values from -0.375 to 0.375
- w_in: bfloat16 [2048, 512], replicated, may hold values from -0.125 to 0.125
- w_out: bfloat16 [512, 128], replicated, may hold values from -0.25 to 0.25
- partner_dev: int32 [4096], P(('blk', 'dp')), may hold values from 0 to 7, as said below
- partner_row: int32 [4096], P(('blk', 'dp')), may hold values from 0 to 127, as said below
Outputs:
- loss_rows: float32 [4096], P(('blk', 'dp'))
- grad_mix: float32 [256, 128], replicated
- grad_in: float32 [2048, 512], replicated
- grad_out: float32 [512, 128], replicated
The draws below stay inside these ranges and needn't reach their ends.
Inputs may be any that keep to these rules, and one draw needn't show every extreme that they name: Among one device's rows every dp index appears as partner_dev exactly 128/8 times. Over the rows that share a blk index, the pairs (partner_dev, partner_row) name every pair of dp index and row of a device exactly once.
All inputs are finite; a program needn't handle non-finite values.
Results may differ from the reference program's by a relative error of at most 0.012.
The reference program's roundings to bfloat16 on the way count: a program that leaves them out, or rounds other values in their place, can miss the bound.
Values may be sent and summed in bfloat16 or wider, within the bound.
No kernel may reach another device: no remote copies, remote signals or barrier semaphores. Data moves between devices by JAX's collectives and lax.ppermute only.
A program may use at most 64 MiB of HBM per device.

```python
import math
import jax
import jax.numpy as jnp
from jax import lax

ANGLES = 64
FILTERS = 128
HIDDEN_SIZE = 512
EMBED = 128
PATCHES = 128
LANES = 256
FEATS = 2048
PEERS = 8
CYCLE = 4
ROWS = 4096
N_BLK = 4
N_DP = 8


def partner_table(key):
    base = jax.random.fold_in(key, 17)
    per_peer = PATCHES // PEERS

    def one_cycle(subkey):
        send_key, recv_key = jax.random.split(subkey)
        send_perm = jax.vmap(lambda each: jax.random.permutation(each, PATCHES))(jax.random.split(send_key, PEERS))
        recv_perm = jax.vmap(lambda each: jax.random.permutation(each, PATCHES))(jax.random.split(recv_key, PEERS))
        sender_index = jnp.broadcast_to(jnp.arange(PEERS, dtype=jnp.int32)[:, None], (PEERS, PATCHES))
        slot = jnp.broadcast_to(jnp.arange(PATCHES, dtype=jnp.int32)[None, :], (PEERS, PATCHES))
        target = jnp.mod(sender_index + slot // per_peer, PEERS)
        target_row = recv_perm[target, slot]
        devices = jnp.zeros((PEERS, PATCHES), jnp.int32).at[sender_index, send_perm].set(target)
        rows_out = jnp.zeros((PEERS, PATCHES), jnp.int32).at[sender_index, send_perm].set(target_row)
        return (devices, rows_out)
    devices, rows_out = jax.vmap(one_cycle)(jax.random.split(base, CYCLE))
    return (devices.reshape(-1), rows_out.reshape(-1))


def draw_partner_dev(key, part):
    return partner_table(key)[0]


def draw_partner_row(key, part):
    return partner_table(key)[1]


def levels(stream_key, shape, cuts, least, top_value):
    def one(dim, shards_of):
        steps = jax.random.uniform(jax.random.fold_in(jax.random.fold_in(stream_key, 6), dim), (shards_of,), jnp.float32, least / len(cuts), top_value / len(cuts))
        return jnp.repeat(jnp.exp(steps), shape[dim] // shards_of).reshape((-1,) + (1,) * (len(shape) - dim - 1))

    factor_of = one(*cuts[0])
    for cut in cuts[1:]:
        factor_of = factor_of * one(*cut)
    return factor_of


def scatter_about(key, dims, scale, limit, pieces=(), kind=jnp.bfloat16):
    gain = levels(key, dims, pieces, -0.22, 0.18) if pieces else 1.0
    values = jax.random.normal(key, dims, jnp.float32) * scale * gain
    return jnp.minimum(jnp.maximum(values, -limit), limit).astype(kind)


def setup_inputs(seed: int = 0) -> dict:
    key_list = jax.random.split(jax.random.key(seed), 7)
    patches = scatter_about(key_list[0], (ROWS, ANGLES, LANES), 1.0, 6.0, ((0, 32),))
    w_mix = scatter_about(key_list[1], (LANES, FILTERS), LANES ** -0.5, 0.375)
    w_in = scatter_about(key_list[2], (FEATS, HIDDEN_SIZE), FEATS ** -0.5, 0.125)
    w_out = scatter_about(key_list[3], (HIDDEN_SIZE, EMBED), HIDDEN_SIZE ** -0.5, 0.25)
    partner_dev = draw_partner_dev(jax.random.fold_in(key_list[6], 71), 0)
    partner_row = draw_partner_row(jax.random.fold_in(key_list[6], 71), 0)
    return dict(patches=patches, w_mix=w_mix, w_in=w_in, w_out=w_out, partner_dev=partner_dev, partner_row=partner_row)


SCALE = 10.0

def dft_table(length, freqs):
    angle_idx = jnp.arange(length, dtype=jnp.int32)
    freq_idx = jnp.arange(freqs, dtype=jnp.int32)
    phase = jnp.mod(freq_idx[None, :] * angle_idx[:, None], length).astype(jnp.float32) * (2.0 * math.pi / length)
    return jnp.concatenate([jnp.cos(phase), -jnp.sin(phase)], axis=1).astype(jnp.bfloat16)

def encode(block, w_mix, w_in, w_out):
    count, length, lanes = block.shape
    filters = w_mix.shape[1]
    freqs = w_in.shape[0] // filters
    angle_table = dft_table(length, freqs)
    spec = jnp.einsum('pac,ak->pkc', block.astype(jnp.float32), angle_table.astype(jnp.float32), precision=lax.Precision.HIGHEST).astype(jnp.bfloat16)
    mixed = jnp.dot(spec.reshape(-1, lanes), w_mix, preferred_element_type=jnp.float32).reshape(count, 2 * freqs, filters)
    real_part = mixed[:, :freqs]
    imag_part = mixed[:, freqs:]
    powers = real_part * real_part + imag_part * imag_part
    features = jnp.log1p(powers).reshape(count, -1)
    mean_removed = features - lax.optimization_barrier(jnp.mean(features, axis=1, keepdims=True))
    reciprocal_scale = lax.rsqrt(lax.optimization_barrier(jnp.mean(mean_removed * mean_removed, axis=1, keepdims=True)) + 1e-05)
    normed = (mean_removed * reciprocal_scale).astype(jnp.bfloat16)
    preact = jnp.dot(normed, w_in, preferred_element_type=jnp.float32)
    hidden = jax.nn.silu(preact).astype(jnp.bfloat16)
    raw_embed = jnp.dot(hidden, w_out, preferred_element_type=jnp.float32)
    norms = jnp.sqrt(lax.optimization_barrier(jnp.sum(raw_embed * raw_embed, axis=1, keepdims=True)) + 1e-06)
    unit32 = raw_embed / norms
    saved = (spec, real_part, imag_part, powers, mean_removed, reciprocal_scale, normed, preact, hidden, unit32, norms)
    return (unit32.astype(jnp.bfloat16), saved)

def encode_back(grad_units, saved, w_in, w_out):
    spec, real_part, imag_part, powers, mean_removed, reciprocal_scale, normed, preact, hidden, unit32, norms = saved
    count = spec.shape[0]
    lanes = spec.shape[2]
    grad_raw = ((grad_units - unit32 * lax.optimization_barrier(jnp.sum(unit32 * grad_units, axis=1, keepdims=True))) / norms).astype(jnp.bfloat16)
    g_out = jnp.dot(hidden.T, grad_raw, preferred_element_type=jnp.float32)
    grad_hid = jnp.dot(grad_raw, w_out.T, preferred_element_type=jnp.float32)
    sigm = jax.nn.sigmoid(preact)
    grad_pre = (grad_hid * sigm * (1.0 + preact * (1.0 - sigm))).astype(jnp.bfloat16)
    g_in = jnp.dot(normed.T, grad_pre, preferred_element_type=jnp.float32)
    norm_gradient = jnp.dot(grad_pre, w_in.T, preferred_element_type=jnp.float32)
    normalized_input = mean_removed * reciprocal_scale
    feature_gradient = reciprocal_scale * (norm_gradient - lax.optimization_barrier(jnp.mean(norm_gradient, axis=1, keepdims=True)) - normalized_input * lax.optimization_barrier(jnp.mean(norm_gradient * normalized_input, axis=1, keepdims=True)))
    grad_pow = feature_gradient.reshape(powers.shape) / (1.0 + powers)
    grad_mixed = jnp.concatenate([2.0 * real_part * grad_pow, 2.0 * imag_part * grad_pow], axis=1).astype(jnp.bfloat16)
    g_mix = jnp.dot(spec.reshape(-1, lanes).T, grad_mixed.reshape(-1, grad_mixed.shape[2]), preferred_element_type=jnp.float32)
    return (g_mix, g_in, g_out)

def group_terms(pair):
    key_rows, spos = pair
    scores = SCALE * jnp.dot(key_rows, key_rows.T, preferred_element_type=jnp.float32)
    width = key_rows.shape[0]
    diagonal = jnp.arange(width)[:, None] == jnp.arange(width)[None, :]
    expo = jnp.where(diagonal, jnp.float32(0.0), jnp.exp(scores))
    zneg = lax.optimization_barrier(jnp.sum(expo, axis=1))
    totals = jnp.exp(spos) + zneg
    numer = jnp.dot(expo.astype(jnp.bfloat16), key_rows, preferred_element_type=jnp.float32)
    weights = (expo / totals[:, None]).astype(jnp.bfloat16)
    keyterm = jnp.dot(weights.T, key_rows, preferred_element_type=jnp.float32)
    return (totals, numer, keyterm)

def reference(patches, w_mix, w_in, w_out, partner_dev, partner_row):
    blocks = patches.reshape(N_BLK * N_DP, PATCHES, ANGLES, LANES)
    units = lax.map(lambda block: encode(block, w_mix, w_in, w_out)[0], blocks)
    units4 = units.reshape(N_BLK, N_DP, PATCHES, EMBED)
    peer_dev = partner_dev.reshape(N_BLK, N_DP, PATCHES)
    peer_row = partner_row.reshape(N_BLK, N_DP, PATCHES)
    blk_ids = jnp.broadcast_to(jnp.arange(N_BLK, dtype=jnp.int32)[:, None, None], peer_dev.shape)
    positive = units4[blk_ids, peer_dev, peer_row]
    spos = SCALE * lax.optimization_barrier(jnp.sum(units4.astype(jnp.float32) * positive.astype(jnp.float32), axis=-1))
    grouped = jnp.transpose(units4, (1, 0, 2, 3)).reshape(N_DP, N_BLK * PATCHES, EMBED)
    spos_grouped = jnp.transpose(spos, (1, 0, 2)).reshape(N_DP, N_BLK * PATCHES)
    totals, numer, keyterm = lax.map(group_terms, (grouped, spos_grouped))
    totals = jnp.transpose(totals.reshape(N_DP, N_BLK, PATCHES), (1, 0, 2))
    numer = jnp.transpose(numer.reshape(N_DP, N_BLK, PATCHES, EMBED), (1, 0, 2, 3))
    keyterm = jnp.transpose(keyterm.reshape(N_DP, N_BLK, PATCHES, EMBED), (1, 0, 2, 3))
    loss_rows = (jnp.log(totals) - spos).reshape(-1)
    coef = SCALE / PATCHES
    ppos = jnp.exp(spos) / totals
    partner_grad = coef * (ppos - 1.0)[..., None] * units4.astype(jnp.float32)
    from_partner = jnp.zeros(units4.shape, jnp.float32).at[blk_ids, peer_dev, peer_row].add(partner_grad)
    grad_units = coef * ((ppos - 1.0)[..., None] * positive.astype(jnp.float32) + numer / totals[..., None]) + coef * keyterm + from_partner
    grad_units = grad_units.reshape(N_BLK * N_DP, PATCHES, EMBED)

    def accumulate(carry, pair):
        block, grad_block = pair
        unused, saved = encode(block, w_mix, w_in, w_out)
        g_mix, g_in, g_out = encode_back(grad_block, saved, w_in, w_out)
        return ((carry[0] + g_mix, carry[1] + g_in, carry[2] + g_out), None)
    start = (jnp.zeros((LANES, FILTERS), jnp.float32), jnp.zeros((FEATS, HIDDEN_SIZE), jnp.float32), jnp.zeros((HIDDEN_SIZE, EMBED), jnp.float32))
    sums, unused = lax.scan(accumulate, start, (blocks, grad_units))
    return (loss_rows, sums[0], sums[1], sums[2])
```

```python
import math

import jax
import jax.numpy as jnp
from jax import lax
from jax.sharding import PartitionSpec as P

SCALE = 10.0


def dft_table(length, freqs):
    angle_idx = jnp.arange(length, dtype=jnp.int32)
    freq_idx = jnp.arange(freqs, dtype=jnp.int32)
    phase = jnp.mod(freq_idx[None, :] * angle_idx[:, None], length).astype(jnp.float32) * (
        2.0 * math.pi / length
    )
    return jnp.concatenate([jnp.cos(phase), -jnp.sin(phase)], axis=1).astype(jnp.bfloat16)


def encode(block, w_mix, w_in, w_out):
    count, length, lanes = block.shape
    filters = w_mix.shape[1]
    freqs = w_in.shape[0] // filters
    angle_table = dft_table(length, freqs)
    spec = jnp.einsum("pac,ak->pkc", block, angle_table, preferred_element_type=jnp.float32).astype(
        jnp.bfloat16
    )
    mixed = jnp.dot(spec.reshape(-1, lanes), w_mix, preferred_element_type=jnp.float32).reshape(
        count, 2 * freqs, filters
    )
    real_part = mixed[:, :freqs]
    imag_part = mixed[:, freqs:]
    powers = real_part * real_part + imag_part * imag_part
    features = jnp.log1p(powers).reshape(count, -1)
    mean_removed = features - jnp.mean(features, axis=1, keepdims=True)
    reciprocal_scale = lax.rsqrt(
        jnp.mean(mean_removed * mean_removed, axis=1, keepdims=True) + 1e-05
    )
    normed = (mean_removed * reciprocal_scale).astype(jnp.bfloat16)
    preact = jnp.dot(normed, w_in, preferred_element_type=jnp.float32)
    hidden = jax.nn.silu(preact).astype(jnp.bfloat16)
    raw_embed = jnp.dot(hidden, w_out, preferred_element_type=jnp.float32)
    norms = jnp.sqrt(jnp.sum(raw_embed * raw_embed, axis=1, keepdims=True) + 1e-06)
    unit32 = raw_embed / norms
    saved = (
        spec,
        real_part,
        imag_part,
        powers,
        mean_removed,
        reciprocal_scale,
        normed,
        preact,
        hidden,
        unit32,
        norms,
    )
    return (unit32.astype(jnp.bfloat16), saved)


def back_upper(grad_units, saved, w_in, w_out):
    (
        spec,
        real_part,
        imag_part,
        powers,
        mean_removed,
        reciprocal_scale,
        normed,
        preact,
        hidden,
        unit32,
        norms,
    ) = saved
    grad_raw = (
        (grad_units - unit32 * jnp.sum(unit32 * grad_units, axis=1, keepdims=True)) / norms
    ).astype(jnp.bfloat16)
    g_out = jnp.dot(hidden.T, grad_raw, preferred_element_type=jnp.float32)
    grad_hid = jnp.dot(grad_raw, w_out.T, preferred_element_type=jnp.float32)
    sigm = jax.nn.sigmoid(preact)
    grad_pre = (grad_hid * sigm * (1.0 + preact * (1.0 - sigm))).astype(jnp.bfloat16)
    g_in = jnp.dot(normed.T, grad_pre, preferred_element_type=jnp.float32)
    norm_gradient = jnp.dot(grad_pre, w_in.T, preferred_element_type=jnp.float32)
    return (g_in, g_out, norm_gradient)


def back_lower(norm_gradient, saved):
    (
        spec,
        real_part,
        imag_part,
        powers,
        mean_removed,
        reciprocal_scale,
        normed,
        preact,
        hidden,
        unit32,
        norms,
    ) = saved
    lanes = spec.shape[2]
    normalized_input = mean_removed * reciprocal_scale
    feature_gradient = reciprocal_scale * (
        norm_gradient
        - jnp.mean(norm_gradient, axis=1, keepdims=True)
        - normalized_input * jnp.mean(norm_gradient * normalized_input, axis=1, keepdims=True)
    )
    grad_pow = feature_gradient.reshape(powers.shape) / (1.0 + powers)
    grad_mixed = jnp.concatenate(
        [2.0 * real_part * grad_pow, 2.0 * imag_part * grad_pow], axis=1
    ).astype(jnp.bfloat16)
    return jnp.dot(
        spec.reshape(-1, lanes).T,
        grad_mixed.reshape(-1, grad_mixed.shape[2]),
        preferred_element_type=jnp.float32,
    )


def negative_part(units, piece, row_ids):
    scores = SCALE * jnp.dot(units, piece.T, preferred_element_type=jnp.float32)
    column = jnp.arange(piece.shape[0], dtype=jnp.int32)
    expo = jnp.where(column[None, :] == row_ids[:, None], jnp.float32(0.0), jnp.exp(scores))
    return (
        jnp.sum(expo, axis=1),
        jnp.dot(expo.astype(jnp.bfloat16), piece, preferred_element_type=jnp.float32),
    )


def key_part(units, piece, tot_piece, row_ids):
    scores = SCALE * jnp.dot(piece, units.T, preferred_element_type=jnp.float32)
    column = jnp.arange(piece.shape[0], dtype=jnp.int32)
    expo = jnp.where(column[:, None] == row_ids[None, :], jnp.float32(0.0), jnp.exp(scores))
    weights = (expo / tot_piece[:, None]).astype(jnp.bfloat16)
    return jnp.dot(weights.T, piece, preferred_element_type=jnp.float32)


def hop_bits(axis):
    size = lax.axis_size(axis)
    steps = size.bit_length() - 1
    assert size == 1 << steps
    return [1 << step for step in range(steps)]


def swap(block, axis, bit):
    size = lax.axis_size(axis)
    return lax.ppermute(block, axis, [(src, src ^ bit) for src in range(size)])


def side(axis, bit):
    return (lax.axis_index(axis) & bit) != 0


def scatter_sum(part, route):
    for axis, bit in route:
        half = part.shape[0] // 2
        upper = side(axis, bit)
        low, high = part[:half], part[half:]
        away = jnp.where(upper, low, high).astype(jnp.bfloat16)
        kept = jnp.where(upper, high, low)
        part = kept + swap(away, axis, bit).astype(jnp.float32)
    return part


def gather_back(part, route):
    for axis, bit in reversed(route):
        other = swap(part, axis, bit)
        upper = side(axis, bit)
        part = jnp.concatenate(
            [jnp.where(upper, other, part), jnp.where(upper, part, other)], axis=0
        )
    return part


def reduce_all(g_mix, g_in, g_out):
    width = g_in.shape[1]
    pieces = [g_mix.reshape(-1, width), g_out.reshape(-1, width)]
    small = jnp.concatenate(pieces, axis=0)
    devices = lax.axis_size("blk") * lax.axis_size("dp")
    unit = 8 * devices
    total = -(-(g_in.shape[0] + small.shape[0]) // (2 * unit)) * 2 * unit
    pad = total - g_in.shape[0] - small.shape[0]
    whole = jnp.concatenate([g_in, small, jnp.zeros((pad, width), jnp.float32)], axis=0)
    across = [("blk", bit) for bit in hop_bits("blk")]
    along = [("dp", bit) for bit in hop_bits("dp")]
    routes = [along[:1] + across + along[1:], along[:1] + across[::-1] + along[1:]]
    half = total // 2
    done = [
        gather_back(scatter_sum(whole[k * half : (k + 1) * half], route).astype(jnp.bfloat16), route)
        for k, route in enumerate(routes)
    ]
    whole = jnp.concatenate(done, axis=0).astype(jnp.float32)
    rows = g_in.shape[0]
    mix_rows = pieces[0].shape[0]
    out_rows = pieces[1].shape[0]
    return (
        whole[rows : rows + mix_rows].reshape(g_mix.shape),
        whole[:rows],
        whole[rows + mix_rows : rows + mix_rows + out_rows].reshape(g_out.shape),
    )


def on_device(patches, w_mix, w_in, w_out, partner_dev, partner_row):
    count = patches.shape[0]
    embed = w_out.shape[1]
    units, saved = encode(patches, w_mix, w_in, w_out)
    peers = lax.axis_size("dp")
    per_peer = count // peers
    sorted_positions = jnp.argsort(partner_dev, stable=True)
    inverse = jnp.argsort(sorted_positions, stable=True)
    wanted = partner_row[sorted_positions].reshape(peers, per_peer)
    asked = lax.all_to_all(wanted, "dp", split_axis=0, concat_axis=0, tiled=True)
    picked = units[asked]
    returned_rows = lax.all_to_all(picked, "dp", split_axis=0, concat_axis=0, tiled=True)
    positive = returned_rows.reshape(count, embed)[inverse]
    spos = SCALE * jnp.sum(units.astype(jnp.float32) * positive.astype(jnp.float32), axis=1)
    row_ids = lax.axis_index("blk") * count + jnp.arange(count, dtype=jnp.int32)
    zpart, npart = negative_part(units, lax.all_gather(units, "blk", axis=0, tiled=True), row_ids)
    totals = jnp.exp(spos) + zpart
    all_totals = lax.all_gather(totals, "blk", axis=0, tiled=True)
    keyterm = key_part(units, lax.all_gather(units, "blk", axis=0, tiled=True), all_totals, row_ids)
    loss_rows = jnp.log(totals) - spos
    coef = SCALE / count
    ppos = jnp.exp(spos) / totals
    partner_grad = coef * (ppos - 1.0)[:, None] * units.astype(jnp.float32)
    outgoing = partner_grad[sorted_positions].reshape(peers, per_peer, embed)
    incoming = lax.all_to_all(outgoing, "dp", split_axis=0, concat_axis=0, tiled=True)
    from_partner = (
        jnp.zeros((count, embed), jnp.float32)
        .at[asked.reshape(-1)]
        .add(incoming.reshape(-1, embed))
    )
    grad_units = (
        coef * ((ppos - 1.0)[:, None] * positive.astype(jnp.float32) + npart / totals[:, None])
        + coef * keyterm
        + from_partner
    )
    g_in, g_out, norm_gradient = back_upper(grad_units, saved, w_in, w_out)
    g_mix = back_lower(norm_gradient, saved)
    g_mix, g_in, g_out = reduce_all(g_mix, g_in, g_out)
    return (loss_rows, g_mix, g_in, g_out)


def solution(mesh):
    placed = (P(("blk", "dp"), None, None), P(), P(), P(), P(("blk", "dp")), P(("blk", "dp")))
    return jax.shard_map(
        on_device,
        mesh=mesh,
        in_specs=placed,
        out_specs=(P(("blk", "dp")), P(), P(), P()),
        check_vma=False,
    )
```

```python
import functools
import math

import jax
import jax.numpy as jnp
import numpy as np
from jax import lax
from jax.experimental import pallas as pl
from jax.experimental.pallas import tpu as pltpu
from jax.sharding import PartitionSpec as P

SCALE = 10.0
SUB = 8
BF16 = jnp.bfloat16
F32 = jnp.float32
VMEM = pl.BlockSpec(memory_space=pltpu.VMEM)
ANY = pl.BlockSpec(memory_space=pl.ANY)


def shape(dims, dtype):
    return jax.ShapeDtypeStruct(tuple(dims), dtype)


def mm(left, right):
    return jnp.dot(left, right, preferred_element_type=F32)


def mm_nt(left, right):
    return lax.dot_general(left, right, (((1,), (1,)), ((), ())), preferred_element_type=F32)


def mm_tn(left, right):
    return lax.dot_general(left, right, (((0,), (0,)), ((), ())), preferred_element_type=F32)


def params(mib):
    return pltpu.CompilerParams(vmem_limit_bytes=mib << 20)


def cost(flops, nbytes):
    return pl.CostEstimate(flops=int(flops), bytes_accessed=int(nbytes), transcendentals=0)


def angle_basis(length, freqs):
    phase = np.mod(np.outer(np.arange(freqs), np.arange(length)), length).astype(np.float32)
    phase = phase * np.float32(2.0 * math.pi / length)
    table = np.concatenate([np.cos(phase), -np.sin(phase)], axis=0).astype(np.float32)
    basis = np.einsum("ka,pq->kpqa", table, np.eye(SUB, dtype=np.float32))
    return jnp.asarray(basis.reshape(2 * freqs * SUB, SUB * length), BF16)


def encode_kernel(
    freqs,
    patch_ref,
    basis_ref,
    mix_ref,
    out_w_ref,
    in_hbm,
    spec_ref,
    mixed_ref,
    units_ref,
    unit32_ref,
    norm_ref,
    rscale_ref,
    normed_ref,
    preact_ref,
    hidden_ref,
    feat,
    in_w,
    sem,
):
    step = pl.program_id(0)
    load = pltpu.make_async_copy(in_hbm, in_w, sem)

    @pl.when(step == 0)
    def _():
        load.start()

    per, length, lanes = patch_ref.shape
    groups = per // SUB
    filters = mix_ref.shape[1]
    half = freqs * SUB
    for s in range(groups):
        block = patch_ref[s * SUB : (s + 1) * SUB].reshape(SUB * length, lanes)
        spec = mm(basis_ref[...], block).astype(BF16)
        spec_ref[s] = spec
        mixed = mm(spec, mix_ref[...])
        mixed_ref[s] = mixed
        real_part, imag_part = mixed[:half], mixed[half:]
        piece = jnp.log1p(real_part * real_part + imag_part * imag_part)
        base = pl.multiple_of((step * groups + s) * SUB, SUB)
        for k in range(freqs):
            feat[pl.ds(base, SUB), k * filters : (k + 1) * filters] = piece[
                k * SUB : (k + 1) * SUB
            ]

    @pl.when(step == pl.num_programs(0) - 1)
    def _():
        load.wait()
        features = feat[...]
        removed = features - jnp.mean(features, axis=1, keepdims=True)
        rscale = lax.rsqrt(jnp.mean(removed * removed, axis=1, keepdims=True) + 1e-05)
        normed = (removed * rscale).astype(BF16)
        normed_ref[...] = normed
        rscale_ref[...] = jnp.broadcast_to(rscale, rscale_ref.shape)
        preact = mm(normed, in_w[...])
        preact_ref[...] = preact
        hidden = (preact * jax.nn.sigmoid(preact)).astype(BF16)
        hidden_ref[...] = hidden
        raw = mm(hidden, out_w_ref[...])
        norms = jnp.sqrt(jnp.sum(raw * raw, axis=1, keepdims=True) + 1e-06)
        norm_ref[...] = jnp.broadcast_to(norms, norm_ref.shape)
        unit32 = raw / norms
        unit32_ref[...] = unit32
        units_ref[...] = unit32.astype(BF16)


def encode(patches, w_mix, w_in, w_out):
    count, length, lanes = patches.shape
    filters = w_mix.shape[1]
    feats, width = w_in.shape
    embed = w_out.shape[1]
    freqs = feats // filters
    per = 2 * SUB
    groups = count // SUB
    rows = 2 * freqs * SUB

    def whole(*dims):
        return pl.BlockSpec(dims, lambda i: (0,) * len(dims))

    outs = [
        (shape((groups, rows, lanes), BF16), pl.BlockSpec((per // SUB, rows, lanes), lambda i: (i, 0, 0))),
        (shape((groups, rows, filters), F32), pl.BlockSpec((per // SUB, rows, filters), lambda i: (i, 0, 0))),
        (shape((count, embed), BF16), whole(count, embed)),
        (shape((count, embed), F32), whole(count, embed)),
        (shape((count, 128), F32), whole(count, 128)),
        (shape((count, 128), F32), whole(count, 128)),
        (shape((count, feats), BF16), whole(count, feats)),
        (shape((count, width), F32), whole(count, width)),
        (shape((count, width), BF16), whole(count, width)),
    ]
    return pl.pallas_call(
        functools.partial(encode_kernel, freqs),
        grid=(count // per,),
        in_specs=[
            pl.BlockSpec((per, length, lanes), lambda i: (i, 0, 0)),
            whole(rows, SUB * length),
            whole(lanes, filters),
            whole(width, embed),
            ANY,
        ],
        out_shape=[each for each, _ in outs],
        out_specs=[spec for _, spec in outs],
        scratch_shapes=[
            pltpu.VMEM((count, feats), F32),
            pltpu.VMEM((feats, width), BF16),
            pltpu.SemaphoreType.DMA,
        ],
        compiler_params=params(24),
        cost_estimate=cost(3e9, 14e6),
    )(patches, angle_basis(length, freqs), w_mix, w_out, w_in)


def negative_kernel(size, *refs):
    pieces, (expo_ref, zneg_ref, numer_ref) = refs[:size], refs[size:]
    units = pieces[0][...]
    count = units.shape[0]
    zneg = numer = None
    for i, piece in enumerate(pieces):
        keys = piece[...]
        expo = jnp.exp(SCALE * mm_nt(units, keys))
        if i == 0:
            row = lax.broadcasted_iota(jnp.int32, expo.shape, 0)
            col = lax.broadcasted_iota(jnp.int32, expo.shape, 1)
            expo = jnp.where(row == col, 0.0, expo)
        expo_ref[:, i * count : (i + 1) * count] = expo
        total = jnp.sum(expo, axis=1, keepdims=True)
        term = mm(expo.astype(BF16), keys)
        zneg = total if zneg is None else zneg + total
        numer = term if numer is None else numer + term
    zneg_ref[...] = jnp.broadcast_to(zneg, zneg_ref.shape)
    numer_ref[...] = numer


def negatives(pieces):
    count, embed = pieces[0].shape
    size = len(pieces)
    return pl.pallas_call(
        functools.partial(negative_kernel, size),
        in_specs=[VMEM] * size,
        out_shape=[
            shape((count, size * count), F32),
            shape((count, 128), F32),
            shape((count, embed), F32),
        ],
        out_specs=[VMEM] * 3,
        compiler_params=params(8),
        cost_estimate=cost(4e8, 1e6),
    )(*pieces)


def as_rows(column, count):
    return jnp.broadcast_to(column, (column.shape[0], count)).T


def positive_kernel(
    dev_ref, row_ref, even_ref, odd_ref, zneg_ref, numer_ref, local_ref, stats_ref, loss_ref
):
    count = dev_ref.shape[1]
    me = lax.axis_index("dp")
    step = dev_ref[...] ^ me
    place = ((step & 1) * even_ref.shape[0] + (step >> 1) * count + row_ref[...]).astype(F32)
    place = jnp.broadcast_to(place, (count, count)).T
    lane = lax.broadcasted_iota(jnp.int32, (count, count), 1).astype(F32)
    positive = None
    blocks = even_ref.shape[0] // count
    for i in range(2 * blocks):
        source = even_ref if i < blocks else odd_ref
        at = (i % blocks) * count
        hit = jnp.where(place - float(i * count) == lane, 1.0, 0.0).astype(BF16)
        term = mm(hit, source[at : at + count, :])
        positive = term if positive is None else positive + term
    units = even_ref[:count, :].astype(F32)
    spos = SCALE * jnp.sum(units * positive, axis=1, keepdims=True)
    top = jnp.exp(spos)
    totals = top + zneg_ref[:, :1]
    less = top / totals - 1.0
    coef = SCALE / count
    local_ref[...] = coef * (less * positive + numer_ref[...] / totals)
    loss_ref[...] = as_rows(jnp.log(totals) - spos, count)[:1]
    stats_ref[...] = jnp.zeros(stats_ref.shape, F32)
    stats_ref[0:1, :] = as_rows(totals, count)[:1]
    stats_ref[1:2, :] = as_rows(coef * less, count)[:1]
    stats_ref[2:3, :] = (dev_ref[...] * count + row_ref[...]).astype(F32)


def positives(partner_dev, partner_row, even, odd, zneg, numer):
    count, embed = numer.shape
    return pl.pallas_call(
        positive_kernel,
        in_specs=[VMEM] * 6,
        out_shape=[shape((count, embed), F32), shape((SUB, count), F32), shape((1, count), F32)],
        out_specs=[VMEM] * 3,
        compiler_params=params(8),
        cost_estimate=cost(4e8, 1e6),
    )(partner_dev.reshape(1, count), partner_row.reshape(1, count), even, odd, zneg, numer)


def upper_kernel(size, *refs):
    pieces, rest = refs[:size], refs[size:]
    stats, rest = rest[:size], rest[size:]
    (
        expo_ref,
        even_ref,
        odd_ref,
        even_stats,
        odd_stats,
        local_ref,
        unit32_ref,
        norm_ref,
        out_w_ref,
        preact_ref,
        pay_ref,
    ) = rest
    count, embed = local_ref.shape
    coef = SCALE / count
    keyterm = None
    for i in range(size):
        expo = expo_ref[:, i * count : (i + 1) * count]
        weights = (expo / stats[i][0:1, :]).astype(BF16)
        term = mm(weights, pieces[i][...])
        keyterm = term if keyterm is None else keyterm + term
    mine = lax.axis_index("dp") * count + lax.broadcasted_iota(jnp.int32, (count, count), 0)
    mine = mine.astype(F32)
    blocks = even_ref.shape[0] // count
    chosen = amount = None
    for i in range(2 * blocks):
        source, table = (even_ref, even_stats) if i < blocks else (odd_ref, odd_stats)
        j = i % blocks
        hit = table[j * SUB + 2 : j * SUB + 3, :] == mine
        share = jnp.where(hit, table[j * SUB + 1 : j * SUB + 2, :], 0.0)
        term = mm(jnp.where(hit, 1.0, 0.0).astype(BF16), source[j * count : (j + 1) * count, :])
        chosen = term if chosen is None else chosen + term
        amount = share if amount is None else amount + share
    back = jnp.sum(amount, axis=1, keepdims=True) * chosen
    grad_units = local_ref[...] + coef * keyterm + back
    unit32 = unit32_ref[...]
    along = jnp.sum(unit32 * grad_units, axis=1, keepdims=True)
    grad_raw = ((grad_units - unit32 * along) / norm_ref[:, :1]).astype(BF16)
    grad_hid = mm_nt(grad_raw, out_w_ref[...])
    preact = preact_ref[...]
    sigm = jax.nn.sigmoid(preact)
    width = preact.shape[1]
    pay_ref[:, :width] = (grad_hid * sigm * (1.0 + preact * (1.0 - sigm))).astype(BF16)
    pay_ref[:, width:] = grad_raw


def upper(pieces, stats, expo, even, odd, even_stats, odd_stats, local, unit32, norms, w_out, preact):
    count, embed = local.shape
    size = len(pieces)
    args = [*pieces, *stats, expo, even, odd, even_stats, odd_stats, local, unit32, norms, w_out, preact]
    return pl.pallas_call(
        functools.partial(upper_kernel, size),
        in_specs=[VMEM] * len(args),
        out_shape=shape((count, preact.shape[1] + embed), BF16),
        out_specs=VMEM,
        compiler_params=params(8),
        cost_estimate=cost(4e8, 2e6),
    )(*args)


def lower_kernel(
    freqs,
    pay_ref,
    normed_ref,
    rscale_ref,
    in_hbm,
    mixed_hbm,
    spec_hbm,
    g_mix_ref,
    in_w,
    mixed,
    spec,
    grad_feat,
    sems,
):
    loads = [
        pltpu.make_async_copy(source, target, sems.at[i])
        for i, (source, target) in enumerate([(in_hbm, in_w), (mixed_hbm, mixed), (spec_hbm, spec)])
    ]
    for each in loads:
        each.start()
    width = in_w.shape[1]
    loads[0].wait()
    grad_norm = mm_nt(pay_ref[:, :width], in_w[...])
    xhat = normed_ref[...].astype(F32)
    mean = jnp.mean(grad_norm, axis=1, keepdims=True)
    slope = jnp.mean(grad_norm * xhat, axis=1, keepdims=True)
    grad_feat[...] = rscale_ref[:, :1] * (grad_norm - mean - xhat * slope)
    loads[1].wait()
    loads[2].wait()
    groups, rows, filters = mixed.shape
    half = freqs * SUB

    def one(g, total):
        real_part, imag_part = mixed[g, :half], mixed[g, half:]
        powers = real_part * real_part + imag_part * imag_part
        base = pl.multiple_of(g * SUB, SUB)
        grads = jnp.concatenate(
            [grad_feat[pl.ds(base, SUB), k * filters : (k + 1) * filters] for k in range(freqs)],
            axis=0,
        )
        share = 2.0 * grads / (1.0 + powers)
        grad_mixed = jnp.concatenate([real_part * share, imag_part * share], axis=0).astype(BF16)
        return total + mm_tn(grad_mixed, spec[g])

    total = lax.fori_loop(0, groups, one, jnp.zeros((filters, spec.shape[2]), F32), unroll=4)
    g_mix_ref[...] = total.T


def lower(pay, normed, rscale, w_in, mixed, spec, freqs):
    count, feats = normed.shape
    groups, rows, filters = mixed.shape
    lanes = spec.shape[2]
    return pl.pallas_call(
        functools.partial(lower_kernel, freqs),
        in_specs=[VMEM] * 3 + [ANY] * 3,
        out_shape=shape((lanes, filters), F32),
        out_specs=VMEM,
        scratch_shapes=[
            pltpu.VMEM(w_in.shape, BF16),
            pltpu.VMEM(mixed.shape, F32),
            pltpu.VMEM(spec.shape, BF16),
            pltpu.VMEM((count, feats), F32),
            pltpu.SemaphoreType.DMA((3,)),
        ],
        compiler_params=params(24),
        cost_estimate=cost(1e9, 7e6),
    )(pay, normed, rscale, w_in, mixed, spec)


def weights_kernel(width, normed_ref, hidden_ref, pay_ref, g_in_ref, g_out_ref):
    grad_pre = pay_ref[:, :width]
    g_in_ref[...] = mm_tn(normed_ref[...], grad_pre)
    g_out_ref[...] = mm_tn(hidden_ref[...], pay_ref[:, width:])


def weight_grads(normed, hidden, pay):
    count, feats = normed.shape
    width = hidden.shape[1]
    embed = pay.shape[1] - width
    return pl.pallas_call(
        functools.partial(weights_kernel, width),
        in_specs=[VMEM] * 3,
        out_shape=[shape((feats, width), F32), shape((width, embed), F32)],
        out_specs=[VMEM] * 2,
        compiler_params=params(24),
        cost_estimate=cost(3e8, 6e6),
    )(normed, hidden, pay)


def hop_bits(axis):
    size = lax.axis_size(axis)
    steps = size.bit_length() - 1
    assert size == 1 << steps
    return [1 << step for step in range(steps)]


def swap(block, axis, bit):
    size = lax.axis_size(axis)
    return lax.ppermute(block, axis, [(src, src ^ bit) for src in range(size)])


def side(axis, bit):
    return (lax.axis_index(axis) & bit) != 0


def scatter_sum(part, route):
    for axis, bit in route:
        half = part.shape[0] // 2
        upper_side = side(axis, bit)
        low, high = part[:half], part[half:]
        away = jnp.where(upper_side, low, high).astype(BF16)
        kept = jnp.where(upper_side, high, low)
        part = kept + swap(away, axis, bit).astype(F32)
    return part


def gather_back(part, route):
    for axis, bit in reversed(route):
        other = swap(part, axis, bit)
        upper_side = side(axis, bit)
        part = jnp.concatenate(
            [jnp.where(upper_side, other, part), jnp.where(upper_side, part, other)], axis=0
        )
    return part


def reduce_all(g_mix, g_in, g_out):
    width = g_in.shape[1]
    pieces = [g_mix.reshape(-1, width), g_out.reshape(-1, width)]
    small = jnp.concatenate(pieces, axis=0)
    devices = lax.axis_size("blk") * lax.axis_size("dp")
    unit = 8 * devices
    total = -(-(g_in.shape[0] + small.shape[0]) // (2 * unit)) * 2 * unit
    pad = total - g_in.shape[0] - small.shape[0]
    whole = jnp.concatenate([g_in, small, jnp.zeros((pad, width), F32)], axis=0)
    across = [("blk", bit) for bit in hop_bits("blk")]
    along = [("dp", bit) for bit in hop_bits("dp")]
    routes = [along[:1] + across + along[1:], along[:1] + across[::-1] + along[1:]]
    half = total // 2
    done = [
        gather_back(scatter_sum(whole[k * half : (k + 1) * half], route).astype(BF16), route)
        for k, route in enumerate(routes)
    ]
    whole = jnp.concatenate(done, axis=0).astype(F32)
    rows = g_in.shape[0]
    mix_rows = pieces[0].shape[0]
    out_rows = pieces[1].shape[0]
    return (
        whole[rows : rows + mix_rows].reshape(g_mix.shape),
        whole[:rows],
        whole[rows + mix_rows : rows + mix_rows + out_rows].reshape(g_out.shape),
    )


def spread(block, axis, hops):
    return [block] + [swap(block, axis, hop) for hop in hops]


def on_device(patches, w_mix, w_in, w_out, partner_dev, partner_row):
    count = patches.shape[0]
    filters = w_mix.shape[1]
    freqs = w_in.shape[0] // filters
    blocks, peers = lax.axis_size("blk"), lax.axis_size("dp")
    assert peers % 2 == 0
    spec, mixed, units, unit32, norms, rscale, normed, preact, hidden = encode(
        patches, w_mix, w_in, w_out
    )
    across, along = range(1, blocks), range(2, peers, 2)
    pieces = spread(units, "blk", across)
    even = jnp.concatenate(spread(units, "dp", along), axis=0)
    odd = swap(even, "dp", 1)
    expo, zneg, numer = negatives(pieces)
    local, stats, loss = positives(partner_dev, partner_row, even, odd, zneg, numer)
    group_stats = spread(stats, "blk", across)
    even_stats = jnp.concatenate(spread(stats, "dp", along), axis=0)
    odd_stats = swap(even_stats, "dp", 1)
    pay = upper(
        pieces, group_stats, expo, even, odd, even_stats, odd_stats, local, unit32, norms, w_out, preact
    )
    g_in, g_out = weight_grads(normed, hidden, pay)
    g_mix = lower(pay, normed, rscale, w_in, mixed, spec, freqs)
    g_mix, g_in, g_out = reduce_all(g_mix, g_in, g_out)
    return (loss.reshape(count), g_mix, g_in, g_out)


def solution(mesh):
    placed = (P(("blk", "dp"), None, None), P(), P(), P(), P(("blk", "dp")), P(("blk", "dp")))
    return jax.shard_map(
        on_device,
        mesh=mesh,
        in_specs=placed,
        out_specs=(P(("blk", "dp")), P(), P(), P()),
        check_vma=False,
    )
```

```python
import functools
import math

import jax
import jax.numpy as jnp
import numpy as np
from jax import lax
from jax.experimental import pallas as pl
from jax.experimental.pallas import tpu as pltpu
from jax.sharding import PartitionSpec as P

SCALE = 10.0
SUB = 8
BF16 = jnp.bfloat16
F32 = jnp.float32
VMEM = pl.BlockSpec(memory_space=pltpu.VMEM)
ANY = pl.BlockSpec(memory_space=pl.ANY)


def shape(dims, dtype):
    return jax.ShapeDtypeStruct(tuple(dims), dtype)


def mm(left, right):
    return jnp.dot(left, right, preferred_element_type=F32)


def mm_nt(left, right):
    return lax.dot_general(left, right, (((1,), (1,)), ((), ())), preferred_element_type=F32)


def mm_tn(left, right):
    return lax.dot_general(left, right, (((0,), (0,)), ((), ())), preferred_element_type=F32)


def params(mib):
    return pltpu.CompilerParams(vmem_limit_bytes=mib << 20)


def cost(flops, nbytes):
    return pl.CostEstimate(flops=int(flops), bytes_accessed=int(nbytes), transcendentals=0)


def angle_basis(length, freqs):
    phase = np.mod(np.outer(np.arange(freqs), np.arange(length)), length).astype(np.float32)
    phase = phase * np.float32(2.0 * math.pi / length)
    table = np.concatenate([np.cos(phase), -np.sin(phase)], axis=0).astype(np.float32)
    basis = np.einsum("ka,pq->kpqa", table, np.eye(SUB, dtype=np.float32))
    return jnp.asarray(basis.reshape(2 * freqs * SUB, SUB * length), BF16)


def encode_kernel(
    freqs,
    size,
    patch_ref,
    basis_ref,
    mix_ref,
    out_w_ref,
    in_hbm,
    spec_ref,
    mixed_ref,
    units_ref,
    unit32_ref,
    norm_ref,
    rscale_ref,
    normed_ref,
    *rest,
):
    pieces, (feat, hidden_ref, in_w, sem) = rest[:size], rest[size:]
    step = pl.program_id(0)
    load = pltpu.make_async_copy(in_hbm, in_w, sem)

    @pl.when(step == 0)
    def _():
        load.start()

    per, length, lanes = patch_ref.shape
    groups = per // SUB
    filters = mix_ref.shape[1]
    half = freqs * SUB
    for s in range(groups):
        block = patch_ref[s * SUB : (s + 1) * SUB].reshape(SUB * length, lanes)
        spec = mm(basis_ref[...], block).astype(BF16)
        spec_ref[s] = spec
        mixed = mm(spec, mix_ref[...])
        mixed_ref[s] = mixed
        real_part, imag_part = mixed[:half], mixed[half:]
        piece = jnp.log1p(real_part * real_part + imag_part * imag_part)
        base = pl.multiple_of((step * groups + s) * SUB, SUB)
        for k in range(freqs):
            feat[pl.ds(base, SUB), k * filters : (k + 1) * filters] = piece[
                k * SUB : (k + 1) * SUB
            ]

    @pl.when(step == pl.num_programs(0) - 1)
    def _():
        load.wait()
        features = feat[...]
        removed = features - jnp.mean(features, axis=1, keepdims=True)
        rscale = lax.rsqrt(jnp.mean(removed * removed, axis=1, keepdims=True) + 1e-05)
        normed = (removed * rscale).astype(BF16)
        normed_ref[...] = normed
        rscale_ref[...] = jnp.broadcast_to(rscale, rscale_ref.shape)
        preact = mm(normed, in_w[...])
        sigm = jax.nn.sigmoid(preact)
        hidden = (preact * sigm).astype(BF16)
        hidden_ref[...] = hidden
        raw = mm(hidden, out_w_ref[...])
        norms = jnp.sqrt(jnp.sum(raw * raw, axis=1, keepdims=True) + 1e-06)
        norm_ref[...] = jnp.broadcast_to(norms, norm_ref.shape)
        unit32 = raw / norms
        unit32_ref[...] = unit32
        units_ref[...] = unit32.astype(BF16)
        slope = (sigm * (1.0 + preact * (1.0 - sigm))).astype(BF16)
        deep, wide = normed_ref.shape[1] // size, hidden_ref.shape[1] // size
        me = lax.axis_index("blk")
        for i, piece_ref in enumerate(pieces):
            owner = me ^ i
            piece_ref[:, :deep] = normed_ref[:, pl.ds(pl.multiple_of(owner * deep, 128), deep)]
            piece_ref[:, deep : deep + slope.shape[1]] = slope
            if wide % 128 == 0:
                piece_ref[:, deep + slope.shape[1] :] = hidden_ref[
                    :, pl.ds(pl.multiple_of(owner * wide, 128), wide)
                ]
            else:
                piece_ref[:, deep + slope.shape[1] :] = hidden_ref[...]


def piece_columns(feats, width, size):
    wide = width // size
    return feats // size, width, wide if wide % 128 == 0 else width


def encode(patches, w_mix, w_in, w_out, size):
    count, length, lanes = patches.shape
    filters = w_mix.shape[1]
    feats, width = w_in.shape
    embed = w_out.shape[1]
    freqs = feats // filters
    per = 2 * SUB
    groups = count // SUB
    rows = 2 * freqs * SUB
    piece = (count, sum(piece_columns(feats, width, size)))

    def whole(*dims):
        return pl.BlockSpec(dims, lambda i: (0,) * len(dims))

    outs = [
        (shape((groups, rows, lanes), BF16), pl.BlockSpec((per // SUB, rows, lanes), lambda i: (i, 0, 0))),
        (shape((groups, rows, filters), F32), pl.BlockSpec((per // SUB, rows, filters), lambda i: (i, 0, 0))),
        (shape((count, embed), BF16), whole(count, embed)),
        (shape((count, embed), F32), whole(count, embed)),
        (shape((count, 128), F32), whole(count, 128)),
        (shape((count, 128), F32), whole(count, 128)),
        (shape((count, feats), BF16), whole(count, feats)),
    ] + [(shape(piece, BF16), whole(*piece))] * size
    return pl.pallas_call(
        functools.partial(encode_kernel, freqs, size),
        grid=(count // per,),
        in_specs=[
            pl.BlockSpec((per, length, lanes), lambda i: (i, 0, 0)),
            whole(rows, SUB * length),
            whole(lanes, filters),
            whole(width, embed),
            ANY,
        ],
        out_shape=[each for each, _ in outs],
        out_specs=[spec for _, spec in outs],
        scratch_shapes=[
            pltpu.VMEM((count, feats), F32),
            pltpu.VMEM((count, width), BF16),
            pltpu.VMEM((feats, width), BF16),
            pltpu.SemaphoreType.DMA,
        ],
        compiler_params=params(60),
        cost_estimate=cost(3e9, 14e6),
    )(patches, angle_basis(length, freqs), w_mix, w_out, w_in)


def exponentials(units, keys, own):
    expo = jnp.exp(SCALE * mm_nt(units, keys))
    if own:
        row = lax.broadcasted_iota(jnp.int32, expo.shape, 0)
        col = lax.broadcasted_iota(jnp.int32, expo.shape, 1)
        expo = jnp.where(row == col, 0.0, expo)
    return expo


def negative_kernel(size, *refs):
    pieces, stacked, (zneg_ref, numer_ref, even_ref) = refs[:size], refs[size:-3], refs[-3:]
    units = pieces[0][...]
    count = units.shape[0]
    even_ref[:count, :] = units
    for i, each in enumerate(stacked):
        even_ref[(i + 1) * count : (i + 2) * count, :] = each[...]
    zneg = numer = None
    for i, piece in enumerate(pieces):
        keys = piece[...]
        expo = exponentials(units, keys, i == 0)
        total = jnp.sum(expo, axis=1, keepdims=True)
        term = mm(expo.astype(BF16), keys)
        zneg = total if zneg is None else zneg + total
        numer = term if numer is None else numer + term
    zneg_ref[...] = jnp.broadcast_to(zneg, zneg_ref.shape)
    numer_ref[...] = numer


def negatives(pieces, stacked):
    count, embed = pieces[0].shape
    size = len(pieces)
    return pl.pallas_call(
        functools.partial(negative_kernel, size),
        in_specs=[VMEM] * (size + len(stacked)),
        out_shape=[
            shape((count, 128), F32),
            shape((count, embed), F32),
            shape(((len(stacked) + 1) * count, embed), BF16),
        ],
        out_specs=[VMEM] * 3,
        compiler_params=params(8),
        cost_estimate=cost(4e8, 1e6),
    )(*pieces, *stacked)


def as_rows(column, count):
    return jnp.broadcast_to(column, (column.shape[0], count)).T


def positive_kernel(
    dev_ref, row_ref, even_ref, odd_ref, zneg_ref, numer_ref, local_ref, stats_ref, loss_ref
):
    count = dev_ref.shape[1]
    me = lax.axis_index("dp")
    step = dev_ref[...] ^ me
    place = ((step & 1) * even_ref.shape[0] + (step >> 1) * count + row_ref[...]).astype(F32)
    place = jnp.broadcast_to(place, (count, count)).T
    lane = lax.broadcasted_iota(jnp.int32, (count, count), 1).astype(F32)
    positive = None
    blocks = even_ref.shape[0] // count
    for i in range(2 * blocks):
        source = even_ref if i < blocks else odd_ref
        at = (i % blocks) * count
        hit = jnp.where(place - float(i * count) == lane, 1.0, 0.0).astype(BF16)
        term = mm(hit, source[at : at + count, :])
        positive = term if positive is None else positive + term
    units = even_ref[:count, :].astype(F32)
    spos = SCALE * jnp.sum(units * positive, axis=1, keepdims=True)
    top = jnp.exp(spos)
    totals = top + zneg_ref[:, :1]
    less = top / totals - 1.0
    coef = SCALE / count
    local_ref[...] = coef * (less * positive + numer_ref[...] / totals)
    loss_ref[...] = as_rows(jnp.log(totals) - spos, count)[:1]
    stats_ref[...] = jnp.zeros(stats_ref.shape, F32)
    stats_ref[0:1, :] = as_rows(totals, count)[:1]
    stats_ref[1:2, :] = as_rows(coef * less, count)[:1]
    stats_ref[2:3, :] = (dev_ref[...] * count + row_ref[...]).astype(F32)


def positives(partner_dev, partner_row, even, odd, zneg, numer):
    count, embed = numer.shape
    return pl.pallas_call(
        positive_kernel,
        in_specs=[VMEM] * 6,
        out_shape=[shape((count, embed), F32), shape((SUB, count), F32), shape((1, count), F32)],
        out_specs=[VMEM] * 3,
        compiler_params=params(8),
        cost_estimate=cost(4e8, 1e6),
    )(partner_dev.reshape(1, count), partner_row.reshape(1, count), even, odd, zneg, numer)


def upper_kernel(size, *refs):
    pieces, rest = refs[:size], refs[size:]
    stats, rest = rest[:size], rest[size:]
    (even_ref, odd_ref, even_stats, odd_stats, local_ref, unit32_ref, norm_ref, out_ref) = rest
    count, embed = local_ref.shape
    coef = SCALE / count
    units = pieces[0][...]
    keyterm = None
    for i in range(size):
        keys = pieces[i][...]
        expo = exponentials(units, keys, i == 0)
        weights = (expo / stats[i][0:1, :]).astype(BF16)
        term = mm(weights, keys)
        keyterm = term if keyterm is None else keyterm + term
    mine = lax.axis_index("dp") * count + lax.broadcasted_iota(jnp.int32, (count, count), 0)
    mine = mine.astype(F32)
    blocks = even_ref.shape[0] // count
    chosen = amount = None
    for i in range(2 * blocks):
        source, table = (even_ref, even_stats) if i < blocks else (odd_ref, odd_stats)
        j = i % blocks
        hit = table[j * SUB + 2 : j * SUB + 3, :] == mine
        share = jnp.where(hit, table[j * SUB + 1 : j * SUB + 2, :], 0.0)
        term = mm(jnp.where(hit, 1.0, 0.0).astype(BF16), source[j * count : (j + 1) * count, :])
        chosen = term if chosen is None else chosen + term
        amount = share if amount is None else amount + share
    back = jnp.sum(amount, axis=1, keepdims=True) * chosen
    grad_units = local_ref[...] + coef * keyterm + back
    unit32 = unit32_ref[...]
    along = jnp.sum(unit32 * grad_units, axis=1, keepdims=True)
    out_ref[...] = ((grad_units - unit32 * along) / norm_ref[:, :1]).astype(BF16)


def upper(pieces, stats, even, odd, even_stats, odd_stats, local, unit32, norms):
    count, embed = local.shape
    size = len(pieces)
    args = [*pieces, *stats, even, odd, even_stats, odd_stats, local, unit32, norms]
    return pl.pallas_call(
        functools.partial(upper_kernel, size),
        in_specs=[VMEM] * len(args),
        out_shape=shape((count, embed), BF16),
        out_specs=VMEM,
        compiler_params=params(8),
        cost_estimate=cost(4e8, 2e6),
    )(*args)


def pre_grads(grad_raw, out_w, slope):
    return (mm_nt(grad_raw, out_w) * slope.astype(F32)).astype(BF16)


def lower_kernel(
    freqs,
    columns,
    raw_ref,
    out_w_ref,
    piece_ref,
    normed_ref,
    rscale_ref,
    in_hbm,
    mixed_hbm,
    spec_hbm,
    g_mix_ref,
    in_w,
    mixed,
    spec,
    grad_feat,
    sems,
):
    loads = [
        pltpu.make_async_copy(source, target, sems.at[i])
        for i, (source, target) in enumerate([(in_hbm, in_w), (mixed_hbm, mixed), (spec_hbm, spec)])
    ]
    for each in loads:
        each.start()
    deep, width, _ = columns
    grad_pre = pre_grads(raw_ref[...], out_w_ref[...], piece_ref[:, deep : deep + width])
    loads[0].wait()
    grad_norm = mm_nt(grad_pre, in_w[...])
    xhat = normed_ref[...].astype(F32)
    mean = jnp.mean(grad_norm, axis=1, keepdims=True)
    slope = jnp.mean(grad_norm * xhat, axis=1, keepdims=True)
    grad_feat[...] = rscale_ref[:, :1] * (grad_norm - mean - xhat * slope)
    loads[1].wait()
    loads[2].wait()
    groups, rows, filters = mixed.shape
    half = freqs * SUB

    def one(g, total):
        real_part, imag_part = mixed[g, :half], mixed[g, half:]
        powers = real_part * real_part + imag_part * imag_part
        base = pl.multiple_of(g * SUB, SUB)
        grads = jnp.concatenate(
            [grad_feat[pl.ds(base, SUB), k * filters : (k + 1) * filters] for k in range(freqs)],
            axis=0,
        )
        share = 2.0 * grads / (1.0 + powers)
        grad_mixed = jnp.concatenate([real_part * share, imag_part * share], axis=0).astype(BF16)
        return total + mm_tn(grad_mixed, spec[g])

    total = lax.fori_loop(0, groups, one, jnp.zeros((filters, spec.shape[2]), F32), unroll=4)
    g_mix_ref[...] = total.T


def lower(grad_raw, w_out, piece, normed, rscale, w_in, mixed, spec, freqs, columns):
    count, feats = normed.shape
    groups, rows, filters = mixed.shape
    lanes = spec.shape[2]
    return pl.pallas_call(
        functools.partial(lower_kernel, freqs, columns),
        in_specs=[VMEM] * 5 + [ANY] * 3,
        out_shape=shape((lanes, filters), F32),
        out_specs=VMEM,
        scratch_shapes=[
            pltpu.VMEM(w_in.shape, BF16),
            pltpu.VMEM(mixed.shape, F32),
            pltpu.VMEM(spec.shape, BF16),
            pltpu.VMEM((count, feats), F32),
            pltpu.SemaphoreType.DMA((3,)),
        ],
        compiler_params=params(60),
        cost_estimate=cost(1e9, 7e6),
    )(grad_raw, w_out, piece, normed, rscale, w_in, mixed, spec)


def up_to(rows, unit):
    return -(-rows // unit) * unit


class Layout:
    def __init__(self, lanes, filters, feats, width, embed, size, peers):
        self.size, self.peers = size, peers
        self.in_rows = feats // size // peers
        self.out_rows = width // size // peers
        self.mix_rows = lanes // peers
        self.top = up_to(self.in_rows, 16)
        self.strip = max(16, up_to(self.out_rows, 16))
        self.mix_blocks = -(-self.mix_rows // self.strip)
        self.rows = self.top + self.strip
        self.width = width
        assert embed == 128 and filters == 128 and (1 + self.mix_blocks) * 128 <= width

    def mix_parts(self):
        for block in range(self.mix_blocks):
            start = block * self.strip
            yield start, min(self.strip, self.mix_rows - start), slice(128 * (block + 1), 128 * (block + 2))


def weights_kernel(lay, columns, *refs):
    size, peers = lay.size, lay.peers
    pieces, raws, rest = refs[:size], refs[size : 2 * size], refs[2 * size :]
    out_w_ref, mix_ref, keep_ref, away_ref, g_in, g_out = rest
    deep, width, wide = columns
    share = width // size
    for i in range(size):
        raw = raws[i][...]
        grad_pre = pre_grads(raw, out_w_ref[...], pieces[i][:, deep : deep + width])
        term_in = mm_tn(pieces[i][:, :deep], grad_pre)
        term_out = mm_tn(pieces[i][:, deep + width :], raw)
        if i == 0:
            g_in[...] = term_in
            g_out[...] = term_out
        else:
            g_in[...] += term_in
            g_out[...] += term_out
    me = lax.axis_index("dp")
    first = 0 if wide == share else lax.axis_index("blk") * share
    keep_ref[...] = jnp.zeros(keep_ref.shape, F32)
    away_ref[...] = jnp.zeros(away_ref.shape, BF16)
    for slot in range(peers):
        owner = me ^ slot
        target = away_ref if slot & 1 else keep_ref
        at = slot >> 1
        target[at, : lay.in_rows, :] = g_in[pl.ds(owner * lay.in_rows, lay.in_rows), :].astype(target.dtype)
        target[at, lay.top : lay.top + lay.out_rows, :128] = g_out[
            pl.ds(first + owner * lay.out_rows, lay.out_rows), :
        ].astype(target.dtype)
        for start, rows, cols in lay.mix_parts():
            target[at, lay.top : lay.top + rows, cols] = mix_ref[
                pl.ds(owner * lay.mix_rows + start, rows), :
            ].astype(target.dtype)


def weight_grads(lay, columns, pieces, raws, w_out, g_mix):
    deep, width, wide = columns
    block = (lay.peers // 2, lay.rows, lay.width)
    args = [*pieces, *raws, w_out, g_mix]
    return pl.pallas_call(
        functools.partial(weights_kernel, lay, columns),
        in_specs=[VMEM] * len(args),
        out_shape=[shape(block, F32), shape(block, BF16)],
        out_specs=[VMEM] * 2,
        scratch_shapes=[pltpu.VMEM((deep, width), F32), pltpu.VMEM((wide, 128), F32)],
        compiler_params=params(16),
        cost_estimate=cost(6e8, 4e6),
    )(*args)


def pair_kernel(keep_ref, got_ref, own_ref, *out_refs):
    own_ref[...] = keep_ref[0] + got_ref[0].astype(F32)
    for i, out_ref in enumerate(out_refs):
        out_ref[...] = (keep_ref[i + 1] + got_ref[i + 1].astype(F32)).astype(BF16)


def pair_sum(keep, got):
    slots, rows, width = keep.shape
    return pl.pallas_call(
        pair_kernel,
        in_specs=[VMEM] * 2,
        out_shape=[shape((rows, width), F32)] + [shape((rows, width), BF16)] * (slots - 1),
        out_specs=[VMEM] * slots,
        compiler_params=params(8),
        cost_estimate=cost(1e6, 2e6),
    )(keep, got)


def total_kernel(own_ref, *refs):
    total = own_ref[...]
    for each in refs[:-1]:
        total = total + each[...].astype(F32)
    refs[-1][...] = total.astype(BF16)


def total_sum(own, got):
    return pl.pallas_call(
        total_kernel,
        in_specs=[VMEM] * (1 + len(got)),
        out_shape=shape(own.shape, BF16),
        out_specs=VMEM,
        compiler_params=params(8),
        cost_estimate=cost(1e6, 1e6),
    )(own, *got)


def finish_kernel(lay, *refs):
    size, slots = lay.size, lay.peers // 2
    evens, odds = refs[:size], refs[size : 2 * size]
    g_mix_ref, g_in_hbm, g_out_ref, stage, sems = refs[2 * size :]
    me_blk, me_dp = lax.axis_index("blk"), lax.axis_index("dp")
    copies = []
    for i in range(size):
        for core, source in enumerate((evens[i], odds[i])):
            for z in range(slots):
                at = z * lay.rows
                owner = me_dp ^ (2 * z + core)
                slot = (i * 2 + core) * slots + z
                stage[slot] = source[at : at + lay.in_rows, :].astype(F32)
                row = ((me_blk ^ i) * lay.peers + owner) * lay.in_rows
                copy = pltpu.make_async_copy(
                    stage.at[slot], g_in_hbm.at[pl.ds(row, lay.in_rows), :], sems.at[slot]
                )
                copy.start()
                copies.append(copy)
                row = ((me_blk ^ i) * lay.peers + owner) * lay.out_rows
                strip = at + lay.top
                g_out_ref[pl.ds(row, lay.out_rows), :] = source[
                    strip : strip + lay.out_rows, :128
                ].astype(F32)
    for core in range(2):
        for z in range(slots):
            strip = z * lay.rows + lay.top
            owner = me_dp ^ (2 * z + core)
            for start, rows, cols in lay.mix_parts():
                blocks = {0: evens, 1: odds}[core]
                terms = [blocks[i][strip : strip + rows, cols].astype(F32) for i in range(size)]
                while len(terms) > 1:
                    terms = [terms[t] + terms[t + 1] for t in range(0, len(terms), 2)]
                g_mix_ref[pl.ds(owner * lay.mix_rows + start, rows), :] = terms[0]
    for copy in copies:
        copy.wait()


def finish(lay, evens, odds, lanes, feats, width):
    slots = lay.size * lay.peers
    return pl.pallas_call(
        functools.partial(finish_kernel, lay),
        in_specs=[VMEM] * (2 * lay.size),
        out_shape=[shape((lanes, 128), F32), shape((feats, width), F32), shape((width, 128), F32)],
        out_specs=[VMEM, ANY, VMEM],
        scratch_shapes=[
            pltpu.VMEM((slots, lay.in_rows, lay.width), F32),
            pltpu.SemaphoreType.DMA((slots,)),
        ],
        compiler_params=params(24),
        cost_estimate=cost(1e6, 8e6),
    )(*evens, *odds)


def swap(block, axis, bit):
    size = lax.axis_size(axis)
    return lax.ppermute(block, axis, [(src, src ^ bit) for src in range(size)])


def spread(block, axis, hops):
    return [block] + [swap(block, axis, hop) for hop in hops]


def on_device(patches, w_mix, w_in, w_out, partner_dev, partner_row):
    count, _, lanes = patches.shape
    filters = w_mix.shape[1]
    feats, width = w_in.shape
    embed = w_out.shape[1]
    freqs = feats // filters
    size, peers = lax.axis_size("blk"), lax.axis_size("dp")
    assert size & (size - 1) == 0 and peers & (peers - 1) == 0 and peers > 1
    across, along = range(1, size), range(2, peers, 2)
    columns = piece_columns(feats, width, size)
    lay = Layout(lanes, filters, feats, width, embed, size, peers)

    spec, mixed, units, unit32, norms, rscale, normed, *early = encode(
        patches, w_mix, w_in, w_out, size
    )
    pieces = spread(units, "blk", across)
    stacked = spread(units, "dp", along)
    pieces[1:], stacked[1:] = lax.optimization_barrier((pieces[1:], stacked[1:]))
    early = lax.optimization_barrier((early, pieces[1:]))[0]
    zneg, numer, even = negatives(pieces, stacked[1:])
    odd = swap(even, "dp", 1)
    factors = [early[0]] + [swap(early[hop], "blk", hop) for hop in across]
    local, stats, loss = positives(partner_dev, partner_row, even, odd, zneg, numer)
    group_stats = spread(stats, "blk", across)
    even_stats = jnp.concatenate(spread(stats, "dp", along), axis=0)
    odd_stats = swap(even_stats, "dp", 1)
    grad_raw = upper(pieces, group_stats, even, odd, even_stats, odd_stats, local, unit32, norms)
    raws = spread(grad_raw, "blk", across)
    g_mix = lower(grad_raw, w_out, early[0], normed, rscale, w_in, mixed, spec, freqs, columns)

    keep, away = weight_grads(lay, columns, factors, raws, w_out, g_mix)
    own, *sends = pair_sum(keep, swap(away, "dp", 1))
    got = [swap(block, "dp", hop) for block, hop in zip(sends, along)]
    share = total_sum(own, got)
    plane = jnp.concatenate(spread(share, "dp", along), axis=0)
    evens = spread(plane, "blk", across)
    odds = [swap(block, "dp", 1) for block in evens]
    g_mix, g_in, g_out = finish(lay, evens, odds, lanes, feats, width)
    return (loss.reshape(count), g_mix, g_in, g_out)


def solution(mesh):
    placed = (P(("blk", "dp"), None, None), P(), P(), P(), P(("blk", "dp")), P(("blk", "dp")))
    return jax.shard_map(
        on_device,
        mesh=mesh,
        in_specs=placed,
        out_specs=(P(("blk", "dp")), P(), P(), P()),
        check_vma=False,
    )
```

```python
import functools
import math

import jax
import jax.numpy as jnp
import numpy as np
from jax import lax
from jax.experimental import pallas as pl
from jax.experimental.pallas import tpu as pltpu
from jax.sharding import PartitionSpec as P


SCALE = 10.0
SUB = 8
BF16 = jnp.bfloat16
F32 = jnp.float32
VMEM = pl.BlockSpec(memory_space=pltpu.VMEM)
ANY = pl.BlockSpec(memory_space=pl.ANY)
HBM = pl.BlockSpec(memory_space=pltpu.MemorySpace.HBM)


def shape(dims, dtype):
    return jax.ShapeDtypeStruct(tuple(dims), dtype)


def mm(left, right):
    return jnp.dot(left, right, preferred_element_type=F32)


def mm_nt(left, right):
    return lax.dot_general(left, right, (((1,), (1,)), ((), ())), preferred_element_type=F32)


def mm_tn(left, right):
    return lax.dot_general(left, right, (((0,), (0,)), ((), ())), preferred_element_type=F32)


def params(mib):
    return pltpu.CompilerParams(vmem_limit_bytes=mib << 20)


def cost(flops, nbytes):
    return pl.CostEstimate(flops=int(flops), bytes_accessed=int(nbytes), transcendentals=0)


def angle_basis(length, freqs):
    phase = np.mod(np.outer(np.arange(freqs), np.arange(length)), length).astype(np.float32)
    phase = phase * np.float32(2.0 * math.pi / length)
    table = np.concatenate([np.cos(phase), -np.sin(phase)], axis=0).astype(np.float32)
    basis = np.einsum("ka,pq->kpqa", table, np.eye(SUB, dtype=np.float32))
    return jnp.asarray(basis.reshape(2 * freqs * SUB, SUB * length), BF16)


def encode_kernel(
    freqs,
    size,
    patch_ref,
    basis_ref,
    mix_ref,
    out_w_ref,
    in_hbm,
    spec_ref,
    mixed_ref,
    units_ref,
    unit32_ref,
    norm_ref,
    rscale_ref,
    normed_ref,
    *rest,
):
    pieces, (feat, hidden_ref, in_w, sem) = rest[:size], rest[size:]
    step = pl.program_id(0)
    load = pltpu.make_async_copy(in_hbm, in_w, sem)

    @pl.when(step == 0)
    def _():
        load.start()

    per, length, lanes = patch_ref.shape
    groups = per // SUB
    filters = mix_ref.shape[1]
    half = freqs * SUB
    for s in range(groups):
        block = patch_ref[s * SUB : (s + 1) * SUB].reshape(SUB * length, lanes)
        spec = mm(basis_ref[...], block).astype(BF16)
        spec_ref[s] = spec
        mixed = mm(spec, mix_ref[...])
        mixed_ref[s] = mixed
        real_part, imag_part = mixed[:half], mixed[half:]
        piece = jnp.log1p(real_part * real_part + imag_part * imag_part)
        base = pl.multiple_of((step * groups + s) * SUB, SUB)
        for k in range(freqs):
            feat[pl.ds(base, SUB), k * filters : (k + 1) * filters] = piece[
                k * SUB : (k + 1) * SUB
            ]

    @pl.when(step == pl.num_programs(0) - 1)
    def _():
        load.wait()
        features = feat[...]
        removed = features - jnp.mean(features, axis=1, keepdims=True)
        rscale = lax.rsqrt(jnp.mean(removed * removed, axis=1, keepdims=True) + 1e-05)
        normed = (removed * rscale).astype(BF16)
        normed_ref[...] = normed
        rscale_ref[...] = jnp.broadcast_to(rscale, rscale_ref.shape)
        preact = mm(normed, in_w[...])
        sigm = jax.nn.sigmoid(preact)
        hidden = (preact * sigm).astype(BF16)
        hidden_ref[...] = hidden
        raw = mm(hidden, out_w_ref[...])
        norms = jnp.sqrt(jnp.sum(raw * raw, axis=1, keepdims=True) + 1e-06)
        norm_ref[...] = jnp.broadcast_to(norms, norm_ref.shape)
        unit32 = raw / norms
        unit32_ref[...] = unit32
        units_ref[...] = unit32.astype(BF16)
        slope = (sigm * (1.0 + preact * (1.0 - sigm))).astype(BF16)
        deep, wide = normed_ref.shape[1] // size, hidden_ref.shape[1] // size
        me = lax.axis_index("blk")
        for i, piece_ref in enumerate(pieces):
            owner = me ^ i
            piece_ref[:, :deep] = normed_ref[:, pl.ds(pl.multiple_of(owner * deep, 128), deep)]
            piece_ref[:, deep : deep + slope.shape[1]] = slope
            if wide % 128 == 0:
                piece_ref[:, deep + slope.shape[1] :] = hidden_ref[
                    :, pl.ds(pl.multiple_of(owner * wide, 128), wide)
                ]
            else:
                piece_ref[:, deep + slope.shape[1] :] = hidden_ref[...]


def piece_columns(feats, width, size):
    wide = width // size
    return feats // size, width, wide if wide % 128 == 0 else width


def encode(patches, w_mix, w_in, w_out, size):
    count, length, lanes = patches.shape
    filters = w_mix.shape[1]
    feats, width = w_in.shape
    embed = w_out.shape[1]
    freqs = feats // filters
    per = 2 * SUB
    groups = count // SUB
    rows = 2 * freqs * SUB
    piece = (count, sum(piece_columns(feats, width, size)))

    def whole(*dims):
        return pl.BlockSpec(dims, lambda i: (0,) * len(dims))

    outs = [
        (shape((groups, rows, lanes), BF16), pl.BlockSpec((per // SUB, rows, lanes), lambda i: (i, 0, 0))),
        (shape((groups, rows, filters), F32), pl.BlockSpec((per // SUB, rows, filters), lambda i: (i, 0, 0))),
        (shape((count, embed), BF16), whole(count, embed)),
        (shape((count, embed), F32), whole(count, embed)),
        (shape((count, 128), F32), whole(count, 128)),
        (shape((count, 128), F32), whole(count, 128)),
        (shape((count, feats), BF16), whole(count, feats)),
    ] + [(shape(piece, BF16), whole(*piece))] * size
    return pl.pallas_call(
        functools.partial(encode_kernel, freqs, size),
        grid=(count // per,),
        in_specs=[
            pl.BlockSpec((per, length, lanes), lambda i: (i, 0, 0)),
            whole(rows, SUB * length),
            whole(lanes, filters),
            whole(width, embed),
            ANY,
        ],
        out_shape=[each for each, _ in outs],
        out_specs=[spec for _, spec in outs],
        scratch_shapes=[
            pltpu.VMEM((count, feats), F32),
            pltpu.VMEM((count, width), BF16),
            pltpu.VMEM((feats, width), BF16),
            pltpu.SemaphoreType.DMA,
        ],
        compiler_params=params(60),
        cost_estimate=cost(3e9, 14e6),
    )(patches, angle_basis(length, freqs), w_mix, w_out, w_in)


def exponentials(units, keys, own):
    expo = jnp.exp(SCALE * mm_nt(units, keys))
    if own:
        row = lax.broadcasted_iota(jnp.int32, expo.shape, 0)
        col = lax.broadcasted_iota(jnp.int32, expo.shape, 1)
        expo = jnp.where(row == col, 0.0, expo)
    return expo


def negative_kernel(size, *refs):
    pieces, stacked, (zneg_ref, numer_ref, even_ref) = refs[:size], refs[size:-3], refs[-3:]
    units = pieces[0][...]
    count = units.shape[0]
    even_ref[:count, :] = units
    for i, each in enumerate(stacked):
        even_ref[(i + 1) * count : (i + 2) * count, :] = each[...]
    zneg = numer = None
    for i, piece in enumerate(pieces):
        keys = piece[...]
        expo = exponentials(units, keys, i == 0)
        total = jnp.sum(expo, axis=1, keepdims=True)
        term = mm(expo.astype(BF16), keys)
        zneg = total if zneg is None else zneg + total
        numer = term if numer is None else numer + term
    zneg_ref[...] = jnp.broadcast_to(zneg, zneg_ref.shape)
    numer_ref[...] = numer


def negatives(pieces, stacked):
    count, embed = pieces[0].shape
    size = len(pieces)
    return pl.pallas_call(
        functools.partial(negative_kernel, size),
        in_specs=[VMEM] * (size + len(stacked)),
        out_shape=[
            shape((count, 128), F32),
            shape((count, embed), F32),
            shape(((len(stacked) + 1) * count, embed), BF16),
        ],
        out_specs=[VMEM] * 3,
        compiler_params=params(8),
        cost_estimate=cost(4e8, 1e6),
    )(*pieces, *stacked)


def as_rows(column, count):
    return jnp.broadcast_to(column, (column.shape[0], count)).T


def positive_kernel(
    dev_ref, row_ref, even_ref, odd_ref, zneg_ref, numer_ref, local_ref, stats_ref, loss_ref
):
    count = dev_ref.shape[1]
    me = lax.axis_index("dp")
    step = dev_ref[...] ^ me
    place = ((step & 1) * even_ref.shape[0] + (step >> 1) * count + row_ref[...]).astype(F32)
    place = jnp.broadcast_to(place, (count, count)).T
    lane = lax.broadcasted_iota(jnp.int32, (count, count), 1).astype(F32)
    positive = None
    blocks = even_ref.shape[0] // count
    for i in range(2 * blocks):
        source = even_ref if i < blocks else odd_ref
        at = (i % blocks) * count
        hit = jnp.where(place - float(i * count) == lane, 1.0, 0.0).astype(BF16)
        term = mm(hit, source[at : at + count, :])
        positive = term if positive is None else positive + term
    units = even_ref[:count, :].astype(F32)
    spos = SCALE * jnp.sum(units * positive, axis=1, keepdims=True)
    top = jnp.exp(spos)
    totals = top + zneg_ref[:, :1]
    less = top / totals - 1.0
    coef = SCALE / count
    local_ref[...] = coef * (less * positive + numer_ref[...] / totals)
    loss_ref[...] = as_rows(jnp.log(totals) - spos, count)[:1]
    stats_ref[...] = jnp.zeros(stats_ref.shape, F32)
    stats_ref[0:1, :] = as_rows(totals, count)[:1]
    stats_ref[1:2, :] = as_rows(coef * less, count)[:1]
    stats_ref[2:3, :] = (dev_ref[...] * count + row_ref[...]).astype(F32)


def positives(partner_dev, partner_row, even, odd, zneg, numer):
    count, embed = numer.shape
    return pl.pallas_call(
        positive_kernel,
        in_specs=[VMEM] * 6,
        out_shape=[shape((count, embed), F32), shape((SUB, count), F32), shape((1, count), F32)],
        out_specs=[VMEM] * 3,
        compiler_params=params(8),
        cost_estimate=cost(4e8, 1e6),
    )(partner_dev.reshape(1, count), partner_row.reshape(1, count), even, odd, zneg, numer)


def upper_kernel(size, *refs):
    pieces, rest = refs[:size], refs[size:]
    stats, rest = rest[:size], rest[size:]
    (even_ref, odd_ref, even_stats, odd_stats, local_ref, unit32_ref, norm_ref, out_ref) = rest
    count, _ = local_ref.shape
    coef = SCALE / count
    units = pieces[0][...]
    keyterm = None
    for i in range(size):
        keys = pieces[i][...]
        expo = exponentials(units, keys, i == 0)
        weights = (expo / stats[i][0:1, :]).astype(BF16)
        term = mm(weights, keys)
        keyterm = term if keyterm is None else keyterm + term
    mine = lax.axis_index("dp") * count + lax.broadcasted_iota(jnp.int32, (count, count), 0)
    mine = mine.astype(F32)
    blocks = even_ref.shape[0] // count
    chosen = amount = None
    for i in range(2 * blocks):
        source, table = (even_ref, even_stats) if i < blocks else (odd_ref, odd_stats)
        j = i % blocks
        hit = table[j * SUB + 2 : j * SUB + 3, :] == mine
        share = jnp.where(hit, table[j * SUB + 1 : j * SUB + 2, :], 0.0)
        term = mm(jnp.where(hit, 1.0, 0.0).astype(BF16), source[j * count : (j + 1) * count, :])
        chosen = term if chosen is None else chosen + term
        amount = share if amount is None else amount + share
    back = jnp.sum(amount, axis=1, keepdims=True) * chosen
    grad_units = local_ref[...] + coef * keyterm + back
    unit32 = unit32_ref[...]
    along = jnp.sum(unit32 * grad_units, axis=1, keepdims=True)
    out_ref[...] = ((grad_units - unit32 * along) / norm_ref[:, :1]).astype(BF16)


def upper(pieces, stats, even, odd, even_stats, odd_stats, local, unit32, norms):
    count, embed = local.shape
    size = len(pieces)
    args = [*pieces, *stats, even, odd, even_stats, odd_stats, local, unit32, norms]
    return pl.pallas_call(
        functools.partial(upper_kernel, size),
        in_specs=[VMEM] * len(args),
        out_shape=shape((count, embed), BF16),
        out_specs=VMEM,
        compiler_params=params(8),
        cost_estimate=cost(4e8, 2e6),
    )(*args)


def pre_grads(grad_raw, out_w, slope):
    return (mm_nt(grad_raw, out_w) * slope.astype(F32)).astype(BF16)


def lower_kernel(
    freqs,
    columns,
    raw_ref,
    out_w_hbm,
    piece_hbm,
    normed_hbm,
    rscale_hbm,
    in_hbm,
    mixed_hbm,
    spec_hbm,
    g_mix_ref,
    out_w,
    slope,
    in_w,
    normed,
    rscale,
    mixed,
    spec,
    grad_feat,
    sems,
):
    deep, width, _ = columns
    sources = [
        out_w_hbm,
        piece_hbm.at[:, deep : deep + width],
        in_hbm,
        normed_hbm,
        rscale_hbm,
        mixed_hbm,
        spec_hbm,
    ]
    targets = [out_w, slope, in_w, normed, rscale, mixed, spec]
    loads = [
        pltpu.make_async_copy(source, target, sems.at[i])
        for i, (source, target) in enumerate(zip(sources, targets))
    ]
    for each in loads:
        each.start()
    loads[0].wait()
    loads[1].wait()
    grad_pre = pre_grads(raw_ref[...], out_w[...], slope[...])
    loads[2].wait()
    grad_norm = mm_nt(grad_pre, in_w[...])
    loads[3].wait()
    loads[4].wait()
    xhat = normed[...].astype(F32)
    mean = jnp.mean(grad_norm, axis=1, keepdims=True)
    tilt = jnp.mean(grad_norm * xhat, axis=1, keepdims=True)
    grad_feat[...] = rscale[:, :1] * (grad_norm - mean - xhat * tilt)
    loads[5].wait()
    loads[6].wait()
    groups, _, filters = mixed.shape
    half = freqs * SUB

    def one(g, total):
        real_part, imag_part = mixed[g, :half], mixed[g, half:]
        powers = real_part * real_part + imag_part * imag_part
        base = pl.multiple_of(g * SUB, SUB)
        grads = jnp.concatenate(
            [grad_feat[pl.ds(base, SUB), k * filters : (k + 1) * filters] for k in range(freqs)],
            axis=0,
        )
        share = 2.0 * grads / (1.0 + powers)
        grad_mixed = jnp.concatenate([real_part * share, imag_part * share], axis=0).astype(BF16)
        return total + mm_tn(grad_mixed, spec[g])

    total = lax.fori_loop(0, groups, one, jnp.zeros((filters, spec.shape[2]), F32), unroll=4)
    g_mix_ref[...] = total.T


def lower(grad_raw, w_out, piece, normed, rscale, w_in, mixed, spec, freqs, columns):
    count, feats = normed.shape
    _, _, filters = mixed.shape
    lanes = spec.shape[2]
    return pl.pallas_call(
        functools.partial(lower_kernel, freqs, columns),
        in_specs=[VMEM] + [HBM] * 7,
        out_shape=shape((lanes, filters), F32),
        out_specs=VMEM,
        scratch_shapes=[
            pltpu.VMEM(w_out.shape, BF16),
            pltpu.VMEM((count, columns[1]), BF16),
            pltpu.VMEM(w_in.shape, BF16),
            pltpu.VMEM((count, feats), BF16),
            pltpu.VMEM(rscale.shape, F32),
            pltpu.VMEM(mixed.shape, F32),
            pltpu.VMEM(spec.shape, BF16),
            pltpu.VMEM((count, feats), F32),
            pltpu.SemaphoreType.DMA((7,)),
        ],
        compiler_params=params(20),
        cost_estimate=cost(1e9, 7e6),
    )(grad_raw, w_out, piece, normed, rscale, w_in, mixed, spec)


def up_to(rows, unit):
    return -(-rows // unit) * unit


class Layout:
    def __init__(self, lanes, filters, feats, width, embed, size, peers):
        self.size, self.peers = size, peers
        self.in_rows = feats // size // peers
        self.out_rows = width // size // peers
        self.mix_rows = lanes // peers
        self.top = up_to(self.in_rows, 16)
        self.strip = max(16, up_to(self.out_rows, 16))
        self.mix_blocks = -(-self.mix_rows // self.strip)
        self.rows = self.top + self.strip
        self.width = width
        assert embed == 128 and filters == 128 and (1 + self.mix_blocks) * 128 <= width

    def mix_parts(self):
        for block in range(self.mix_blocks):
            start = block * self.strip
            yield start, min(self.strip, self.mix_rows - start), slice(128 * (block + 1), 128 * (block + 2))


def weights_kernel(lay, columns, *refs):
    size, peers = lay.size, lay.peers
    pieces, raws, rest = refs[:size], refs[size : 2 * size], refs[2 * size :]
    out_w_ref, mix_ref, keep_ref, away_ref, g_in, g_out = rest
    deep, width, wide = columns
    share = width // size
    for i in range(size):
        raw = raws[i][...]
        grad_pre = pre_grads(raw, out_w_ref[...], pieces[i][:, deep : deep + width])
        term_in = mm_tn(pieces[i][:, :deep], grad_pre)
        term_out = mm_tn(pieces[i][:, deep + width :], raw)
        if i == 0:
            g_in[...] = term_in
            g_out[...] = term_out
        else:
            g_in[...] += term_in
            g_out[...] += term_out
    me = lax.axis_index("dp")
    first = 0 if wide == share else lax.axis_index("blk") * share
    keep_ref[...] = jnp.zeros(keep_ref.shape, F32)
    away_ref[...] = jnp.zeros(away_ref.shape, BF16)
    for slot in range(peers):
        owner = me ^ slot
        target = away_ref if slot & 1 else keep_ref
        at = slot >> 1
        target[at, : lay.in_rows, :] = g_in[pl.ds(owner * lay.in_rows, lay.in_rows), :].astype(target.dtype)
        target[at, lay.top : lay.top + lay.out_rows, :128] = g_out[
            pl.ds(first + owner * lay.out_rows, lay.out_rows), :
        ].astype(target.dtype)
        for start, rows, cols in lay.mix_parts():
            target[at, lay.top : lay.top + rows, cols] = mix_ref[
                pl.ds(owner * lay.mix_rows + start, rows), :
            ].astype(target.dtype)


def weight_grads(lay, columns, pieces, raws, w_out, g_mix):
    deep, width, wide = columns
    block = (lay.peers // 2, lay.rows, lay.width)
    args = [*pieces, *raws, w_out, g_mix]
    return pl.pallas_call(
        functools.partial(weights_kernel, lay, columns),
        in_specs=[VMEM] * len(args),
        out_shape=[shape(block, F32), shape(block, BF16)],
        out_specs=[VMEM] * 2,
        scratch_shapes=[pltpu.VMEM((deep, width), F32), pltpu.VMEM((wide, 128), F32)],
        compiler_params=params(16),
        cost_estimate=cost(6e8, 4e6),
    )(*args)


def pair_kernel(keep_ref, got_ref, own_ref, *out_refs):
    own_ref[...] = keep_ref[0] + got_ref[0].astype(F32)
    for i, out_ref in enumerate(out_refs):
        out_ref[...] = (keep_ref[i + 1] + got_ref[i + 1].astype(F32)).astype(BF16)


def pair_sum(keep, got):
    slots, rows, width = keep.shape
    return pl.pallas_call(
        pair_kernel,
        in_specs=[VMEM] * 2,
        out_shape=[shape((rows, width), F32)] + [shape((rows, width), BF16)] * (slots - 1),
        out_specs=[VMEM] * slots,
        compiler_params=params(8),
        cost_estimate=cost(1e6, 2e6),
    )(keep, got)


def total_kernel(own_ref, *refs):
    total = own_ref[...]
    for each in refs[:-1]:
        total = total + each[...].astype(F32)
    refs[-1][...] = total.astype(BF16)


def total_sum(own, got):
    return pl.pallas_call(
        total_kernel,
        in_specs=[VMEM] * (1 + len(got)),
        out_shape=shape(own.shape, BF16),
        out_specs=VMEM,
        compiler_params=params(8),
        cost_estimate=cost(1e6, 1e6),
    )(own, *got)


def finish_kernel(lay, *refs):
    size, slots = lay.size, lay.peers // 2
    evens, odds = refs[:size], refs[size : 2 * size]
    g_mix_ref, g_in_hbm, g_out_ref, stage, sems = refs[2 * size :]
    me_blk, me_dp = lax.axis_index("blk"), lax.axis_index("dp")
    copies = []
    for i in range(size):
        for core, source in enumerate((evens[i], odds[i])):
            for z in range(slots):
                at = z * lay.rows
                owner = me_dp ^ (2 * z + core)
                slot = (i * 2 + core) * slots + z
                stage[slot] = source[at : at + lay.in_rows, :].astype(F32)
                row = ((me_blk ^ i) * lay.peers + owner) * lay.in_rows
                copy = pltpu.make_async_copy(
                    stage.at[slot], g_in_hbm.at[pl.ds(row, lay.in_rows), :], sems.at[slot]
                )
                copy.start()
                copies.append(copy)
                row = ((me_blk ^ i) * lay.peers + owner) * lay.out_rows
                strip = at + lay.top
                g_out_ref[pl.ds(row, lay.out_rows), :] = source[
                    strip : strip + lay.out_rows, :128
                ].astype(F32)
    for core in range(2):
        for z in range(slots):
            strip = z * lay.rows + lay.top
            owner = me_dp ^ (2 * z + core)
            for start, rows, cols in lay.mix_parts():
                blocks = {0: evens, 1: odds}[core]
                terms = [blocks[i][strip : strip + rows, cols].astype(F32) for i in range(size)]
                while len(terms) > 1:
                    terms = [terms[t] + terms[t + 1] for t in range(0, len(terms), 2)]
                g_mix_ref[pl.ds(owner * lay.mix_rows + start, rows), :] = terms[0]
    for copy in copies:
        copy.wait()


def finish(lay, evens, odds, lanes, feats, width):
    slots = lay.size * lay.peers
    return pl.pallas_call(
        functools.partial(finish_kernel, lay),
        in_specs=[VMEM] * (2 * lay.size),
        out_shape=[shape((lanes, 128), F32), shape((feats, width), F32), shape((width, 128), F32)],
        out_specs=[VMEM, ANY, VMEM],
        scratch_shapes=[
            pltpu.VMEM((slots, lay.in_rows, lay.width), F32),
            pltpu.SemaphoreType.DMA((slots,)),
        ],
        compiler_params=params(24),
        cost_estimate=cost(1e6, 8e6),
    )(*evens, *odds)


def swap(block, axis, bit):
    size = lax.axis_size(axis)
    return lax.ppermute(block, axis, [(src, src ^ bit) for src in range(size)])


def spread(block, axis, hops):
    return [block] + [swap(block, axis, hop) for hop in hops]


def on_device(patches, w_mix, w_in, w_out, partner_dev, partner_row):
    count, _, lanes = patches.shape
    filters = w_mix.shape[1]
    feats, width = w_in.shape
    embed = w_out.shape[1]
    freqs = feats // filters
    size, peers = lax.axis_size("blk"), lax.axis_size("dp")
    assert size & (size - 1) == 0 and peers & (peers - 1) == 0 and peers > 1
    across, along = range(1, size), range(2, peers, 2)
    columns = piece_columns(feats, width, size)
    lay = Layout(lanes, filters, feats, width, embed, size, peers)

    spec, mixed, units, unit32, norms, rscale, normed, *early = encode(
        patches, w_mix, w_in, w_out, size
    )
    stacked = spread(units, "dp", along)
    pieces = spread(units, "blk", across)
    pieces[1:], stacked[1:] = lax.optimization_barrier((pieces[1:], stacked[1:]))
    zneg, numer, even = negatives(pieces, stacked[1:])
    odd = swap(even, "dp", 1)
    local, stats, loss = positives(partner_dev, partner_row, even, odd, zneg, numer)
    dp_stats = spread(stats, "dp", along)
    group_stats = spread(stats, "blk", across)
    dp_stats[1:], group_stats[1:] = lax.optimization_barrier((dp_stats[1:], group_stats[1:]))
    factors = [early[0]] + [swap(early[hop], "blk", hop) for hop in across]
    even_stats = jnp.concatenate(dp_stats, axis=0)
    odd_stats = swap(even_stats, "dp", 1)
    grad_raw = upper(pieces, group_stats, even, odd, even_stats, odd_stats, local, unit32, norms)
    raws = spread(grad_raw, "blk", across)
    g_mix = lower(grad_raw, w_out, early[0], normed, rscale, w_in, mixed, spec, freqs, columns)
    keep, away = weight_grads(lay, columns, factors, raws, w_out, g_mix)
    got = swap(away, "dp", 1)
    own, *sends = pair_sum(keep, got)
    got = [swap(block, "dp", hop) for block, hop in zip(sends, along)]
    share = total_sum(own, got)
    plane = jnp.concatenate(spread(share, "dp", along), axis=0)
    evens = spread(plane, "blk", across)
    odds = [swap(block, "dp", 1) for block in evens]
    g_mix, g_in, g_out = finish(lay, evens, odds, lanes, feats, width)
    return (loss.reshape(count), g_mix, g_in, g_out)


def solution(mesh):
    placed = (P(("blk", "dp"), None, None), P(), P(), P(), P(("blk", "dp")), P(("blk", "dp")))
    return jax.shard_map(
        on_device,
        mesh=mesh,
        in_specs=placed,
        out_specs=(P(("blk", "dp")), P(), P(), P()),
        check_vma=False,
    )
```

```python
import functools
import math

import jax
import jax.numpy as jnp
import numpy as np
from jax import lax
from jax.experimental import pallas as pl
from jax.experimental.pallas import tpu as pltpu
from jax.sharding import PartitionSpec as P


SCALE = 10.0
SUB = 8
BF16 = jnp.bfloat16
F32 = jnp.float32
VMEM = pl.BlockSpec(memory_space=pltpu.VMEM)
ANY = pl.BlockSpec(memory_space=pl.ANY)


def shape(dims, dtype):
    return jax.ShapeDtypeStruct(tuple(dims), dtype)


def hbm(value):
    return pltpu.with_memory_space_constraint(value, pltpu.MemorySpace.HBM)


def mm(left, right):
    return jnp.dot(left, right, preferred_element_type=F32)


def mm_nt(left, right):
    return lax.dot_general(left, right, (((1,), (1,)), ((), ())), preferred_element_type=F32)


def mm_tn(left, right):
    return lax.dot_general(left, right, (((0,), (0,)), ((), ())), preferred_element_type=F32)


def params(mib):
    return pltpu.CompilerParams(vmem_limit_bytes=mib << 20)


def cost(flops, nbytes):
    return pl.CostEstimate(flops=int(flops), bytes_accessed=int(nbytes), transcendentals=0)


def angle_basis(length, freqs):
    phase = np.mod(np.outer(np.arange(freqs), np.arange(length)), length).astype(np.float32)
    phase = phase * np.float32(2.0 * math.pi / length)
    table = np.concatenate([np.cos(phase), -np.sin(phase)], axis=0).astype(np.float32)
    basis = np.einsum("ka,pq->kpqa", table, np.eye(SUB, dtype=np.float32))
    return jnp.asarray(basis.reshape(2 * freqs * SUB, SUB * length), BF16)


def encode_kernel(
    freqs,
    size,
    rounds,
    patch_hbm,
    basis_hbm,
    mix_hbm,
    out_hbm,
    in_hbm,
    spec_hbm,
    mixed_hbm,
    normed_hbm,
    *rest,
):
    piece_hbms, rest = rest[:size], rest[size:]
    units_ref, unit32_ref, norm_ref, rscale_ref, *rest = rest
    patches, basis, mix, out_w, in_w, spec, mixed, feat, normed, slope, hidden, *sems = rest
    table_sems, patch_sems, spec_sems, mixed_sems, out_sems = sems
    count, length, lanes = patches.shape
    filters = mix.shape[1]
    half = freqs * SUB
    per = count // rounds
    groups = per // SUB

    def table(i, source, target):
        return pltpu.make_async_copy(source, target, table_sems.at[i])

    tables = [
        table(i, *pair)
        for i, pair in enumerate(
            [(basis_hbm, basis), (mix_hbm, mix), (in_hbm, in_w), (out_hbm, out_w)]
        )
    ]

    def fetch(r):
        rows = pl.ds(r * per, per)
        return pltpu.make_async_copy(patch_hbm.at[rows], patches.at[rows], patch_sems.at[r])

    def keep(r):
        rows = pl.ds(r * groups, groups)
        return (
            pltpu.make_async_copy(spec.at[rows], spec_hbm.at[rows], spec_sems.at[r]),
            pltpu.make_async_copy(mixed.at[rows], mixed_hbm.at[rows], mixed_sems.at[r]),
        )

    tables[0].start()
    fetch(0).start()
    tables[1].start()
    for r in range(1, rounds):
        fetch(r).start()
    tables[2].start()
    tables[3].start()
    tables[0].wait()
    tables[1].wait()

    def one(r, carry):
        fetch(r).wait()
        for s in range(groups):
            g = r * groups + s
            base = pl.multiple_of(g * SUB, SUB)
            block = patches[pl.ds(base, SUB)].reshape(SUB * length, lanes)
            part = mm(basis[...], block).astype(BF16)
            spec[g] = part
            both = mm(part, mix[...])
            mixed[g] = both
            real_part, imag_part = both[:half], both[half:]
            piece = jnp.log1p(real_part * real_part + imag_part * imag_part)
            for k in range(freqs):
                feat[pl.ds(base, SUB), k * filters : (k + 1) * filters] = piece[
                    k * SUB : (k + 1) * SUB
                ]
        for each in keep(r):
            each.start()
        return carry

    lax.fori_loop(0, rounds, one, 0)
    features = feat[...]
    removed = features - jnp.mean(features, axis=1, keepdims=True)
    rscale = lax.rsqrt(jnp.mean(removed * removed, axis=1, keepdims=True) + 1e-05)
    normed[...] = (removed * rscale).astype(BF16)
    rscale_ref[...] = jnp.broadcast_to(rscale, rscale_ref.shape)
    deep, width, wide = piece_columns(normed.shape[1], hidden.shape[1], size)
    me = lax.axis_index("blk")
    outs = [pltpu.make_async_copy(normed, normed_hbm, out_sems.at[0])]
    for i, piece_hbm in enumerate(piece_hbms):
        columns = pl.ds(pl.multiple_of((me ^ i) * deep, 128), deep)
        outs.append(
            pltpu.make_async_copy(
                normed.at[:, columns], piece_hbm.at[:, :deep], out_sems.at[len(outs)]
            )
        )
    for each in outs:
        each.start()
    tables[2].wait()
    preact = mm(normed[...], in_w[...])
    sigm = jax.nn.sigmoid(preact)
    hidden[...] = (preact * sigm).astype(BF16)
    slope[...] = (sigm * (1.0 + preact * (1.0 - sigm))).astype(BF16)
    late = []
    for i, piece_hbm in enumerate(piece_hbms):
        if wide == hidden.shape[1]:
            columns = pl.ds(0, wide)
        else:
            columns = pl.ds(pl.multiple_of((me ^ i) * wide, 128), wide)
        for source, target in (
            (slope, piece_hbm.at[:, deep : deep + width]),
            (hidden.at[:, columns], piece_hbm.at[:, deep + width :]),
        ):
            late.append(
                pltpu.make_async_copy(source, target, out_sems.at[len(outs) + len(late)])
            )
    for each in late:
        each.start()
    tables[3].wait()
    raw = mm(hidden[...], out_w[...])
    norms = jnp.sqrt(jnp.sum(raw * raw, axis=1, keepdims=True) + 1e-06)
    norm_ref[...] = jnp.broadcast_to(norms, norm_ref.shape)
    unit32 = raw / norms
    unit32_ref[...] = unit32
    units_ref[...] = unit32.astype(BF16)
    for r in range(rounds):
        for each in keep(r):
            each.wait()
    for each in outs + late:
        each.wait()


def piece_columns(feats, width, size):
    wide = width // size
    return feats // size, width, wide if wide % 128 == 0 else width


def encode(patches, w_mix, w_in, w_out, size):
    count, length, lanes = patches.shape
    filters = w_mix.shape[1]
    feats, width = w_in.shape
    embed = w_out.shape[1]
    freqs = feats // filters
    rounds = 4
    assert count % (rounds * SUB) == 0
    groups = count // SUB
    rows = 2 * freqs * SUB
    piece = (count, sum(piece_columns(feats, width, size)))
    HBM = pltpu.MemorySpace.HBM
    kept = [
        HBM((groups, rows, lanes), BF16),
        HBM((groups, rows, filters), F32),
        HBM((count, feats), BF16),
    ] + [HBM(piece, BF16)] * size
    near = [shape((count, embed), BF16), shape((count, embed), F32)] + [shape((count, 128), F32)] * 2
    return pl.pallas_call(
        functools.partial(encode_kernel, freqs, size, rounds),
        in_specs=[ANY] * 5,
        out_shape=kept + near,
        out_specs=[ANY] * len(kept) + [VMEM] * len(near),
        scratch_shapes=[
            pltpu.VMEM(patches.shape, BF16),
            pltpu.VMEM((rows, SUB * length), BF16),
            pltpu.VMEM(w_mix.shape, BF16),
            pltpu.VMEM(w_out.shape, BF16),
            pltpu.VMEM(w_in.shape, BF16),
            pltpu.VMEM((groups, rows, lanes), BF16),
            pltpu.VMEM((groups, rows, filters), F32),
            pltpu.VMEM((count, feats), F32),
            pltpu.VMEM((count, feats), BF16),
            pltpu.VMEM((count, width), BF16),
            pltpu.VMEM((count, width), BF16),
            pltpu.SemaphoreType.DMA((4,)),
            pltpu.SemaphoreType.DMA((rounds,)),
            pltpu.SemaphoreType.DMA((rounds,)),
            pltpu.SemaphoreType.DMA((rounds,)),
            pltpu.SemaphoreType.DMA((1 + 3 * size,)),
        ],
        compiler_params=params(24),
        cost_estimate=cost(3e9, 14e6),
    )(*map(hbm, (patches, angle_basis(length, freqs), w_mix, w_out, w_in)))


def exponentials(units, keys, own):
    expo = jnp.exp(SCALE * mm_nt(units, keys))
    if own:
        row = lax.broadcasted_iota(jnp.int32, expo.shape, 0)
        col = lax.broadcasted_iota(jnp.int32, expo.shape, 1)
        expo = jnp.where(row == col, 0.0, expo)
    return expo


def negative_kernel(size, *refs):
    pieces, stacked, (zneg_ref, numer_ref, even_ref) = refs[:size], refs[size:-3], refs[-3:]
    units = pieces[0][...]
    count = units.shape[0]
    even_ref[:count, :] = units
    for i, each in enumerate(stacked):
        even_ref[(i + 1) * count : (i + 2) * count, :] = each[...]
    zneg = numer = None
    for i, piece in enumerate(pieces):
        keys = piece[...]
        expo = exponentials(units, keys, i == 0)
        total = jnp.sum(expo, axis=1, keepdims=True)
        term = mm(expo.astype(BF16), keys)
        zneg = total if zneg is None else zneg + total
        numer = term if numer is None else numer + term
    zneg_ref[...] = jnp.broadcast_to(zneg, zneg_ref.shape)
    numer_ref[...] = numer


def negatives(pieces, stacked):
    count, embed = pieces[0].shape
    size = len(pieces)
    return pl.pallas_call(
        functools.partial(negative_kernel, size),
        in_specs=[VMEM] * (size + len(stacked)),
        out_shape=[
            shape((count, 128), F32),
            shape((count, embed), F32),
            shape(((len(stacked) + 1) * count, embed), BF16),
        ],
        out_specs=[VMEM] * 3,
        compiler_params=params(8),
        cost_estimate=cost(4e8, 1e6),
    )(*pieces, *stacked)


def as_rows(column, count):
    return jnp.broadcast_to(column, (column.shape[0], count)).T


def positive_kernel(
    dev_ref, row_ref, even_ref, odd_ref, zneg_ref, numer_ref, local_ref, stats_ref, loss_ref
):
    count = dev_ref.shape[1]
    me = lax.axis_index("dp")
    step = dev_ref[...] ^ me
    place = ((step & 1) * even_ref.shape[0] + (step >> 1) * count + row_ref[...]).astype(F32)
    place = jnp.broadcast_to(place, (count, count)).T
    lane = lax.broadcasted_iota(jnp.int32, (count, count), 1).astype(F32)
    positive = None
    blocks = even_ref.shape[0] // count
    for i in range(2 * blocks):
        source = even_ref if i < blocks else odd_ref
        at = (i % blocks) * count
        hit = jnp.where(place - float(i * count) == lane, 1.0, 0.0).astype(BF16)
        term = mm(hit, source[at : at + count, :])
        positive = term if positive is None else positive + term
    units = even_ref[:count, :].astype(F32)
    spos = SCALE * jnp.sum(units * positive, axis=1, keepdims=True)
    top = jnp.exp(spos)
    totals = top + zneg_ref[:, :1]
    less = top / totals - 1.0
    coef = SCALE / count
    local_ref[...] = coef * (less * positive + numer_ref[...] / totals)
    loss_ref[...] = as_rows(jnp.log(totals) - spos, count)[:1]
    stats_ref[...] = jnp.zeros(stats_ref.shape, F32)
    stats_ref[0:1, :] = as_rows(totals, count)[:1]
    stats_ref[1:2, :] = as_rows(coef * less, count)[:1]
    stats_ref[2:3, :] = (dev_ref[...] * count + row_ref[...]).astype(F32)


def positives(partner_dev, partner_row, even, odd, zneg, numer):
    count, embed = numer.shape
    return pl.pallas_call(
        positive_kernel,
        in_specs=[VMEM] * 6,
        out_shape=[shape((count, embed), F32), shape((SUB, count), F32), shape((1, count), F32)],
        out_specs=[VMEM] * 3,
        compiler_params=params(8),
        cost_estimate=cost(4e8, 1e6),
    )(partner_dev.reshape(1, count), partner_row.reshape(1, count), even, odd, zneg, numer)


def upper_kernel(size, *refs):
    pieces, rest = refs[:size], refs[size:]
    stats, rest = rest[:size], rest[size:]
    (even_ref, odd_ref, even_stats, odd_stats, local_ref, unit32_ref, norm_ref, out_ref) = rest
    count, _ = local_ref.shape
    coef = SCALE / count
    units = pieces[0][...]
    keyterm = None
    for i in range(size):
        keys = pieces[i][...]
        expo = exponentials(units, keys, i == 0)
        weights = (expo / stats[i][0:1, :]).astype(BF16)
        term = mm(weights, keys)
        keyterm = term if keyterm is None else keyterm + term
    mine = lax.axis_index("dp") * count + lax.broadcasted_iota(jnp.int32, (count, count), 0)
    mine = mine.astype(F32)
    blocks = even_ref.shape[0] // count
    chosen = amount = None
    for i in range(2 * blocks):
        source, table = (even_ref, even_stats) if i < blocks else (odd_ref, odd_stats)
        j = i % blocks
        hit = table[j * SUB + 2 : j * SUB + 3, :] == mine
        share = jnp.where(hit, table[j * SUB + 1 : j * SUB + 2, :], 0.0)
        term = mm(jnp.where(hit, 1.0, 0.0).astype(BF16), source[j * count : (j + 1) * count, :])
        chosen = term if chosen is None else chosen + term
        amount = share if amount is None else amount + share
    back = jnp.sum(amount, axis=1, keepdims=True) * chosen
    grad_units = local_ref[...] + coef * keyterm + back
    unit32 = unit32_ref[...]
    along = jnp.sum(unit32 * grad_units, axis=1, keepdims=True)
    out_ref[...] = ((grad_units - unit32 * along) / norm_ref[:, :1]).astype(BF16)


def upper(pieces, stats, even, odd, even_stats, odd_stats, local, unit32, norms):
    count, embed = local.shape
    size = len(pieces)
    args = [*pieces, *stats, even, odd, even_stats, odd_stats, local, unit32, norms]
    return pl.pallas_call(
        functools.partial(upper_kernel, size),
        in_specs=[VMEM] * len(args),
        out_shape=shape((count, embed), BF16),
        out_specs=VMEM,
        compiler_params=params(8),
        cost_estimate=cost(4e8, 2e6),
    )(*args)


def pre_grads(grad_raw, out_w, slope):
    return (mm_nt(grad_raw, out_w) * slope.astype(F32)).astype(BF16)


def lower_kernel(
    freqs,
    columns,
    raw_ref,
    out_w_hbm,
    piece_hbm,
    normed_hbm,
    rscale_ref,
    in_hbm,
    mixed_hbm,
    spec_hbm,
    g_mix_ref,
    out_w,
    slope,
    in_w,
    normed,
    mixed,
    spec,
    grad_feat,
    sems,
):
    deep, width, _ = columns
    sources = [
        out_w_hbm,
        piece_hbm.at[:, deep : deep + width],
        in_hbm,
        normed_hbm,
        mixed_hbm,
        spec_hbm,
    ]
    targets = [out_w, slope, in_w, normed, mixed, spec]
    loads = [
        pltpu.make_async_copy(source, target, sems.at[i])
        for i, (source, target) in enumerate(zip(sources, targets))
    ]
    for each in loads:
        each.start()
    loads[0].wait()
    loads[1].wait()
    grad_pre = pre_grads(raw_ref[...], out_w[...], slope[...])
    loads[2].wait()
    grad_norm = mm_nt(grad_pre, in_w[...])
    loads[3].wait()
    xhat = normed[...].astype(F32)
    mean = jnp.mean(grad_norm, axis=1, keepdims=True)
    tilt = jnp.mean(grad_norm * xhat, axis=1, keepdims=True)
    grad_feat[...] = rscale_ref[:, :1] * (grad_norm - mean - xhat * tilt)
    loads[4].wait()
    loads[5].wait()
    groups, _, filters = mixed.shape
    half = freqs * SUB

    def one(g, total):
        real_part, imag_part = mixed[g, :half], mixed[g, half:]
        powers = real_part * real_part + imag_part * imag_part
        base = pl.multiple_of(g * SUB, SUB)
        grads = jnp.concatenate(
            [grad_feat[pl.ds(base, SUB), k * filters : (k + 1) * filters] for k in range(freqs)],
            axis=0,
        )
        share = 2.0 * grads / (1.0 + powers)
        grad_mixed = jnp.concatenate([real_part * share, imag_part * share], axis=0).astype(BF16)
        return total + mm_tn(grad_mixed, spec[g])

    total = lax.fori_loop(0, groups, one, jnp.zeros((filters, spec.shape[2]), F32), unroll=4)
    g_mix_ref[...] = total.T


def lower(grad_raw, w_out, piece, normed, rscale, w_in, mixed, spec, freqs, columns):
    count, feats = normed.shape
    _, _, filters = mixed.shape
    lanes = spec.shape[2]
    return pl.pallas_call(
        functools.partial(lower_kernel, freqs, columns),
        in_specs=[VMEM] + [ANY] * 3 + [VMEM] + [ANY] * 3,
        out_shape=shape((lanes, filters), F32),
        out_specs=VMEM,
        scratch_shapes=[
            pltpu.VMEM(w_out.shape, BF16),
            pltpu.VMEM((count, columns[1]), BF16),
            pltpu.VMEM(w_in.shape, BF16),
            pltpu.VMEM((count, feats), BF16),
            pltpu.VMEM(mixed.shape, F32),
            pltpu.VMEM(spec.shape, BF16),
            pltpu.VMEM((count, feats), F32),
            pltpu.SemaphoreType.DMA((6,)),
        ],
        compiler_params=params(20),
        cost_estimate=cost(1e9, 7e6),
    )(grad_raw, *map(hbm, (w_out, piece, normed)), rscale, *map(hbm, (w_in, mixed, spec)))


def up_to(rows, unit):
    return -(-rows // unit) * unit


class Layout:
    def __init__(self, lanes, filters, feats, width, embed, size, peers):
        self.size, self.peers = size, peers
        self.in_rows = feats // size // peers
        self.out_rows = width // size // peers
        self.mix_rows = lanes // peers
        self.top = up_to(self.in_rows, 16)
        self.strip = max(16, up_to(self.out_rows, 16))
        self.mix_blocks = -(-self.mix_rows // self.strip)
        self.rows = self.top + self.strip
        self.width = width
        assert embed == 128 and filters == 128 and (1 + self.mix_blocks) * 128 <= width

    def mix_parts(self):
        for block in range(self.mix_blocks):
            start = block * self.strip
            yield start, min(self.strip, self.mix_rows - start), slice(128 * (block + 1), 128 * (block + 2))


def weights_kernel(lay, columns, *refs):
    size, peers = lay.size, lay.peers
    pieces, raws, rest = refs[:size], refs[size : 2 * size], refs[2 * size :]
    out_w_ref, mix_ref, keep_ref, away_ref, g_in, g_out = rest
    deep, width, wide = columns
    share = width // size
    for i in range(size):
        raw = raws[i][...]
        grad_pre = pre_grads(raw, out_w_ref[...], pieces[i][:, deep : deep + width])
        term_in = mm_tn(pieces[i][:, :deep], grad_pre)
        term_out = mm_tn(pieces[i][:, deep + width :], raw)
        if i == 0:
            g_in[...] = term_in
            g_out[...] = term_out
        else:
            g_in[...] += term_in
            g_out[...] += term_out
    me = lax.axis_index("dp")
    first = 0 if wide == share else lax.axis_index("blk") * share
    keep_ref[...] = jnp.zeros(keep_ref.shape, F32)
    away_ref[...] = jnp.zeros(away_ref.shape, BF16)
    for slot in range(peers):
        owner = me ^ slot
        target = away_ref if slot & 1 else keep_ref
        at = slot >> 1
        target[at, : lay.in_rows, :] = g_in[pl.ds(owner * lay.in_rows, lay.in_rows), :].astype(target.dtype)
        target[at, lay.top : lay.top + lay.out_rows, :128] = g_out[
            pl.ds(first + owner * lay.out_rows, lay.out_rows), :
        ].astype(target.dtype)
        for start, rows, cols in lay.mix_parts():
            target[at, lay.top : lay.top + rows, cols] = mix_ref[
                pl.ds(owner * lay.mix_rows + start, rows), :
            ].astype(target.dtype)


def weight_grads(lay, columns, pieces, raws, w_out, g_mix):
    deep, width, wide = columns
    block = (lay.peers // 2, lay.rows, lay.width)
    args = [*pieces, *raws, w_out, g_mix]
    return pl.pallas_call(
        functools.partial(weights_kernel, lay, columns),
        in_specs=[VMEM] * len(args),
        out_shape=[shape(block, F32), shape(block, BF16)],
        out_specs=[VMEM] * 2,
        scratch_shapes=[pltpu.VMEM((deep, width), F32), pltpu.VMEM((wide, 128), F32)],
        compiler_params=params(16),
        cost_estimate=cost(6e8, 4e6),
    )(*args)


def pair_kernel(keep_ref, got_ref, own_ref, *out_refs):
    own_ref[...] = keep_ref[0] + got_ref[0].astype(F32)
    for i, out_ref in enumerate(out_refs):
        out_ref[...] = (keep_ref[i + 1] + got_ref[i + 1].astype(F32)).astype(BF16)


def pair_sum(keep, got):
    slots, rows, width = keep.shape
    return pl.pallas_call(
        pair_kernel,
        in_specs=[VMEM] * 2,
        out_shape=[shape((rows, width), F32)] + [shape((rows, width), BF16)] * (slots - 1),
        out_specs=[VMEM] * slots,
        compiler_params=params(8),
        cost_estimate=cost(1e6, 2e6),
    )(keep, got)


def total_kernel(own_ref, *refs):
    total = own_ref[...]
    for each in refs[:-1]:
        total = total + each[...].astype(F32)
    refs[-1][...] = total.astype(BF16)


def total_sum(own, got):
    return pl.pallas_call(
        total_kernel,
        in_specs=[VMEM] * (1 + len(got)),
        out_shape=shape(own.shape, BF16),
        out_specs=VMEM,
        compiler_params=params(8),
        cost_estimate=cost(1e6, 1e6),
    )(own, *got)


def finish_kernel(lay, *refs):
    size, slots = lay.size, lay.peers // 2
    evens, odds = refs[:size], refs[size : 2 * size]
    g_mix_ref, g_in_hbm, g_out_ref, stage, sems = refs[2 * size :]
    me_blk, me_dp = lax.axis_index("blk"), lax.axis_index("dp")
    copies = []
    for i in range(size):
        for core, source in enumerate((evens[i], odds[i])):
            for z in range(slots):
                at = z * lay.rows
                owner = me_dp ^ (2 * z + core)
                slot = (i * 2 + core) * slots + z
                stage[slot] = source[at : at + lay.in_rows, :].astype(F32)
                row = ((me_blk ^ i) * lay.peers + owner) * lay.in_rows
                copy = pltpu.make_async_copy(
                    stage.at[slot], g_in_hbm.at[pl.ds(row, lay.in_rows), :], sems.at[slot]
                )
                copy.start()
                copies.append(copy)
                row = ((me_blk ^ i) * lay.peers + owner) * lay.out_rows
                strip = at + lay.top
                g_out_ref[pl.ds(row, lay.out_rows), :] = source[
                    strip : strip + lay.out_rows, :128
                ].astype(F32)
    for core in range(2):
        for z in range(slots):
            strip = z * lay.rows + lay.top
            owner = me_dp ^ (2 * z + core)
            for start, rows, cols in lay.mix_parts():
                blocks = {0: evens, 1: odds}[core]
                terms = [blocks[i][strip : strip + rows, cols].astype(F32) for i in range(size)]
                while len(terms) > 1:
                    terms = [terms[t] + terms[t + 1] for t in range(0, len(terms), 2)]
                g_mix_ref[pl.ds(owner * lay.mix_rows + start, rows), :] = terms[0]
    for copy in copies:
        copy.wait()


def finish(lay, evens, odds, lanes, feats, width):
    slots = lay.size * lay.peers
    return pl.pallas_call(
        functools.partial(finish_kernel, lay),
        in_specs=[VMEM] * (2 * lay.size),
        out_shape=[shape((lanes, 128), F32), shape((feats, width), F32), shape((width, 128), F32)],
        out_specs=[VMEM, ANY, VMEM],
        scratch_shapes=[
            pltpu.VMEM((slots, lay.in_rows, lay.width), F32),
            pltpu.SemaphoreType.DMA((slots,)),
        ],
        compiler_params=params(24),
        cost_estimate=cost(1e6, 8e6),
    )(*evens, *odds)


def stack_kernel(*refs):
    rows = refs[0].shape[0]
    for i, each in enumerate(refs[:-1]):
        refs[-1][i * rows : (i + 1) * rows, :] = each[...]


def stack(blocks):
    rows, width = blocks[0].shape
    return pl.pallas_call(
        stack_kernel,
        in_specs=[VMEM] * len(blocks),
        out_shape=shape((len(blocks) * rows, width), blocks[0].dtype),
        out_specs=VMEM,
        compiler_params=params(8),
        cost_estimate=cost(1e3, 1e5),
    )(*blocks)


def swap(block, axis, bit):
    size = lax.axis_size(axis)
    return lax.ppermute(block, axis, [(src, src ^ bit) for src in range(size)])


def spread(block, axis, hops):
    return [block] + [swap(block, axis, hop) for hop in hops]


def on_device(patches, w_mix, w_in, w_out, partner_dev, partner_row):
    count, _, lanes = patches.shape
    filters = w_mix.shape[1]
    feats, width = w_in.shape
    embed = w_out.shape[1]
    freqs = feats // filters
    size, peers = lax.axis_size("blk"), lax.axis_size("dp")
    assert size & (size - 1) == 0 and peers & (peers - 1) == 0 and peers > 1
    across, along = range(1, size), range(2, peers, 2)
    columns = piece_columns(feats, width, size)
    lay = Layout(lanes, filters, feats, width, embed, size, peers)

    spec, mixed, normed, *rest = encode(patches, w_mix, w_in, w_out, size)
    early, (units, unit32, norms, rscale) = rest[:size], rest[size:]
    stacked = spread(units, "dp", along)
    pieces = spread(units, "blk", across)
    pieces[1:], stacked[1:] = lax.optimization_barrier((pieces[1:], stacked[1:]))
    zneg, numer, even = negatives(pieces, stacked[1:])
    odd = swap(even, "dp", 1)
    local, stats, loss = positives(partner_dev, partner_row, even, odd, zneg, numer)
    dp_stats = spread(stats, "dp", along)
    group_stats = spread(stats, "blk", across)
    dp_stats[1:], group_stats[1:] = lax.optimization_barrier((dp_stats[1:], group_stats[1:]))
    factors = [early[0]] + [swap(early[hop], "blk", hop) for hop in across]
    even_stats = stack(dp_stats)
    odd_stats = swap(even_stats, "dp", 1)
    grad_raw = upper(pieces, group_stats, even, odd, even_stats, odd_stats, local, unit32, norms)
    raws = spread(grad_raw, "blk", across)
    g_mix = lower(grad_raw, w_out, early[0], normed, rscale, w_in, mixed, spec, freqs, columns)
    keep, away = weight_grads(lay, columns, factors, raws, w_out, g_mix)
    got = swap(away, "dp", 1)
    own, *sends = pair_sum(keep, got)
    got = [swap(block, "dp", hop) for block, hop in zip(sends, along)]
    share = total_sum(own, got)
    plane = stack(spread(share, "dp", along))
    evens = spread(plane, "blk", across)
    odds = [swap(block, "dp", 1) for block in evens]
    g_mix, g_in, g_out = finish(lay, evens, odds, lanes, feats, width)
    return (loss.reshape(count), g_mix, g_in, g_out)


def solution(mesh):
    placed = (P(("blk", "dp"), None, None), P(), P(), P(), P(("blk", "dp")), P(("blk", "dp")))
    return jax.shard_map(
        on_device,
        mesh=mesh,
        in_specs=placed,
        out_specs=(P(("blk", "dp")), P(), P(), P()),
        check_vma=False,
    )
```

```python
import functools
import math

import jax
import jax.numpy as jnp
import numpy as np
from jax import lax
from jax.experimental import pallas as pl
from jax.experimental.pallas import tpu as pltpu
from jax.sharding import PartitionSpec as P


SCALE = 10.0
SUB = 8
BF16 = jnp.bfloat16
F32 = jnp.float32
VMEM = pl.BlockSpec(memory_space=pltpu.VMEM)
ANY = pl.BlockSpec(memory_space=pl.ANY)


def shape(dims, dtype):
    return jax.ShapeDtypeStruct(tuple(dims), dtype)


def hbm(value):
    return pltpu.with_memory_space_constraint(value, pltpu.MemorySpace.HBM)


def mm(left, right):
    return jnp.dot(left, right, preferred_element_type=F32)


def mm_nt(left, right):
    return lax.dot_general(left, right, (((1,), (1,)), ((), ())), preferred_element_type=F32)


def mm_tn(left, right):
    return lax.dot_general(left, right, (((0,), (0,)), ((), ())), preferred_element_type=F32)


def params(mib):
    return pltpu.CompilerParams(vmem_limit_bytes=mib << 20)


def cost(flops, nbytes):
    return pl.CostEstimate(flops=int(flops), bytes_accessed=int(nbytes), transcendentals=0)


def angle_basis(length, freqs):
    phase = np.mod(np.outer(np.arange(freqs), np.arange(length)), length).astype(np.float32)
    phase = phase * np.float32(2.0 * math.pi / length)
    table = np.concatenate([np.cos(phase), -np.sin(phase)], axis=0).astype(np.float32)
    basis = np.einsum("ka,pq->kpqa", table, np.eye(SUB, dtype=np.float32))
    return jnp.asarray(basis.reshape(2 * freqs * SUB, SUB * length), BF16)


def encode_kernel(freqs, size, rounds, patch_hbm, basis_hbm, mix_hbm, out_hbm, in_hbm, *rest):
    piece_hbms, rest = rest[:size], rest[size:]
    spec, mixed, normed, in_w, units_ref, unit32_ref, norm_ref, rscale_ref, *rest = rest
    patches, basis, mix, out_w, feat, slope, hidden, *sems = rest
    table_sems, patch_sems, out_sems = sems
    count, length, lanes = patches.shape
    filters = mix.shape[1]
    half = freqs * SUB
    per = count // rounds
    groups = per // SUB

    def table(i, source, target):
        return pltpu.make_async_copy(source, target, table_sems.at[i])

    tables = [
        table(i, *pair)
        for i, pair in enumerate(
            [(basis_hbm, basis), (mix_hbm, mix), (in_hbm, in_w), (out_hbm, out_w)]
        )
    ]

    def fetch(r):
        rows = pl.ds(r * per, per)
        return pltpu.make_async_copy(patch_hbm.at[rows], patches.at[rows], patch_sems.at[r])

    tables[0].start()
    fetch(0).start()
    tables[1].start()
    for r in range(1, rounds):
        fetch(r).start()
    tables[2].start()
    tables[3].start()
    tables[0].wait()
    tables[1].wait()

    def one(r, carry):
        fetch(r).wait()
        for s in range(groups):
            g = r * groups + s
            base = pl.multiple_of(g * SUB, SUB)
            block = patches[pl.ds(base, SUB)].reshape(SUB * length, lanes)
            part = mm(basis[...], block).astype(BF16)
            spec[g] = part
            both = mm(part, mix[...])
            mixed[g] = both
            real_part, imag_part = both[:half], both[half:]
            piece = jnp.log1p(real_part * real_part + imag_part * imag_part)
            for k in range(freqs):
                feat[pl.ds(base, SUB), k * filters : (k + 1) * filters] = piece[
                    k * SUB : (k + 1) * SUB
                ]
        return carry

    lax.fori_loop(0, rounds, one, 0)
    features = feat[...]
    removed = features - jnp.mean(features, axis=1, keepdims=True)
    rscale = lax.rsqrt(jnp.mean(removed * removed, axis=1, keepdims=True) + 1e-05)
    normed[...] = (removed * rscale).astype(BF16)
    rscale_ref[...] = jnp.broadcast_to(rscale, rscale_ref.shape)
    deep, width, wide = piece_columns(normed.shape[1], hidden.shape[1], size)
    me = lax.axis_index("blk")
    outs = []
    for i, piece_hbm in enumerate(piece_hbms):
        columns = pl.ds(pl.multiple_of((me ^ i) * deep, 128), deep)
        outs.append(
            pltpu.make_async_copy(
                normed.at[:, columns], piece_hbm.at[:, :deep], out_sems.at[len(outs)]
            )
        )
    for each in outs:
        each.start()
    tables[2].wait()
    preact = mm(normed[...], in_w[...])
    sigm = jax.nn.sigmoid(preact)
    hidden[...] = (preact * sigm).astype(BF16)
    slope[...] = (sigm * (1.0 + preact * (1.0 - sigm))).astype(BF16)
    late = []
    for i, piece_hbm in enumerate(piece_hbms):
        if wide == hidden.shape[1]:
            columns = pl.ds(0, wide)
        else:
            columns = pl.ds(pl.multiple_of((me ^ i) * wide, 128), wide)
        for source, target in (
            (slope, piece_hbm.at[:, deep : deep + width]),
            (hidden.at[:, columns], piece_hbm.at[:, deep + width :]),
        ):
            late.append(
                pltpu.make_async_copy(source, target, out_sems.at[len(outs) + len(late)])
            )
    for each in late:
        each.start()
    tables[3].wait()
    raw = mm(hidden[...], out_w[...])
    norms = jnp.sqrt(jnp.sum(raw * raw, axis=1, keepdims=True) + 1e-06)
    norm_ref[...] = jnp.broadcast_to(norms, norm_ref.shape)
    unit32 = raw / norms
    unit32_ref[...] = unit32
    units_ref[...] = unit32.astype(BF16)
    for each in outs + late:
        each.wait()


def piece_columns(feats, width, size):
    wide = width // size
    return feats // size, width, wide if wide % 128 == 0 else width


def encode(patches, w_mix, w_in, w_out, size):
    count, length, lanes = patches.shape
    filters = w_mix.shape[1]
    feats, width = w_in.shape
    embed = w_out.shape[1]
    freqs = feats // filters
    rounds = 4
    assert count % (rounds * SUB) == 0
    groups = count // SUB
    rows = 2 * freqs * SUB
    piece = (count, sum(piece_columns(feats, width, size)))
    kept = [pltpu.MemorySpace.HBM(piece, BF16)] * size
    near = [
        shape((groups, rows, lanes), BF16),
        shape((groups, rows, filters), F32),
        shape((count, feats), BF16),
        shape(w_in.shape, BF16),
        shape((count, embed), BF16),
        shape((count, embed), F32),
        shape((count, 128), F32),
        shape((count, 128), F32),
    ]
    return pl.pallas_call(
        functools.partial(encode_kernel, freqs, size, rounds),
        in_specs=[ANY] * 5,
        out_shape=kept + near,
        out_specs=[ANY] * len(kept) + [VMEM] * len(near),
        scratch_shapes=[
            pltpu.VMEM(patches.shape, BF16),
            pltpu.VMEM((rows, SUB * length), BF16),
            pltpu.VMEM(w_mix.shape, BF16),
            pltpu.VMEM(w_out.shape, BF16),
            pltpu.VMEM((count, feats), F32),
            pltpu.VMEM((count, width), BF16),
            pltpu.VMEM((count, width), BF16),
            pltpu.SemaphoreType.DMA((4,)),
            pltpu.SemaphoreType.DMA((rounds,)),
            pltpu.SemaphoreType.DMA((3 * size,)),
        ],
        compiler_params=params(24),
        cost_estimate=cost(3e9, 14e6),
    )(*map(hbm, (patches, angle_basis(length, freqs), w_mix, w_out, w_in)))


def exponentials(units, keys, own):
    expo = jnp.exp(SCALE * mm_nt(units, keys))
    if own:
        row = lax.broadcasted_iota(jnp.int32, expo.shape, 0)
        col = lax.broadcasted_iota(jnp.int32, expo.shape, 1)
        expo = jnp.where(row == col, 0.0, expo)
    return expo


def negative_kernel(size, *refs):
    pieces, stacked, (zneg_ref, numer_ref, even_ref) = refs[:size], refs[size:-3], refs[-3:]
    units = pieces[0][...]
    count = units.shape[0]
    even_ref[:count, :] = units
    for i, each in enumerate(stacked):
        even_ref[(i + 1) * count : (i + 2) * count, :] = each[...]
    zneg = numer = None
    for i, piece in enumerate(pieces):
        keys = piece[...]
        expo = exponentials(units, keys, i == 0)
        total = jnp.sum(expo, axis=1, keepdims=True)
        term = mm(expo.astype(BF16), keys)
        zneg = total if zneg is None else zneg + total
        numer = term if numer is None else numer + term
    zneg_ref[...] = jnp.broadcast_to(zneg, zneg_ref.shape)
    numer_ref[...] = numer


def negatives(pieces, stacked):
    count, embed = pieces[0].shape
    size = len(pieces)
    return pl.pallas_call(
        functools.partial(negative_kernel, size),
        in_specs=[VMEM] * (size + len(stacked)),
        out_shape=[
            shape((count, 128), F32),
            shape((count, embed), F32),
            shape(((len(stacked) + 1) * count, embed), BF16),
        ],
        out_specs=[VMEM] * 3,
        compiler_params=params(8),
        cost_estimate=cost(4e8, 1e6),
    )(*pieces, *stacked)


def as_rows(column, count):
    return jnp.broadcast_to(column, (column.shape[0], count)).T


def positive_kernel(
    dev_ref, row_ref, even_ref, odd_ref, zneg_ref, numer_ref, local_ref, stats_ref, loss_ref
):
    count = dev_ref.shape[1]
    me = lax.axis_index("dp")
    step = dev_ref[...] ^ me
    place = ((step & 1) * even_ref.shape[0] + (step >> 1) * count + row_ref[...]).astype(F32)
    place = jnp.broadcast_to(place, (count, count)).T
    lane = lax.broadcasted_iota(jnp.int32, (count, count), 1).astype(F32)
    positive = None
    blocks = even_ref.shape[0] // count
    for i in range(2 * blocks):
        source = even_ref if i < blocks else odd_ref
        at = (i % blocks) * count
        hit = jnp.where(place - float(i * count) == lane, 1.0, 0.0).astype(BF16)
        term = mm(hit, source[at : at + count, :])
        positive = term if positive is None else positive + term
    units = even_ref[:count, :].astype(F32)
    spos = SCALE * jnp.sum(units * positive, axis=1, keepdims=True)
    top = jnp.exp(spos)
    totals = top + zneg_ref[:, :1]
    less = top / totals - 1.0
    coef = SCALE / count
    local_ref[...] = coef * (less * positive + numer_ref[...] / totals)
    loss_ref[...] = as_rows(jnp.log(totals) - spos, count)[:1]
    stats_ref[...] = jnp.zeros(stats_ref.shape, F32)
    stats_ref[0:1, :] = as_rows(totals, count)[:1]
    stats_ref[1:2, :] = as_rows(coef * less, count)[:1]
    stats_ref[2:3, :] = (dev_ref[...] * count + row_ref[...]).astype(F32)


def positives(partner_dev, partner_row, even, odd, zneg, numer):
    count, embed = numer.shape
    return pl.pallas_call(
        positive_kernel,
        in_specs=[VMEM] * 6,
        out_shape=[shape((count, embed), F32), shape((SUB, count), F32), shape((1, count), F32)],
        out_specs=[VMEM] * 3,
        compiler_params=params(8),
        cost_estimate=cost(4e8, 1e6),
    )(partner_dev.reshape(1, count), partner_row.reshape(1, count), even, odd, zneg, numer)


def upper_kernel(size, *refs):
    pieces, rest = refs[:size], refs[size:]
    stats, rest = rest[:size], rest[size:]
    (even_ref, odd_ref, even_stats, odd_stats, local_ref, unit32_ref, norm_ref, out_ref) = rest
    count, _ = local_ref.shape
    coef = SCALE / count
    units = pieces[0][...]
    keyterm = None
    for i in range(size):
        keys = pieces[i][...]
        expo = exponentials(units, keys, i == 0)
        weights = (expo / stats[i][0:1, :]).astype(BF16)
        term = mm(weights, keys)
        keyterm = term if keyterm is None else keyterm + term
    mine = lax.axis_index("dp") * count + lax.broadcasted_iota(jnp.int32, (count, count), 0)
    mine = mine.astype(F32)
    blocks = even_ref.shape[0] // count
    chosen = amount = None
    for i in range(2 * blocks):
        source, table = (even_ref, even_stats) if i < blocks else (odd_ref, odd_stats)
        j = i % blocks
        hit = table[j * SUB + 2 : j * SUB + 3, :] == mine
        share = jnp.where(hit, table[j * SUB + 1 : j * SUB + 2, :], 0.0)
        term = mm(jnp.where(hit, 1.0, 0.0).astype(BF16), source[j * count : (j + 1) * count, :])
        chosen = term if chosen is None else chosen + term
        amount = share if amount is None else amount + share
    back = jnp.sum(amount, axis=1, keepdims=True) * chosen
    grad_units = local_ref[...] + coef * keyterm + back
    unit32 = unit32_ref[...]
    along = jnp.sum(unit32 * grad_units, axis=1, keepdims=True)
    out_ref[...] = ((grad_units - unit32 * along) / norm_ref[:, :1]).astype(BF16)


def upper(pieces, stats, even, odd, even_stats, odd_stats, local, unit32, norms):
    count, embed = local.shape
    size = len(pieces)
    args = [*pieces, *stats, even, odd, even_stats, odd_stats, local, unit32, norms]
    return pl.pallas_call(
        functools.partial(upper_kernel, size),
        in_specs=[VMEM] * len(args),
        out_shape=shape((count, embed), BF16),
        out_specs=VMEM,
        compiler_params=params(8),
        cost_estimate=cost(4e8, 2e6),
    )(*args)


def pre_grads(grad_raw, out_w, slope):
    return (mm_nt(grad_raw, out_w) * slope.astype(F32)).astype(BF16)


def lower_kernel(
    freqs,
    columns,
    raw_ref,
    rscale_ref,
    in_w,
    normed,
    mixed,
    spec,
    out_w_hbm,
    piece_hbm,
    g_mix_ref,
    out_w,
    slope,
    grad_feat,
    sems,
):
    deep, width, _ = columns
    loads = [
        pltpu.make_async_copy(out_w_hbm, out_w, sems.at[0]),
        pltpu.make_async_copy(piece_hbm.at[:, deep : deep + width], slope, sems.at[1]),
    ]
    for each in loads:
        each.start()
    for each in loads:
        each.wait()
    grad_pre = pre_grads(raw_ref[...], out_w[...], slope[...])
    grad_norm = mm_nt(grad_pre, in_w[...])
    xhat = normed[...].astype(F32)
    mean = jnp.mean(grad_norm, axis=1, keepdims=True)
    tilt = jnp.mean(grad_norm * xhat, axis=1, keepdims=True)
    grad_feat[...] = rscale_ref[:, :1] * (grad_norm - mean - xhat * tilt)
    groups, _, filters = mixed.shape
    half = freqs * SUB

    def one(g, total):
        real_part, imag_part = mixed[g, :half], mixed[g, half:]
        powers = real_part * real_part + imag_part * imag_part
        base = pl.multiple_of(g * SUB, SUB)
        grads = jnp.concatenate(
            [grad_feat[pl.ds(base, SUB), k * filters : (k + 1) * filters] for k in range(freqs)],
            axis=0,
        )
        share = 2.0 * grads / (1.0 + powers)
        grad_mixed = jnp.concatenate([real_part * share, imag_part * share], axis=0).astype(BF16)
        return total + mm_tn(grad_mixed, spec[g])

    total = lax.fori_loop(0, groups, one, jnp.zeros((filters, spec.shape[2]), F32), unroll=4)
    g_mix_ref[...] = total.T


def lower(grad_raw, w_out, piece, normed, rscale, in_w, mixed, spec, freqs, columns):
    count, feats = normed.shape
    _, _, filters = mixed.shape
    lanes = spec.shape[2]
    return pl.pallas_call(
        functools.partial(lower_kernel, freqs, columns),
        in_specs=[VMEM] * 6 + [ANY] * 2,
        out_shape=shape((lanes, filters), F32),
        out_specs=VMEM,
        scratch_shapes=[
            pltpu.VMEM(w_out.shape, BF16),
            pltpu.VMEM((count, columns[1]), BF16),
            pltpu.VMEM((count, feats), F32),
            pltpu.SemaphoreType.DMA((2,)),
        ],
        compiler_params=params(20),
        cost_estimate=cost(1e9, 7e6),
    )(grad_raw, rscale, in_w, normed, mixed, spec, hbm(w_out), hbm(piece))


def up_to(rows, unit):
    return -(-rows // unit) * unit


class Layout:
    def __init__(self, lanes, filters, feats, width, embed, size, peers):
        self.size, self.peers = size, peers
        self.in_rows = feats // size // peers
        self.out_rows = width // size // peers
        self.mix_rows = lanes // peers
        self.top = up_to(self.in_rows, 16)
        self.strip = max(16, up_to(self.out_rows, 16))
        self.mix_blocks = -(-self.mix_rows // self.strip)
        self.rows = self.top + self.strip
        self.width = width
        assert embed == 128 and filters == 128 and (1 + self.mix_blocks) * 128 <= width

    def mix_parts(self):
        for block in range(self.mix_blocks):
            start = block * self.strip
            yield start, min(self.strip, self.mix_rows - start), slice(128 * (block + 1), 128 * (block + 2))


def weights_kernel(lay, columns, *refs):
    size, peers = lay.size, lay.peers
    pieces, raws, rest = refs[:size], refs[size : 2 * size], refs[2 * size :]
    out_w_ref, mix_ref, keep_ref, away_ref, g_in, g_out = rest
    deep, width, wide = columns
    share = width // size
    for i in range(size):
        raw = raws[i][...]
        grad_pre = pre_grads(raw, out_w_ref[...], pieces[i][:, deep : deep + width])
        term_in = mm_tn(pieces[i][:, :deep], grad_pre)
        term_out = mm_tn(pieces[i][:, deep + width :], raw)
        if i == 0:
            g_in[...] = term_in
            g_out[...] = term_out
        else:
            g_in[...] += term_in
            g_out[...] += term_out
    me = lax.axis_index("dp")
    first = 0 if wide == share else lax.axis_index("blk") * share
    keep_ref[...] = jnp.zeros(keep_ref.shape, F32)
    away_ref[...] = jnp.zeros(away_ref.shape, BF16)
    for slot in range(peers):
        owner = me ^ slot
        target = away_ref if slot & 1 else keep_ref
        at = slot >> 1
        target[at, : lay.in_rows, :] = g_in[pl.ds(owner * lay.in_rows, lay.in_rows), :].astype(target.dtype)
        target[at, lay.top : lay.top + lay.out_rows, :128] = g_out[
            pl.ds(first + owner * lay.out_rows, lay.out_rows), :
        ].astype(target.dtype)
        for start, rows, cols in lay.mix_parts():
            target[at, lay.top : lay.top + rows, cols] = mix_ref[
                pl.ds(owner * lay.mix_rows + start, rows), :
            ].astype(target.dtype)


def weight_grads(lay, columns, pieces, raws, w_out, g_mix):
    deep, width, wide = columns
    block = (lay.peers // 2, lay.rows, lay.width)
    args = [*pieces, *raws, w_out, g_mix]
    return pl.pallas_call(
        functools.partial(weights_kernel, lay, columns),
        in_specs=[VMEM] * len(args),
        out_shape=[shape(block, F32), shape(block, BF16)],
        out_specs=[VMEM] * 2,
        scratch_shapes=[pltpu.VMEM((deep, width), F32), pltpu.VMEM((wide, 128), F32)],
        compiler_params=params(16),
        cost_estimate=cost(6e8, 4e6),
    )(*args)


def pair_kernel(keep_ref, got_ref, own_ref, *out_refs):
    own_ref[...] = keep_ref[0] + got_ref[0].astype(F32)
    for i, out_ref in enumerate(out_refs):
        out_ref[...] = (keep_ref[i + 1] + got_ref[i + 1].astype(F32)).astype(BF16)


def pair_sum(keep, got):
    slots, rows, width = keep.shape
    return pl.pallas_call(
        pair_kernel,
        in_specs=[VMEM] * 2,
        out_shape=[shape((rows, width), F32)] + [shape((rows, width), BF16)] * (slots - 1),
        out_specs=[VMEM] * slots,
        compiler_params=params(8),
        cost_estimate=cost(1e6, 2e6),
    )(keep, got)


def total_kernel(own_ref, *refs):
    total = own_ref[...]
    for each in refs[:-1]:
        total = total + each[...].astype(F32)
    refs[-1][...] = total.astype(BF16)


def total_sum(own, got):
    return pl.pallas_call(
        total_kernel,
        in_specs=[VMEM] * (1 + len(got)),
        out_shape=shape(own.shape, BF16),
        out_specs=VMEM,
        compiler_params=params(8),
        cost_estimate=cost(1e6, 1e6),
    )(own, *got)


def finish_kernel(lay, parts, done, closing, *refs):
    slots = lay.peers // 2
    part_refs, refs = dict(zip(parts, refs)), refs[len(parts) :]
    if done:
        refs = refs[2:]
    g_in_hbm, g_out_hbm, *refs = refs
    if closing:
        g_mix_ref, *refs = refs
    stage, strip_stage, sems, strip_sems = refs
    me_blk, me_dp = lax.axis_index("blk"), lax.axis_index("dp")
    copies = []
    slot = 0
    for (hop, core, half), source in part_refs.items():
        if closing and (hop, core, half) not in closing:
            continue
        for z in range(slots // 2):
            at = z * lay.rows
            owner = (me_blk ^ hop) * lay.peers + (me_dp ^ (half * slots + 2 * z + core))
            stage[slot] = source[at : at + lay.in_rows, :].astype(F32)
            strip = at + lay.top
            strip_stage[slot] = source[strip : strip + lay.out_rows, :128].astype(F32)
            for kept, target, rows, sem in (
                (stage, g_in_hbm, lay.in_rows, sems),
                (strip_stage, g_out_hbm, lay.out_rows, strip_sems),
            ):
                copy = pltpu.make_async_copy(
                    kept.at[slot], target.at[pl.ds(owner * rows, rows), :], sem.at[slot]
                )
                copy.start()
                copies.append(copy)
            slot += 1
    if closing:
        for core in range(2):
            for half in range(2):
                for z in range(slots // 2):
                    strip = z * lay.rows + lay.top
                    owner = me_dp ^ (half * slots + 2 * z + core)
                    for start, rows, cols in lay.mix_parts():
                        terms = [
                            part_refs[hop, core, half][strip : strip + rows, cols].astype(F32)
                            for hop in range(lay.size)
                        ]
                        while len(terms) > 1:
                            terms = [terms[t] + terms[t + 1] for t in range(0, len(terms), 2)]
                        g_mix_ref[pl.ds(owner * lay.mix_rows + start, rows), :] = terms[0]
    for copy in copies:
        copy.wait()


def finish(lay, parts, done, closing, lanes, feats, width):
    slots = (len(closing) if closing else len(parts)) * lay.peers // 4
    outs = [shape((feats, width), F32), shape((width, 128), F32)]
    specs = [ANY, ANY]
    if closing:
        outs.append(shape((lanes, 128), F32))
        specs.append(VMEM)
    return pl.pallas_call(
        functools.partial(finish_kernel, lay, tuple(parts), bool(done), closing),
        in_specs=[VMEM] * len(parts) + [ANY] * len(done),
        out_shape=outs,
        out_specs=specs,
        scratch_shapes=[
            pltpu.VMEM((slots, lay.in_rows, lay.width), F32),
            pltpu.VMEM((slots, lay.out_rows, 128), F32),
            pltpu.SemaphoreType.DMA((slots,)),
            pltpu.SemaphoreType.DMA((slots,)),
        ],
        input_output_aliases={len(parts) + i: i for i in range(len(done))},
        compiler_params=params(24),
        cost_estimate=cost(1e6, 8e6),
    )(*parts.values(), *done)


def stack_kernel(*refs):
    rows = refs[0].shape[0]
    for i, each in enumerate(refs[:-1]):
        refs[-1][i * rows : (i + 1) * rows, :] = each[...]


def stack(blocks):
    rows, width = blocks[0].shape
    return pl.pallas_call(
        stack_kernel,
        in_specs=[VMEM] * len(blocks),
        out_shape=shape((len(blocks) * rows, width), blocks[0].dtype),
        out_specs=VMEM,
        compiler_params=params(8),
        cost_estimate=cost(1e3, 1e5),
    )(*blocks)


def swap(block, axis, bit):
    size = lax.axis_size(axis)
    return lax.ppermute(block, axis, [(src, src ^ bit) for src in range(size)])


def spread(block, axis, hops):
    return [block] + [swap(block, axis, hop) for hop in hops]


def on_device(patches, w_mix, w_in, w_out, partner_dev, partner_row):
    count, _, lanes = patches.shape
    filters = w_mix.shape[1]
    feats, width = w_in.shape
    embed = w_out.shape[1]
    freqs = feats // filters
    size, peers = lax.axis_size("blk"), lax.axis_size("dp")
    assert size & (size - 1) == 0 and peers & (peers - 1) == 0 and peers > 1
    across, along = range(1, size), range(2, peers, 2)
    columns = piece_columns(feats, width, size)
    lay = Layout(lanes, filters, feats, width, embed, size, peers)

    *early, spec, mixed, normed, in_w, units, unit32, norms, rscale = encode(
        patches, w_mix, w_in, w_out, size
    )
    stacked = spread(units, "dp", along)
    pieces = spread(units, "blk", across)
    pieces[1:], stacked[1:] = lax.optimization_barrier((pieces[1:], stacked[1:]))
    zneg, numer, even = negatives(pieces, stacked[1:])
    odd = swap(even, "dp", 1)
    local, stats, loss = positives(partner_dev, partner_row, even, odd, zneg, numer)
    dp_stats = spread(stats, "dp", along)
    group_stats = spread(stats, "blk", across)
    dp_stats[1:], group_stats[1:] = lax.optimization_barrier((dp_stats[1:], group_stats[1:]))
    factors = [early[0]] + [swap(early[hop], "blk", hop) for hop in across]
    even_stats = stack(dp_stats)
    odd_stats = swap(even_stats, "dp", 1)
    grad_raw = upper(pieces, group_stats, even, odd, even_stats, odd_stats, local, unit32, norms)
    raws = spread(grad_raw, "blk", across)
    g_mix = lower(grad_raw, w_out, early[0], normed, rscale, in_w, mixed, spec, freqs, columns)
    keep, away = weight_grads(lay, columns, factors, raws, w_out, g_mix)
    got = swap(away, "dp", 1)
    own, *sends = pair_sum(keep, got)
    got = [swap(block, "dp", hop) for block, hop in zip(sends, along)]
    share = total_sum(own, got)
    shares = spread(share, "dp", along)
    middle = len(shares) // 2
    planes = {(0, 0): stack(shares[:middle]), (0, 1): stack(shares[middle:])}
    single = [hop for hop in across if hop & (hop - 1) == 0]
    several = [hop for hop in across if hop & (hop - 1)]
    for turn in range(2):
        for k, hop in enumerate(single):
            half = (k + turn) % 2
            planes[hop, half] = swap(planes[0, half], "blk", hop)
    for hop in several:
        low, high = hop & -hop, 1 << (hop.bit_length() - 1)
        planes[hop, 0] = swap(planes[hop ^ high, 0], "blk", high)
        planes[hop, 1] = swap(planes[hop ^ low, 1], "blk", low)
    parts, done = {}, []
    groups = [group for group in ([0], single, several) if group]
    for order, group in enumerate(groups):
        fresh = {}
        for hop in group:
            for half in range(2):
                fresh[hop, 0, half] = planes[hop, half]
                fresh[hop, 1, half] = swap(planes[hop, half], "dp", 1)
        parts.update(fresh)
        last = order == len(groups) - 1
        done = finish(
            lay, parts if last else fresh, done, tuple(fresh) if last else (), lanes, feats, width
        )
    g_in, g_out, g_mix = done
    return (loss.reshape(count), g_mix, g_in, g_out)


def solution(mesh):
    placed = (P(("blk", "dp"), None, None), P(), P(), P(), P(("blk", "dp")), P(("blk", "dp")))
    return jax.shard_map(
        on_device,
        mesh=mesh,
        in_specs=placed,
        out_specs=(P(("blk", "dp")), P(), P(), P()),
        check_vma=False,
    )
```

```python
import functools
import math

import jax
import jax.numpy as jnp
import numpy as np
from jax import lax
from jax.experimental import pallas as pl
from jax.experimental.pallas import tpu as pltpu
from jax.sharding import PartitionSpec as P


SCALE = 10.0
SUB = 8
BF16 = jnp.bfloat16
F32 = jnp.float32
VMEM = pl.BlockSpec(memory_space=pltpu.VMEM)
ANY = pl.BlockSpec(memory_space=pl.ANY)


def shape(dims, dtype):
    return jax.ShapeDtypeStruct(tuple(dims), dtype)


def hbm(value):
    return pltpu.with_memory_space_constraint(value, pltpu.MemorySpace.HBM)


def mm(left, right):
    return jnp.dot(left, right, preferred_element_type=F32)


def mm_nt(left, right):
    return lax.dot_general(left, right, (((1,), (1,)), ((), ())), preferred_element_type=F32)


def mm_tn(left, right):
    return lax.dot_general(left, right, (((0,), (0,)), ((), ())), preferred_element_type=F32)


def params(mib):
    return pltpu.CompilerParams(vmem_limit_bytes=mib << 20)


def cost(flops, nbytes):
    return pl.CostEstimate(flops=int(flops), bytes_accessed=int(nbytes), transcendentals=0)


def angle_basis(length, freqs):
    phase = np.mod(np.outer(np.arange(freqs), np.arange(length)), length).astype(np.float32)
    phase = phase * np.float32(2.0 * math.pi / length)
    table = np.concatenate([np.cos(phase), -np.sin(phase)], axis=0).astype(np.float32)
    basis = np.einsum("ka,pq->kpqa", table, np.eye(SUB, dtype=np.float32))
    return jnp.asarray(basis.reshape(2 * freqs * SUB, SUB * length), BF16)


def encode_kernel(freqs, size, rounds, patch_hbm, basis_hbm, mix_hbm, out_hbm, in_hbm, *rest):
    piece_hbms, rest = rest[:size], rest[size:]
    spec, mixed, normed, in_w, units_ref, unit32_ref, norm_ref, rscale_ref, *rest = rest
    patches, basis, mix, out_w, feat, slope, hidden, *sems = rest
    table_sems, patch_sems, out_sems = sems
    count, length, lanes = patches.shape
    filters = mix.shape[1]
    half = freqs * SUB
    per = count // rounds
    groups = per // SUB

    def table(i, source, target):
        return pltpu.make_async_copy(source, target, table_sems.at[i])

    tables = [
        table(i, *pair)
        for i, pair in enumerate(
            [(basis_hbm, basis), (mix_hbm, mix), (in_hbm, in_w), (out_hbm, out_w)]
        )
    ]

    def fetch(r):
        rows = pl.ds(r * per, per)
        return pltpu.make_async_copy(patch_hbm.at[rows], patches.at[rows], patch_sems.at[r])

    tables[0].start()
    fetch(0).start()
    tables[1].start()
    for r in range(1, rounds):
        fetch(r).start()
    tables[2].start()
    tables[3].start()
    tables[0].wait()
    tables[1].wait()

    def one(r, carry):
        fetch(r).wait()
        for s in range(groups):
            g = r * groups + s
            base = pl.multiple_of(g * SUB, SUB)
            block = patches[pl.ds(base, SUB)].reshape(SUB * length, lanes)
            part = mm(basis[...], block).astype(BF16)
            spec[g] = part
            both = mm(part, mix[...])
            mixed[g] = both
            real_part, imag_part = both[:half], both[half:]
            piece = jnp.log1p(real_part * real_part + imag_part * imag_part)
            for k in range(freqs):
                feat[pl.ds(base, SUB), k * filters : (k + 1) * filters] = piece[
                    k * SUB : (k + 1) * SUB
                ]
        return carry

    lax.fori_loop(0, rounds, one, 0)
    features = feat[...]
    removed = features - jnp.mean(features, axis=1, keepdims=True)
    rscale = lax.rsqrt(jnp.mean(removed * removed, axis=1, keepdims=True) + 1e-05)
    normed[...] = (removed * rscale).astype(BF16)
    rscale_ref[...] = jnp.broadcast_to(rscale, rscale_ref.shape)
    deep, width, wide = piece_columns(normed.shape[1], hidden.shape[1], size)
    me = lax.axis_index("blk")
    outs = []
    for i, piece_hbm in enumerate(piece_hbms):
        columns = pl.ds(pl.multiple_of((me ^ i) * deep, 128), deep)
        outs.append(
            pltpu.make_async_copy(
                normed.at[:, columns], piece_hbm.at[:, :deep], out_sems.at[len(outs)]
            )
        )
    for each in outs:
        each.start()
    tables[2].wait()
    preact = mm(normed[...], in_w[...])
    sigm = jax.nn.sigmoid(preact)
    hidden[...] = (preact * sigm).astype(BF16)
    slope[...] = (sigm * (1.0 + preact * (1.0 - sigm))).astype(BF16)
    late = []
    for i, piece_hbm in enumerate(piece_hbms):
        if wide == hidden.shape[1]:
            columns = pl.ds(0, wide)
        else:
            columns = pl.ds(pl.multiple_of((me ^ i) * wide, 128), wide)
        for source, target in (
            (slope, piece_hbm.at[:, deep : deep + width]),
            (hidden.at[:, columns], piece_hbm.at[:, deep + width :]),
        ):
            late.append(
                pltpu.make_async_copy(source, target, out_sems.at[len(outs) + len(late)])
            )
    for each in late:
        each.start()
    tables[3].wait()
    raw = mm(hidden[...], out_w[...])
    norms = jnp.sqrt(jnp.sum(raw * raw, axis=1, keepdims=True) + 1e-06)
    norm_ref[...] = jnp.broadcast_to(norms, norm_ref.shape)
    unit32 = raw / norms
    unit32_ref[...] = unit32
    units_ref[...] = unit32.astype(BF16)
    for each in outs + late:
        each.wait()


def piece_columns(feats, width, size):
    wide = width // size
    return feats // size, width, wide if wide % 128 == 0 else width


def encode(patches, w_mix, w_in, w_out, size):
    count, length, lanes = patches.shape
    filters = w_mix.shape[1]
    feats, width = w_in.shape
    embed = w_out.shape[1]
    freqs = feats // filters
    rounds = 4
    assert count % (rounds * SUB) == 0
    groups = count // SUB
    rows = 2 * freqs * SUB
    piece = (count, sum(piece_columns(feats, width, size)))
    kept = [pltpu.MemorySpace.HBM(piece, BF16)] * size
    near = [
        shape((groups, rows, lanes), BF16),
        shape((groups, rows, filters), F32),
        shape((count, feats), BF16),
        shape(w_in.shape, BF16),
        shape((count, embed), BF16),
        shape((count, embed), F32),
        shape((count, 128), F32),
        shape((count, 128), F32),
    ]
    return pl.pallas_call(
        functools.partial(encode_kernel, freqs, size, rounds),
        in_specs=[ANY] * 5,
        out_shape=kept + near,
        out_specs=[ANY] * len(kept) + [VMEM] * len(near),
        scratch_shapes=[
            pltpu.VMEM(patches.shape, BF16),
            pltpu.VMEM((rows, SUB * length), BF16),
            pltpu.VMEM(w_mix.shape, BF16),
            pltpu.VMEM(w_out.shape, BF16),
            pltpu.VMEM((count, feats), F32),
            pltpu.VMEM((count, width), BF16),
            pltpu.VMEM((count, width), BF16),
            pltpu.SemaphoreType.DMA((4,)),
            pltpu.SemaphoreType.DMA((rounds,)),
            pltpu.SemaphoreType.DMA((3 * size,)),
        ],
        compiler_params=params(24),
        cost_estimate=cost(3e9, 14e6),
    )(*map(hbm, (patches, angle_basis(length, freqs), w_mix, w_out, w_in)))


def exponentials(units, keys, own):
    expo = jnp.exp(SCALE * mm_nt(units, keys))
    if own:
        row = lax.broadcasted_iota(jnp.int32, expo.shape, 0)
        col = lax.broadcasted_iota(jnp.int32, expo.shape, 1)
        expo = jnp.where(row == col, 0.0, expo)
    return expo


def pair_up_kernel(own_ref, other_ref, out_ref):
    rows = own_ref.shape[0]
    own, other = own_ref[...], other_ref[...]
    first = lax.axis_index("dp") % 2 == 0
    out_ref[:rows, :] = jnp.where(first, own, other)
    out_ref[rows:, :] = jnp.where(first, other, own)


def pair_up(own, other):
    rows, width = own.shape
    return pl.pallas_call(
        pair_up_kernel,
        in_specs=[VMEM] * 2,
        out_shape=shape((2 * rows, width), own.dtype),
        out_specs=VMEM,
        compiler_params=params(8),
        cost_estimate=cost(1e3, 1e5),
    )(own, other)


def cross(pair):
    size, peers = lax.axis_size("blk"), lax.axis_size("dp")
    got = []
    for k in range(1, max(size, peers // 2)):
        routes = []
        for blk in range(size):
            for dp in range(peers):
                if dp % 2 == 0 and 2 * k < peers:
                    routes.append((blk * peers + dp, blk * peers + (dp ^ (2 * k))))
                if dp % 2 == 1 and k < size:
                    routes.append((blk * peers + dp, (blk ^ k) * peers + dp))
        got.append(lax.ppermute(pair, ("blk", "dp"), routes))
    return got


def crossed(got_ref, swapped_ref, rows):
    first = lax.axis_index("dp") % 2 == 0

    def along(k, core):
        at = (2 * (k - 1) + core) * rows
        return jnp.where(first, got_ref[at : at + rows, :], swapped_ref[at : at + rows, :])

    def across(k):
        at = 2 * (k - 1) * rows
        low = jnp.where(first, swapped_ref[at : at + rows, :], got_ref[at + rows : at + 2 * rows, :])
        return low

    return along, across


def as_rows(column, count):
    return jnp.broadcast_to(column, (column.shape[0], count)).T


def scores_kernel(
    size,
    peers,
    dev_ref,
    row_ref,
    units_ref,
    pair_ref,
    got_ref,
    swapped_ref,
    local_ref,
    stats_ref,
    loss_ref,
    group_ref,
    around_ref,
):
    units = units_ref[...]
    count = units.shape[0]
    along, across = crossed(got_ref, swapped_ref, count)
    zneg = numer = None
    for i in range(size):
        keys = across(i) if i else units
        group_ref[i * count : (i + 1) * count, :] = keys
        expo = exponentials(units, keys, i == 0)
        total = jnp.sum(expo, axis=1, keepdims=True)
        term = mm(expo.astype(BF16), keys)
        zneg = total if zneg is None else zneg + total
        numer = term if numer is None else numer + term
    me = lax.axis_index("dp")
    dev = dev_ref[...]
    place = (2 * ((dev ^ me) >> 1) + (dev & 1)) * count + row_ref[...]
    place = jnp.broadcast_to(place.astype(F32), (count, count)).T
    lane = lax.broadcasted_iota(jnp.int32, (count, count), 1).astype(F32)
    positive = None
    for i in range(peers):
        k, core = i // 2, i % 2
        source = along(k, core) if k else pair_ref[core * count : (core + 1) * count, :]
        around_ref[i * count : (i + 1) * count, :] = source
        hit = jnp.where(place - float(i * count) == lane, 1.0, 0.0).astype(BF16)
        term = mm(hit, source)
        positive = term if positive is None else positive + term
    spos = SCALE * jnp.sum(units.astype(F32) * positive, axis=1, keepdims=True)
    top = jnp.exp(spos)
    totals = top + zneg
    less = top / totals - 1.0
    coef = SCALE / count
    local_ref[...] = coef * (less * positive + numer / totals)
    loss_ref[...] = as_rows(jnp.log(totals) - spos, count)[:1]
    stats_ref[...] = jnp.zeros(stats_ref.shape, F32)
    stats_ref[0:1, :] = as_rows(totals, count)[:1]
    stats_ref[1:2, :] = as_rows(coef * less, count)[:1]
    stats_ref[2:3, :] = (dev * count + row_ref[...]).astype(F32)


def scores(partner_dev, partner_row, units, pair, got, swapped, size, peers):
    count, embed = units.shape
    return pl.pallas_call(
        functools.partial(scores_kernel, size, peers),
        in_specs=[VMEM] * 6,
        out_shape=[
            shape((count, embed), F32),
            shape((SUB, count), F32),
            shape((1, count), F32),
            shape((size * count, embed), BF16),
            shape((peers * count, embed), BF16),
        ],
        out_specs=[VMEM] * 5,
        compiler_params=params(16),
        cost_estimate=cost(4e8, 1e6),
    )(partner_dev.reshape(1, count), partner_row.reshape(1, count), units, pair, got, swapped)


def upper_kernel(
    size,
    peers,
    group_ref,
    around_ref,
    stats_ref,
    pair_ref,
    got_ref,
    swapped_ref,
    local_ref,
    unit32_ref,
    norm_ref,
    out_ref,
):
    count, _ = local_ref.shape
    coef = SCALE / count
    along, across = crossed(got_ref, swapped_ref, SUB)
    units = group_ref[:count, :]
    keyterm = None
    for i in range(size):
        keys = group_ref[i * count : (i + 1) * count, :]
        expo = exponentials(units, keys, i == 0)
        totals = (across(i) if i else stats_ref[...])[0:1, :]
        term = mm((expo / totals).astype(BF16), keys)
        keyterm = term if keyterm is None else keyterm + term
    mine = lax.axis_index("dp") * count + lax.broadcasted_iota(jnp.int32, (count, count), 0)
    mine = mine.astype(F32)
    chosen = amount = None
    for i in range(peers):
        k, core = i // 2, i % 2
        table = along(k, core) if k else pair_ref[core * SUB : (core + 1) * SUB, :]
        hit = table[2:3, :] == mine
        share = jnp.where(hit, table[1:2, :], 0.0)
        term = mm(jnp.where(hit, 1.0, 0.0).astype(BF16), around_ref[i * count : (i + 1) * count, :])
        chosen = term if chosen is None else chosen + term
        amount = share if amount is None else amount + share
    back = jnp.sum(amount, axis=1, keepdims=True) * chosen
    grad_units = local_ref[...] + coef * keyterm + back
    unit32 = unit32_ref[...]
    tilt = jnp.sum(unit32 * grad_units, axis=1, keepdims=True)
    out_ref[...] = ((grad_units - unit32 * tilt) / norm_ref[:, :1]).astype(BF16)


def upper(group, around, stats, pair, got, swapped, local, unit32, norms, size, peers):
    count, embed = local.shape
    args = [group, around, stats, pair, got, swapped, local, unit32, norms]
    return pl.pallas_call(
        functools.partial(upper_kernel, size, peers),
        in_specs=[VMEM] * len(args),
        out_shape=shape((count, embed), BF16),
        out_specs=VMEM,
        compiler_params=params(16),
        cost_estimate=cost(4e8, 2e6),
    )(*args)


def pre_grads(grad_raw, out_w, slope):
    return (mm_nt(grad_raw, out_w) * slope.astype(F32)).astype(BF16)


def lower_kernel(
    freqs,
    columns,
    raw_ref,
    rscale_ref,
    in_w,
    normed,
    mixed,
    spec,
    out_w_hbm,
    piece_hbm,
    g_mix_ref,
    out_w,
    slope,
    grad_feat,
    sems,
):
    deep, width, _ = columns
    loads = [
        pltpu.make_async_copy(out_w_hbm, out_w, sems.at[0]),
        pltpu.make_async_copy(piece_hbm.at[:, deep : deep + width], slope, sems.at[1]),
    ]
    for each in loads:
        each.start()
    for each in loads:
        each.wait()
    grad_pre = pre_grads(raw_ref[...], out_w[...], slope[...])
    grad_norm = mm_nt(grad_pre, in_w[...])
    xhat = normed[...].astype(F32)
    mean = jnp.mean(grad_norm, axis=1, keepdims=True)
    tilt = jnp.mean(grad_norm * xhat, axis=1, keepdims=True)
    grad_feat[...] = rscale_ref[:, :1] * (grad_norm - mean - xhat * tilt)
    groups, _, filters = mixed.shape
    half = freqs * SUB

    def one(g, total):
        real_part, imag_part = mixed[g, :half], mixed[g, half:]
        powers = real_part * real_part + imag_part * imag_part
        base = pl.multiple_of(g * SUB, SUB)
        grads = jnp.concatenate(
            [grad_feat[pl.ds(base, SUB), k * filters : (k + 1) * filters] for k in range(freqs)],
            axis=0,
        )
        share = 2.0 * grads / (1.0 + powers)
        grad_mixed = jnp.concatenate([real_part * share, imag_part * share], axis=0).astype(BF16)
        return total + mm_tn(grad_mixed, spec[g])

    total = lax.fori_loop(0, groups, one, jnp.zeros((filters, spec.shape[2]), F32), unroll=4)
    g_mix_ref[...] = total.T


def lower(grad_raw, w_out, piece, normed, rscale, in_w, mixed, spec, freqs, columns):
    count, feats = normed.shape
    _, _, filters = mixed.shape
    lanes = spec.shape[2]
    return pl.pallas_call(
        functools.partial(lower_kernel, freqs, columns),
        in_specs=[VMEM] * 6 + [ANY] * 2,
        out_shape=shape((lanes, filters), F32),
        out_specs=VMEM,
        scratch_shapes=[
            pltpu.VMEM(w_out.shape, BF16),
            pltpu.VMEM((count, columns[1]), BF16),
            pltpu.VMEM((count, feats), F32),
            pltpu.SemaphoreType.DMA((2,)),
        ],
        compiler_params=params(20),
        cost_estimate=cost(1e9, 7e6),
    )(grad_raw, rscale, in_w, normed, mixed, spec, hbm(w_out), hbm(piece))


def up_to(rows, unit):
    return -(-rows // unit) * unit


class Layout:
    def __init__(self, lanes, filters, feats, width, embed, size, peers):
        self.size, self.peers = size, peers
        self.in_rows = feats // size // peers
        self.out_rows = width // size // peers
        self.mix_rows = lanes // peers
        self.top = up_to(self.in_rows, 16)
        self.strip = max(16, up_to(self.out_rows, 16))
        self.mix_blocks = -(-self.mix_rows // self.strip)
        self.rows = self.top + self.strip
        self.width = width
        assert embed == 128 and filters == 128 and (1 + self.mix_blocks) * 128 <= width

    def mix_parts(self):
        for block in range(self.mix_blocks):
            start = block * self.strip
            yield start, min(self.strip, self.mix_rows - start), slice(128 * (block + 1), 128 * (block + 2))


def weights_kernel(lay, columns, *refs):
    size, peers = lay.size, lay.peers
    pieces, raws, rest = refs[:size], refs[size : 2 * size], refs[2 * size :]
    out_w_ref, mix_ref, keep_ref, away_ref, g_in, g_out = rest
    deep, width, wide = columns
    share = width // size
    for i in range(size):
        raw = raws[i][...]
        grad_pre = pre_grads(raw, out_w_ref[...], pieces[i][:, deep : deep + width])
        term_in = mm_tn(pieces[i][:, :deep], grad_pre)
        term_out = mm_tn(pieces[i][:, deep + width :], raw)
        if i == 0:
            g_in[...] = term_in
            g_out[...] = term_out
        else:
            g_in[...] += term_in
            g_out[...] += term_out
    me = lax.axis_index("dp")
    first = 0 if wide == share else lax.axis_index("blk") * share
    keep_ref[...] = jnp.zeros(keep_ref.shape, F32)
    away_ref[...] = jnp.zeros(away_ref.shape, BF16)
    for slot in range(peers):
        owner = me ^ slot
        target = away_ref if slot & 1 else keep_ref
        at = slot >> 1
        target[at, : lay.in_rows, :] = g_in[pl.ds(owner * lay.in_rows, lay.in_rows), :].astype(target.dtype)
        target[at, lay.top : lay.top + lay.out_rows, :128] = g_out[
            pl.ds(first + owner * lay.out_rows, lay.out_rows), :
        ].astype(target.dtype)
        for start, rows, cols in lay.mix_parts():
            target[at, lay.top : lay.top + rows, cols] = mix_ref[
                pl.ds(owner * lay.mix_rows + start, rows), :
            ].astype(target.dtype)


def weight_grads(lay, columns, pieces, raws, w_out, g_mix):
    deep, width, wide = columns
    block = (lay.peers // 2, lay.rows, lay.width)
    args = [*pieces, *raws, w_out, g_mix]
    return pl.pallas_call(
        functools.partial(weights_kernel, lay, columns),
        in_specs=[VMEM] * len(args),
        out_shape=[shape(block, F32), shape(block, BF16)],
        out_specs=[VMEM] * 2,
        scratch_shapes=[pltpu.VMEM((deep, width), F32), pltpu.VMEM((wide, 128), F32)],
        compiler_params=params(16),
        cost_estimate=cost(6e8, 4e6),
    )(*args)


def pair_kernel(keep_ref, got_ref, own_ref, *out_refs):
    own_ref[...] = keep_ref[0] + got_ref[0].astype(F32)
    for i, out_ref in enumerate(out_refs):
        out_ref[...] = (keep_ref[i + 1] + got_ref[i + 1].astype(F32)).astype(BF16)


def pair_sum(keep, got):
    slots, rows, width = keep.shape
    return pl.pallas_call(
        pair_kernel,
        in_specs=[VMEM] * 2,
        out_shape=[shape((rows, width), F32)] + [shape((rows, width), BF16)] * (slots - 1),
        out_specs=[VMEM] * slots,
        compiler_params=params(8),
        cost_estimate=cost(1e6, 2e6),
    )(keep, got)


def total_kernel(own_ref, *refs):
    total = own_ref[...]
    for each in refs[:-1]:
        total = total + each[...].astype(F32)
    refs[-1][...] = total.astype(BF16)


def total_sum(own, got):
    return pl.pallas_call(
        total_kernel,
        in_specs=[VMEM] * (1 + len(got)),
        out_shape=shape(own.shape, BF16),
        out_specs=VMEM,
        compiler_params=params(8),
        cost_estimate=cost(1e6, 1e6),
    )(own, *got)


def finish_kernel(lay, parts, done, closing, *refs):
    slots = lay.peers // 2
    part_refs, refs = dict(zip(parts, refs)), refs[len(parts) :]
    if done:
        refs = refs[2:]
    g_in_hbm, g_out_hbm, *refs = refs
    if closing:
        g_mix_ref, *refs = refs
    stage, strip_stage, sems, strip_sems = refs
    me_blk, me_dp = lax.axis_index("blk"), lax.axis_index("dp")
    copies = []
    slot = 0
    for (hop, core, half), source in part_refs.items():
        if closing and (hop, core, half) not in closing:
            continue
        for z in range(slots // 2):
            at = z * lay.rows
            owner = (me_blk ^ hop) * lay.peers + (me_dp ^ (half * slots + 2 * z + core))
            stage[slot] = source[at : at + lay.in_rows, :].astype(F32)
            strip = at + lay.top
            strip_stage[slot] = source[strip : strip + lay.out_rows, :128].astype(F32)
            for kept, target, rows, sem in (
                (stage, g_in_hbm, lay.in_rows, sems),
                (strip_stage, g_out_hbm, lay.out_rows, strip_sems),
            ):
                copy = pltpu.make_async_copy(
                    kept.at[slot], target.at[pl.ds(owner * rows, rows), :], sem.at[slot]
                )
                copy.start()
                copies.append(copy)
            slot += 1
    if closing:
        for core in range(2):
            for half in range(2):
                for z in range(slots // 2):
                    strip = z * lay.rows + lay.top
                    owner = me_dp ^ (half * slots + 2 * z + core)
                    for start, rows, cols in lay.mix_parts():
                        terms = [
                            part_refs[hop, core, half][strip : strip + rows, cols].astype(F32)
                            for hop in range(lay.size)
                        ]
                        while len(terms) > 1:
                            terms = [terms[t] + terms[t + 1] for t in range(0, len(terms), 2)]
                        g_mix_ref[pl.ds(owner * lay.mix_rows + start, rows), :] = terms[0]
    for copy in copies:
        copy.wait()


def finish(lay, parts, done, closing, lanes, feats, width):
    slots = (len(closing) if closing else len(parts)) * lay.peers // 4
    outs = [shape((feats, width), F32), shape((width, 128), F32)]
    specs = [ANY, ANY]
    if closing:
        outs.append(shape((lanes, 128), F32))
        specs.append(VMEM)
    return pl.pallas_call(
        functools.partial(finish_kernel, lay, tuple(parts), bool(done), closing),
        in_specs=[VMEM] * len(parts) + [ANY] * len(done),
        out_shape=outs,
        out_specs=specs,
        scratch_shapes=[
            pltpu.VMEM((slots, lay.in_rows, lay.width), F32),
            pltpu.VMEM((slots, lay.out_rows, 128), F32),
            pltpu.SemaphoreType.DMA((slots,)),
            pltpu.SemaphoreType.DMA((slots,)),
        ],
        input_output_aliases={len(parts) + i: i for i in range(len(done))},
        compiler_params=params(24),
        cost_estimate=cost(1e6, 8e6),
    )(*parts.values(), *done)


def stack_kernel(*refs):
    rows = refs[0].shape[0]
    for i, each in enumerate(refs[:-1]):
        refs[-1][i * rows : (i + 1) * rows, :] = each[...]


def stack(blocks):
    rows, width = blocks[0].shape
    return pl.pallas_call(
        stack_kernel,
        in_specs=[VMEM] * len(blocks),
        out_shape=shape((len(blocks) * rows, width), blocks[0].dtype),
        out_specs=VMEM,
        compiler_params=params(8),
        cost_estimate=cost(1e3, 1e5),
    )(*blocks)


def swap(block, axis, bit):
    size = lax.axis_size(axis)
    return lax.ppermute(block, axis, [(src, src ^ bit) for src in range(size)])


def spread(block, axis, hops):
    return [block] + [swap(block, axis, hop) for hop in hops]


def on_device(patches, w_mix, w_in, w_out, partner_dev, partner_row):
    count, _, lanes = patches.shape
    filters = w_mix.shape[1]
    feats, width = w_in.shape
    embed = w_out.shape[1]
    freqs = feats // filters
    size, peers = lax.axis_size("blk"), lax.axis_size("dp")
    assert size & (size - 1) == 0 and peers & (peers - 1) == 0 and peers > 1
    across, along = range(1, size), range(2, peers, 2)
    columns = piece_columns(feats, width, size)
    lay = Layout(lanes, filters, feats, width, embed, size, peers)

    *early, spec, mixed, normed, in_w, units, unit32, norms, rscale = encode(
        patches, w_mix, w_in, w_out, size
    )
    other = swap(units, "dp", 1)
    pair = pair_up(units, other)
    got = stack(lax.optimization_barrier(cross(pair)))
    factors = [early[0]] + [swap(early[hop], "blk", hop) for hop in across]
    swapped = swap(got, "dp", 1)
    local, stats, loss, group, around = scores(
        partner_dev, partner_row, units, pair, got, swapped, size, peers
    )
    other = swap(stats, "dp", 1)
    pair = pair_up(stats, other)
    got = stack(lax.optimization_barrier(cross(pair)))
    swapped = swap(got, "dp", 1)
    grad_raw = upper(group, around, stats, pair, got, swapped, local, unit32, norms, size, peers)
    raws = spread(grad_raw, "blk", across)
    g_mix = lower(grad_raw, w_out, early[0], normed, rscale, in_w, mixed, spec, freqs, columns)
    keep, away = weight_grads(lay, columns, factors, raws, w_out, g_mix)
    got = swap(away, "dp", 1)
    own, *sends = pair_sum(keep, got)
    got = [swap(block, "dp", hop) for block, hop in zip(sends, along)]
    share = total_sum(own, got)
    shares = spread(share, "dp", along)
    middle = len(shares) // 2
    planes = {(0, 0): stack(shares[:middle]), (0, 1): stack(shares[middle:])}
    single = [hop for hop in across if hop & (hop - 1) == 0]
    several = [hop for hop in across if hop & (hop - 1)]
    for turn in range(2):
        for k, hop in enumerate(single):
            half = (k + turn) % 2
            planes[hop, half] = swap(planes[0, half], "blk", hop)
    for hop in several:
        low, high = hop & -hop, 1 << (hop.bit_length() - 1)
        planes[hop, 0] = swap(planes[hop ^ high, 0], "blk", high)
        planes[hop, 1] = swap(planes[hop ^ low, 1], "blk", low)
    parts, done = {}, []
    groups = [group for group in ([0], single, several) if group]
    for order, group in enumerate(groups):
        fresh = {}
        for hop in group:
            for half in range(2):
                fresh[hop, 0, half] = planes[hop, half]
                fresh[hop, 1, half] = swap(planes[hop, half], "dp", 1)
        parts.update(fresh)
        last = order == len(groups) - 1
        done = finish(
            lay, parts if last else fresh, done, tuple(fresh) if last else (), lanes, feats, width
        )
    g_in, g_out, g_mix = done
    return (loss.reshape(count), g_mix, g_in, g_out)


def solution(mesh):
    placed = (P(("blk", "dp"), None, None), P(), P(), P(), P(("blk", "dp")), P(("blk", "dp")))
    return jax.shard_map(
        on_device,
        mesh=mesh,
        in_specs=placed,
        out_specs=(P(("blk", "dp")), P(), P(), P()),
        check_vma=False,
    )
```

```python
import functools
import math

import jax
import jax.numpy as jnp
import numpy as np
from jax import lax
from jax.experimental import pallas as pl
from jax.experimental.pallas import tpu as pltpu
from jax.sharding import PartitionSpec as P


SCALE = 10.0
SUB = 8
BF16 = jnp.bfloat16
F32 = jnp.float32
VMEM = pl.BlockSpec(memory_space=pltpu.VMEM)
ANY = pl.BlockSpec(memory_space=pl.ANY)


def shape(dims, dtype):
    return jax.ShapeDtypeStruct(tuple(dims), dtype)


def hbm(value):
    return pltpu.with_memory_space_constraint(value, pltpu.MemorySpace.HBM)


def mm(left, right):
    return jnp.dot(left, right, preferred_element_type=F32)


def mm_nt(left, right):
    return lax.dot_general(left, right, (((1,), (1,)), ((), ())), preferred_element_type=F32)


def mm_tn(left, right):
    return lax.dot_general(left, right, (((0,), (0,)), ((), ())), preferred_element_type=F32)


def params(mib):
    return pltpu.CompilerParams(vmem_limit_bytes=mib << 20)


def cost(flops, nbytes):
    return pl.CostEstimate(flops=int(flops), bytes_accessed=int(nbytes), transcendentals=0)


def angle_basis(length, freqs):
    phase = np.mod(np.outer(np.arange(freqs), np.arange(length)), length).astype(np.float32)
    phase = phase * np.float32(2.0 * math.pi / length)
    table = np.concatenate([np.cos(phase), -np.sin(phase)], axis=0).astype(np.float32)
    basis = np.einsum("ka,pq->kpqa", table, np.eye(SUB, dtype=np.float32))
    return jnp.asarray(basis.reshape(2 * freqs * SUB, SUB * length), BF16)


def encode_kernel(freqs, size, rounds, patch_hbm, basis_hbm, mix_hbm, out_hbm, in_hbm, *rest):
    piece_hbms, rest = rest[:size], rest[size:]
    spec, mixed, normed, in_w, units_ref, unit32_ref, norm_ref, rscale_ref, *rest = rest
    patches, basis, mix, out_w, feat, slope, hidden, *sems = rest
    table_sems, patch_sems, out_sems = sems
    count, length, lanes = patches.shape
    filters = mix.shape[1]
    half = freqs * SUB
    per = count // rounds
    groups = per // SUB

    def table(i, source, target):
        return pltpu.make_async_copy(source, target, table_sems.at[i])

    tables = [
        table(i, *pair)
        for i, pair in enumerate(
            [(basis_hbm, basis), (mix_hbm, mix), (in_hbm, in_w), (out_hbm, out_w)]
        )
    ]

    def fetch(r):
        rows = pl.ds(r * per, per)
        return pltpu.make_async_copy(patch_hbm.at[rows], patches.at[rows], patch_sems.at[r])

    tables[0].start()
    fetch(0).start()
    tables[1].start()
    for r in range(1, rounds):
        fetch(r).start()
    tables[2].start()
    tables[3].start()
    tables[0].wait()
    tables[1].wait()

    def one(r, carry):
        fetch(r).wait()
        for s in range(groups):
            g = r * groups + s
            base = pl.multiple_of(g * SUB, SUB)
            block = patches[pl.ds(base, SUB)].reshape(SUB * length, lanes)
            part = mm(basis[...], block).astype(BF16)
            spec[g] = part
            both = mm(part, mix[...])
            real_part, imag_part = both[:half], both[half:]
            powers = real_part * real_part + imag_part * imag_part
            share = 2.0 / (1.0 + powers)
            mixed[g, :half] = real_part * share
            mixed[g, half:] = imag_part * share
            piece = jnp.log1p(powers)
            for k in range(freqs):
                feat[pl.ds(base, SUB), k * filters : (k + 1) * filters] = piece[
                    k * SUB : (k + 1) * SUB
                ]
        return carry

    lax.fori_loop(0, rounds, one, 0)
    features = feat[...]
    removed = features - jnp.mean(features, axis=1, keepdims=True)
    rscale = lax.rsqrt(jnp.mean(removed * removed, axis=1, keepdims=True) + 1e-05)
    normed[...] = (removed * rscale).astype(BF16)
    rscale_ref[...] = jnp.broadcast_to(rscale, rscale_ref.shape)
    deep, width, wide = piece_columns(normed.shape[1], hidden.shape[1], size)
    me = lax.axis_index("blk")
    outs = []
    for i, piece_hbm in enumerate(piece_hbms):
        columns = pl.ds(pl.multiple_of((me ^ i) * deep, 128), deep)
        outs.append(
            pltpu.make_async_copy(
                normed.at[:, columns], piece_hbm.at[:, :deep], out_sems.at[len(outs)]
            )
        )
    for each in outs:
        each.start()
    tables[2].wait()
    preact = mm(normed[...], in_w[...])
    sigm = jax.nn.sigmoid(preact)
    hidden[...] = (preact * sigm).astype(BF16)
    slope[...] = (sigm * (1.0 + preact * (1.0 - sigm))).astype(BF16)
    late = []
    for i, piece_hbm in enumerate(piece_hbms):
        if wide == hidden.shape[1]:
            columns = pl.ds(0, wide)
        else:
            columns = pl.ds(pl.multiple_of((me ^ i) * wide, 128), wide)
        for source, target in (
            (slope, piece_hbm.at[:, deep : deep + width]),
            (hidden.at[:, columns], piece_hbm.at[:, deep + width :]),
        ):
            late.append(
                pltpu.make_async_copy(source, target, out_sems.at[len(outs) + len(late)])
            )
    for each in late:
        each.start()
    tables[3].wait()
    raw = mm(hidden[...], out_w[...])
    norms = jnp.sqrt(jnp.sum(raw * raw, axis=1, keepdims=True) + 1e-06)
    norm_ref[...] = jnp.broadcast_to(norms, norm_ref.shape)
    unit32 = raw / norms
    unit32_ref[...] = unit32
    units_ref[...] = unit32.astype(BF16)
    for each in outs + late:
        each.wait()


def piece_columns(feats, width, size):
    wide = width // size
    return feats // size, width, wide if wide % 128 == 0 else width


def encode(patches, w_mix, w_in, w_out, size):
    count, length, lanes = patches.shape
    filters = w_mix.shape[1]
    feats, width = w_in.shape
    embed = w_out.shape[1]
    freqs = feats // filters
    rounds = 4
    assert count % (rounds * SUB) == 0
    groups = count // SUB
    rows = 2 * freqs * SUB
    piece = (count, sum(piece_columns(feats, width, size)))
    kept = [pltpu.MemorySpace.HBM(piece, BF16)] * size
    near = [
        shape((groups, rows, lanes), BF16),
        shape((groups, rows, filters), F32),
        shape((count, feats), BF16),
        shape(w_in.shape, BF16),
        shape((count, embed), BF16),
        shape((count, embed), F32),
        shape((count, 128), F32),
        shape((count, 128), F32),
    ]
    return pl.pallas_call(
        functools.partial(encode_kernel, freqs, size, rounds),
        in_specs=[ANY] * 5,
        out_shape=kept + near,
        out_specs=[ANY] * len(kept) + [VMEM] * len(near),
        scratch_shapes=[
            pltpu.VMEM(patches.shape, BF16),
            pltpu.VMEM((rows, SUB * length), BF16),
            pltpu.VMEM(w_mix.shape, BF16),
            pltpu.VMEM(w_out.shape, BF16),
            pltpu.VMEM((count, feats), F32),
            pltpu.VMEM((count, width), BF16),
            pltpu.VMEM((count, width), BF16),
            pltpu.SemaphoreType.DMA((4,)),
            pltpu.SemaphoreType.DMA((rounds,)),
            pltpu.SemaphoreType.DMA((3 * size,)),
        ],
        compiler_params=params(24),
        cost_estimate=cost(3e9, 14e6),
    )(*map(hbm, (patches, angle_basis(length, freqs), w_mix, w_out, w_in)))


def exponentials(units, keys, own):
    expo = jnp.exp(SCALE * mm_nt(units, keys))
    if own:
        row = lax.broadcasted_iota(jnp.int32, expo.shape, 0)
        col = lax.broadcasted_iota(jnp.int32, expo.shape, 1)
        expo = jnp.where(row == col, 0.0, expo)
    return expo


def pair_up_kernel(own_ref, other_ref, out_ref):
    rows = own_ref.shape[0]
    own, other = own_ref[...], other_ref[...]
    first = lax.axis_index("dp") % 2 == 0
    out_ref[:rows, :] = jnp.where(first, own, other)
    out_ref[rows:, :] = jnp.where(first, other, own)


def pair_up(own, other):
    rows, width = own.shape
    return pl.pallas_call(
        pair_up_kernel,
        in_specs=[VMEM] * 2,
        out_shape=shape((2 * rows, width), own.dtype),
        out_specs=VMEM,
        compiler_params=params(8),
        cost_estimate=cost(1e3, 1e5),
    )(own, other)


def cross(pair):
    size, peers = lax.axis_size("blk"), lax.axis_size("dp")
    got = []
    for k in range(1, max(size, peers // 2)):
        routes = []
        for blk in range(size):
            for dp in range(peers):
                if dp % 2 == 0 and 2 * k < peers:
                    routes.append((blk * peers + dp, blk * peers + (dp ^ (2 * k))))
                if dp % 2 == 1 and k < size:
                    routes.append((blk * peers + dp, (blk ^ k) * peers + dp))
        got.append(lax.ppermute(pair, ("blk", "dp"), routes))
    return got


def crossed(got_ref, swapped_ref, rows):
    first = lax.axis_index("dp") % 2 == 0

    def along(k, core):
        at = (2 * (k - 1) + core) * rows
        return jnp.where(first, got_ref[at : at + rows, :], swapped_ref[at : at + rows, :])

    def across(k):
        at = 2 * (k - 1) * rows
        low = jnp.where(first, swapped_ref[at : at + rows, :], got_ref[at + rows : at + 2 * rows, :])
        return low

    return along, across


def as_rows(column, count):
    return jnp.broadcast_to(column, (column.shape[0], count)).T


def scores_kernel(
    size,
    peers,
    dev_ref,
    row_ref,
    units_ref,
    pair_ref,
    got_ref,
    swapped_ref,
    local_ref,
    stats_ref,
    loss_ref,
    group_ref,
    around_ref,
):
    units = units_ref[...]
    count = units.shape[0]
    along, across = crossed(got_ref, swapped_ref, count)
    zneg = numer = None
    for i in range(size):
        keys = across(i) if i else units
        group_ref[i * count : (i + 1) * count, :] = keys
        expo = exponentials(units, keys, i == 0)
        total = jnp.sum(expo, axis=1, keepdims=True)
        term = mm(expo.astype(BF16), keys)
        zneg = total if zneg is None else zneg + total
        numer = term if numer is None else numer + term
    me = lax.axis_index("dp")
    dev = dev_ref[...]
    place = (2 * ((dev ^ me) >> 1) + (dev & 1)) * count + row_ref[...]
    place = jnp.broadcast_to(place.astype(F32), (count, count)).T
    lane = lax.broadcasted_iota(jnp.int32, (count, count), 1).astype(F32)
    positive = None
    for i in range(peers):
        k, core = i // 2, i % 2
        source = along(k, core) if k else pair_ref[core * count : (core + 1) * count, :]
        around_ref[i * count : (i + 1) * count, :] = source
        hit = jnp.where(place - float(i * count) == lane, 1.0, 0.0).astype(BF16)
        term = mm(hit, source)
        positive = term if positive is None else positive + term
    spos = SCALE * jnp.sum(units.astype(F32) * positive, axis=1, keepdims=True)
    top = jnp.exp(spos)
    totals = top + zneg
    less = top / totals - 1.0
    coef = SCALE / count
    local_ref[...] = coef * (less * positive + numer / totals)
    loss_ref[...] = as_rows(jnp.log(totals) - spos, count)[:1]
    stats_ref[...] = jnp.zeros(stats_ref.shape, F32)
    stats_ref[0:1, :] = as_rows(totals, count)[:1]
    stats_ref[1:2, :] = as_rows(coef * less, count)[:1]
    stats_ref[2:3, :] = (dev * count + row_ref[...]).astype(F32)


def scores(partner_dev, partner_row, units, pair, got, swapped, size, peers):
    count, embed = units.shape
    return pl.pallas_call(
        functools.partial(scores_kernel, size, peers),
        in_specs=[VMEM] * 6,
        out_shape=[
            shape((count, embed), F32),
            shape((SUB, count), F32),
            shape((1, count), F32),
            shape((size * count, embed), BF16),
            shape((peers * count, embed), BF16),
        ],
        out_specs=[VMEM] * 5,
        compiler_params=params(16),
        cost_estimate=cost(4e8, 1e6),
    )(partner_dev.reshape(1, count), partner_row.reshape(1, count), units, pair, got, swapped)


def upper_kernel(
    size,
    peers,
    group_ref,
    around_ref,
    stats_ref,
    pair_ref,
    got_ref,
    swapped_ref,
    local_ref,
    unit32_ref,
    norm_ref,
    out_ref,
):
    count, _ = local_ref.shape
    coef = SCALE / count
    along, across = crossed(got_ref, swapped_ref, SUB)
    units = group_ref[:count, :]
    keyterm = None
    for i in range(size):
        keys = group_ref[i * count : (i + 1) * count, :]
        expo = exponentials(units, keys, i == 0)
        totals = (across(i) if i else stats_ref[...])[0:1, :]
        term = mm((expo / totals).astype(BF16), keys)
        keyterm = term if keyterm is None else keyterm + term
    mine = lax.axis_index("dp") * count + lax.broadcasted_iota(jnp.int32, (count, count), 0)
    mine = mine.astype(F32)
    chosen = amount = None
    for i in range(peers):
        k, core = i // 2, i % 2
        table = along(k, core) if k else pair_ref[core * SUB : (core + 1) * SUB, :]
        hit = table[2:3, :] == mine
        share = jnp.where(hit, table[1:2, :], 0.0)
        term = mm(jnp.where(hit, 1.0, 0.0).astype(BF16), around_ref[i * count : (i + 1) * count, :])
        chosen = term if chosen is None else chosen + term
        amount = share if amount is None else amount + share
    back = jnp.sum(amount, axis=1, keepdims=True) * chosen
    grad_units = local_ref[...] + coef * keyterm + back
    unit32 = unit32_ref[...]
    tilt = jnp.sum(unit32 * grad_units, axis=1, keepdims=True)
    out_ref[...] = ((grad_units - unit32 * tilt) / norm_ref[:, :1]).astype(BF16)


def upper(group, around, stats, pair, got, swapped, local, unit32, norms, size, peers):
    count, embed = local.shape
    args = [group, around, stats, pair, got, swapped, local, unit32, norms]
    return pl.pallas_call(
        functools.partial(upper_kernel, size, peers),
        in_specs=[VMEM] * len(args),
        out_shape=shape((count, embed), BF16),
        out_specs=VMEM,
        compiler_params=params(16),
        cost_estimate=cost(4e8, 2e6),
    )(*args)


def pre_grads(grad_raw, out_w, slope):
    return (mm_nt(grad_raw, out_w) * slope.astype(F32)).astype(BF16)


def lower_kernel(
    freqs,
    columns,
    raw_ref,
    rscale_ref,
    in_w,
    normed,
    mixed,
    spec,
    out_w_hbm,
    piece_hbm,
    g_mix_ref,
    out_w,
    slope,
    grad_feat,
    sems,
):
    deep, width, _ = columns
    loads = [
        pltpu.make_async_copy(out_w_hbm, out_w, sems.at[0]),
        pltpu.make_async_copy(piece_hbm.at[:, deep : deep + width], slope, sems.at[1]),
    ]
    for each in loads:
        each.start()
    for each in loads:
        each.wait()
    grad_pre = pre_grads(raw_ref[...], out_w[...], slope[...])
    grad_norm = mm_nt(grad_pre, in_w[...])
    xhat = normed[...].astype(F32)
    mean = jnp.mean(grad_norm, axis=1, keepdims=True)
    tilt = jnp.mean(grad_norm * xhat, axis=1, keepdims=True)
    grad_feat[...] = rscale_ref[:, :1] * (grad_norm - mean - xhat * tilt)
    groups, _, filters = mixed.shape
    half = freqs * SUB

    def one(g, total):
        base = pl.multiple_of(g * SUB, SUB)
        grads = jnp.concatenate(
            [grad_feat[pl.ds(base, SUB), k * filters : (k + 1) * filters] for k in range(freqs)],
            axis=0,
        )
        grad_mixed = jnp.concatenate(
            [mixed[g, :half] * grads, mixed[g, half:] * grads], axis=0
        ).astype(BF16)
        return total + mm_tn(grad_mixed, spec[g])

    total = lax.fori_loop(0, groups, one, jnp.zeros((filters, spec.shape[2]), F32), unroll=4)
    g_mix_ref[...] = total.T


def lower(grad_raw, w_out, piece, normed, rscale, in_w, mixed, spec, freqs, columns):
    count, feats = normed.shape
    _, _, filters = mixed.shape
    lanes = spec.shape[2]
    return pl.pallas_call(
        functools.partial(lower_kernel, freqs, columns),
        in_specs=[VMEM] * 6 + [ANY] * 2,
        out_shape=shape((lanes, filters), F32),
        out_specs=VMEM,
        scratch_shapes=[
            pltpu.VMEM(w_out.shape, BF16),
            pltpu.VMEM((count, columns[1]), BF16),
            pltpu.VMEM((count, feats), F32),
            pltpu.SemaphoreType.DMA((2,)),
        ],
        compiler_params=params(20),
        cost_estimate=cost(1e9, 7e6),
    )(grad_raw, rscale, in_w, normed, mixed, spec, hbm(w_out), hbm(piece))


def up_to(rows, unit):
    return -(-rows // unit) * unit


class Layout:
    def __init__(self, lanes, filters, feats, width, embed, size, peers):
        self.size, self.peers = size, peers
        self.in_rows = feats // size // peers
        self.out_rows = width // size // peers
        self.mix_rows = lanes // peers
        self.top = up_to(self.in_rows, 16)
        self.strip = max(16, up_to(self.out_rows, 16))
        self.mix_blocks = -(-self.mix_rows // self.strip)
        self.rows = self.top + self.strip
        self.width = width
        assert embed == 128 and filters == 128 and (1 + self.mix_blocks) * 128 <= width

    def mix_parts(self):
        for block in range(self.mix_blocks):
            start = block * self.strip
            yield start, min(self.strip, self.mix_rows - start), slice(128 * (block + 1), 128 * (block + 2))


def weights_kernel(lay, columns, *refs):
    size, peers = lay.size, lay.peers
    pieces, raws, rest = refs[:size], refs[size : 2 * size], refs[2 * size :]
    out_w_ref, mix_ref, keep_ref, away_ref, g_in, g_out = rest
    deep, width, wide = columns
    share = width // size
    for i in range(size):
        raw = raws[i][...]
        grad_pre = pre_grads(raw, out_w_ref[...], pieces[i][:, deep : deep + width])
        term_in = mm_tn(pieces[i][:, :deep], grad_pre)
        term_out = mm_tn(pieces[i][:, deep + width :], raw)
        if i == 0:
            g_in[...] = term_in
            g_out[...] = term_out
        else:
            g_in[...] += term_in
            g_out[...] += term_out
    me = lax.axis_index("dp")
    first = 0 if wide == share else lax.axis_index("blk") * share
    keep_ref[...] = jnp.zeros(keep_ref.shape, F32)
    away_ref[...] = jnp.zeros(away_ref.shape, BF16)
    for slot in range(peers):
        owner = me ^ slot
        target = away_ref if slot & 1 else keep_ref
        at = slot >> 1
        target[at, : lay.in_rows, :] = g_in[pl.ds(owner * lay.in_rows, lay.in_rows), :].astype(target.dtype)
        target[at, lay.top : lay.top + lay.out_rows, :128] = g_out[
            pl.ds(first + owner * lay.out_rows, lay.out_rows), :
        ].astype(target.dtype)
        for start, rows, cols in lay.mix_parts():
            target[at, lay.top : lay.top + rows, cols] = mix_ref[
                pl.ds(owner * lay.mix_rows + start, rows), :
            ].astype(target.dtype)


def weight_grads(lay, columns, pieces, raws, w_out, g_mix):
    deep, width, wide = columns
    block = (lay.peers // 2, lay.rows, lay.width)
    args = [*pieces, *raws, w_out, g_mix]
    return pl.pallas_call(
        functools.partial(weights_kernel, lay, columns),
        in_specs=[VMEM] * len(args),
        out_shape=[shape(block, F32), shape(block, BF16)],
        out_specs=[VMEM] * 2,
        scratch_shapes=[pltpu.VMEM((deep, width), F32), pltpu.VMEM((wide, 128), F32)],
        compiler_params=params(16),
        cost_estimate=cost(6e8, 4e6),
    )(*args)


def pair_kernel(keep_ref, got_ref, own_ref, *out_refs):
    own_ref[...] = keep_ref[0] + got_ref[0].astype(F32)
    for i, out_ref in enumerate(out_refs):
        out_ref[...] = (keep_ref[i + 1] + got_ref[i + 1].astype(F32)).astype(BF16)


def pair_sum(keep, got):
    slots, rows, width = keep.shape
    return pl.pallas_call(
        pair_kernel,
        in_specs=[VMEM] * 2,
        out_shape=[shape((rows, width), F32)] + [shape((rows, width), BF16)] * (slots - 1),
        out_specs=[VMEM] * slots,
        compiler_params=params(8),
        cost_estimate=cost(1e6, 2e6),
    )(keep, got)


def total_kernel(own_ref, *refs):
    total = own_ref[...]
    for each in refs[:-1]:
        total = total + each[...].astype(F32)
    refs[-1][...] = total.astype(BF16)


def total_sum(own, got):
    return pl.pallas_call(
        total_kernel,
        in_specs=[VMEM] * (1 + len(got)),
        out_shape=shape(own.shape, BF16),
        out_specs=VMEM,
        compiler_params=params(8),
        cost_estimate=cost(1e6, 1e6),
    )(own, *got)


def finish_kernel(lay, parts, done, closing, *refs):
    slots = lay.peers // 2
    part_refs, refs = dict(zip(parts, refs)), refs[len(parts) :]
    if done:
        refs = refs[2:]
    g_in_hbm, g_out_hbm, *refs = refs
    if closing:
        g_mix_ref, *refs = refs
    stage, strip_stage, sems, strip_sems = refs
    me_blk, me_dp = lax.axis_index("blk"), lax.axis_index("dp")
    copies = []
    slot = 0
    for (hop, core, half), source in part_refs.items():
        if closing and (hop, core, half) not in closing:
            continue
        for z in range(slots // 2):
            at = z * lay.rows
            owner = (me_blk ^ hop) * lay.peers + (me_dp ^ (half * slots + 2 * z + core))
            stage[slot] = source[at : at + lay.in_rows, :].astype(F32)
            strip = at + lay.top
            strip_stage[slot] = source[strip : strip + lay.out_rows, :128].astype(F32)
            for kept, target, rows, sem in (
                (stage, g_in_hbm, lay.in_rows, sems),
                (strip_stage, g_out_hbm, lay.out_rows, strip_sems),
            ):
                copy = pltpu.make_async_copy(
                    kept.at[slot], target.at[pl.ds(owner * rows, rows), :], sem.at[slot]
                )
                copy.start()
                copies.append(copy)
            slot += 1
    if closing:
        for core in range(2):
            for half in range(2):
                for z in range(slots // 2):
                    strip = z * lay.rows + lay.top
                    owner = me_dp ^ (half * slots + 2 * z + core)
                    for start, rows, cols in lay.mix_parts():
                        terms = [
                            part_refs[hop, core, half][strip : strip + rows, cols].astype(F32)
                            for hop in range(lay.size)
                        ]
                        while len(terms) > 1:
                            terms = [terms[t] + terms[t + 1] for t in range(0, len(terms), 2)]
                        g_mix_ref[pl.ds(owner * lay.mix_rows + start, rows), :] = terms[0]
    for copy in copies:
        copy.wait()


def finish(lay, parts, done, closing, lanes, feats, width):
    slots = (len(closing) if closing else len(parts)) * lay.peers // 4
    outs = [shape((feats, width), F32), shape((width, 128), F32)]
    specs = [ANY, ANY]
    if closing:
        outs.append(shape((lanes, 128), F32))
        specs.append(VMEM)
    return pl.pallas_call(
        functools.partial(finish_kernel, lay, tuple(parts), bool(done), closing),
        in_specs=[VMEM] * len(parts) + [ANY] * len(done),
        out_shape=outs,
        out_specs=specs,
        scratch_shapes=[
            pltpu.VMEM((slots, lay.in_rows, lay.width), F32),
            pltpu.VMEM((slots, lay.out_rows, 128), F32),
            pltpu.SemaphoreType.DMA((slots,)),
            pltpu.SemaphoreType.DMA((slots,)),
        ],
        input_output_aliases={len(parts) + i: i for i in range(len(done))},
        compiler_params=params(24),
        cost_estimate=cost(1e6, 8e6),
    )(*parts.values(), *done)


def stack_kernel(*refs):
    rows = refs[0].shape[0]
    for i, each in enumerate(refs[:-1]):
        refs[-1][i * rows : (i + 1) * rows, :] = each[...]


def stack(blocks):
    rows, width = blocks[0].shape
    return pl.pallas_call(
        stack_kernel,
        in_specs=[VMEM] * len(blocks),
        out_shape=shape((len(blocks) * rows, width), blocks[0].dtype),
        out_specs=VMEM,
        compiler_params=params(8),
        cost_estimate=cost(1e3, 1e5),
    )(*blocks)


def swap(block, axis, bit):
    size = lax.axis_size(axis)
    return lax.ppermute(block, axis, [(src, src ^ bit) for src in range(size)])


def spread(block, axis, hops):
    return [block] + [swap(block, axis, hop) for hop in hops]


def on_device(patches, w_mix, w_in, w_out, partner_dev, partner_row):
    count, _, lanes = patches.shape
    filters = w_mix.shape[1]
    feats, width = w_in.shape
    embed = w_out.shape[1]
    freqs = feats // filters
    size, peers = lax.axis_size("blk"), lax.axis_size("dp")
    assert size & (size - 1) == 0 and peers & (peers - 1) == 0 and peers > 1
    across, along = range(1, size), range(2, peers, 2)
    columns = piece_columns(feats, width, size)
    lay = Layout(lanes, filters, feats, width, embed, size, peers)

    *early, spec, mixed, normed, in_w, units, unit32, norms, rscale = encode(
        patches, w_mix, w_in, w_out, size
    )
    other = swap(units, "dp", 1)
    pair = pair_up(units, other)
    got = stack(lax.optimization_barrier(cross(pair)))
    factors = [early[0]] + [swap(early[hop], "blk", hop) for hop in across]
    swapped = swap(got, "dp", 1)
    local, stats, loss, group, around = scores(
        partner_dev, partner_row, units, pair, got, swapped, size, peers
    )
    other = swap(stats, "dp", 1)
    pair = pair_up(stats, other)
    got = stack(lax.optimization_barrier(cross(pair)))
    swapped = swap(got, "dp", 1)
    grad_raw = upper(group, around, stats, pair, got, swapped, local, unit32, norms, size, peers)
    raws = spread(grad_raw, "blk", across)
    g_mix = lower(grad_raw, w_out, early[0], normed, rscale, in_w, mixed, spec, freqs, columns)
    keep, away = weight_grads(lay, columns, factors, raws, w_out, g_mix)
    got = swap(away, "dp", 1)
    own, *sends = pair_sum(keep, got)
    got = [swap(block, "dp", hop) for block, hop in zip(sends, along)]
    share = total_sum(own, got)
    shares = spread(share, "dp", along)
    middle = len(shares) // 2
    planes = {(0, 0): stack(shares[:middle]), (0, 1): stack(shares[middle:])}
    single = [hop for hop in across if hop & (hop - 1) == 0]
    several = [hop for hop in across if hop & (hop - 1)]
    for half in range(2):
        for hop in single:
            planes[hop, half] = swap(planes[0, half], "blk", hop)
        for hop in several:
            bit = hop & -hop if half else 1 << (hop.bit_length() - 1)
            planes[hop, half] = swap(planes[hop ^ bit, half], "blk", bit)
    parts, done = {}, []
    groups = [group for group in ([0], single, several) if group]
    for order, group in enumerate(groups):
        fresh = {}
        for hop in group:
            for half in range(2):
                fresh[hop, 0, half] = planes[hop, half]
                fresh[hop, 1, half] = swap(planes[hop, half], "dp", 1)
        parts.update(fresh)
        last = order == len(groups) - 1
        done = finish(
            lay, parts if last else fresh, done, tuple(fresh) if last else (), lanes, feats, width
        )
    g_in, g_out, g_mix = done
    return (loss.reshape(count), g_mix, g_in, g_out)


def solution(mesh):
    placed = (P(("blk", "dp"), None, None), P(), P(), P(), P(("blk", "dp")), P(("blk", "dp")))
    return jax.shard_map(
        on_device,
        mesh=mesh,
        in_specs=placed,
        out_specs=(P(("blk", "dp")), P(), P(), P()),
        check_vma=False,
    )
```

```python
import functools
import math

import jax
import jax.numpy as jnp
import numpy as np
from jax import lax
from jax.experimental import pallas as pl
from jax.experimental.pallas import tpu as pltpu
from jax.sharding import PartitionSpec as P


SCALE = 10.0
SUB = 8
BF16 = jnp.bfloat16
F32 = jnp.float32
VMEM = pl.BlockSpec(memory_space=pltpu.VMEM)
ANY = pl.BlockSpec(memory_space=pl.ANY)


def shape(dims, dtype):
    return jax.ShapeDtypeStruct(tuple(dims), dtype)


def hbm(value):
    return pltpu.with_memory_space_constraint(value, pltpu.MemorySpace.HBM)


def mm(left, right):
    return jnp.dot(left, right, preferred_element_type=F32)


def mm_nt(left, right):
    return lax.dot_general(left, right, (((1,), (1,)), ((), ())), preferred_element_type=F32)


def mm_tn(left, right):
    return lax.dot_general(left, right, (((0,), (0,)), ((), ())), preferred_element_type=F32)


def params(mib):
    return pltpu.CompilerParams(vmem_limit_bytes=mib << 20)


def cost(flops, nbytes):
    return pl.CostEstimate(flops=int(flops), bytes_accessed=int(nbytes), transcendentals=0)


def angle_basis(length, freqs):
    phase = np.mod(np.outer(np.arange(freqs), np.arange(length)), length).astype(np.float32)
    phase = phase * np.float32(2.0 * math.pi / length)
    table = np.concatenate([np.cos(phase), -np.sin(phase)], axis=0).astype(np.float32)
    basis = np.einsum("ka,pq->kpqa", table, np.eye(SUB, dtype=np.float32))
    return jnp.asarray(basis.reshape(2 * freqs * SUB, SUB * length), BF16)


def encode_kernel(freqs, size, rounds, patch_hbm, basis_hbm, mix_hbm, out_hbm, in_hbm, *rest):
    piece_hbms, rest = rest[:size], rest[size:]
    spec, mixed, normed, in_w, out_w, slope, units_ref, unit32_ref, norm_ref, rscale_ref, *rest = rest
    patches, basis, mix, feat, hidden, *sems = rest
    table_sems, patch_sems, out_sems = sems
    count, length, lanes = patches.shape
    filters = mix.shape[1]
    half = freqs * SUB
    per = count // rounds
    groups = per // SUB

    def table(i, source, target):
        return pltpu.make_async_copy(source, target, table_sems.at[i])

    tables = [
        table(i, *pair)
        for i, pair in enumerate(
            [(basis_hbm, basis), (mix_hbm, mix), (in_hbm, in_w), (out_hbm, out_w)]
        )
    ]

    def fetch(r):
        rows = pl.ds(r * per, per)
        return pltpu.make_async_copy(patch_hbm.at[rows], patches.at[rows], patch_sems.at[r])

    tables[0].start()
    fetch(0).start()
    tables[1].start()
    for r in range(1, rounds):
        fetch(r).start()
    tables[2].start()
    tables[3].start()
    tables[0].wait()
    tables[1].wait()

    def one(r, carry):
        fetch(r).wait()
        for s in range(groups):
            g = r * groups + s
            base = pl.multiple_of(g * SUB, SUB)
            block = patches[pl.ds(base, SUB)].reshape(SUB * length, lanes)
            part = mm(basis[...], block).astype(BF16)
            spec[g] = part
            both = mm(part, mix[...])
            real_part, imag_part = both[:half], both[half:]
            powers = real_part * real_part + imag_part * imag_part
            share = 2.0 / (1.0 + powers)
            mixed[g, :half] = real_part * share
            mixed[g, half:] = imag_part * share
            piece = jnp.log1p(powers)
            for k in range(freqs):
                feat[pl.ds(base, SUB), k * filters : (k + 1) * filters] = piece[
                    k * SUB : (k + 1) * SUB
                ]
        return carry

    lax.fori_loop(0, rounds, one, 0)
    features = feat[...]
    removed = features - jnp.mean(features, axis=1, keepdims=True)
    rscale = lax.rsqrt(jnp.mean(removed * removed, axis=1, keepdims=True) + 1e-05)
    normed[...] = (removed * rscale).astype(BF16)
    rscale_ref[...] = jnp.broadcast_to(rscale, rscale_ref.shape)
    deep, width, wide = piece_columns(normed.shape[1], hidden.shape[1], size)
    me = lax.axis_index("blk")
    outs = []
    for i, piece_hbm in enumerate(piece_hbms):
        columns = pl.ds(pl.multiple_of((me ^ i) * deep, 128), deep)
        outs.append(
            pltpu.make_async_copy(
                normed.at[:, columns], piece_hbm.at[:, :deep], out_sems.at[len(outs)]
            )
        )
    for each in outs:
        each.start()
    tables[2].wait()
    preact = mm(normed[...], in_w[...])
    sigm = jax.nn.sigmoid(preact)
    hidden[...] = (preact * sigm).astype(BF16)
    slope[...] = (sigm * (1.0 + preact * (1.0 - sigm))).astype(BF16)
    late = []
    for i, piece_hbm in enumerate(piece_hbms):
        if wide == hidden.shape[1]:
            columns = pl.ds(0, wide)
        else:
            columns = pl.ds(pl.multiple_of((me ^ i) * wide, 128), wide)
        for source, target in (
            (slope, piece_hbm.at[:, deep : deep + width]),
            (hidden.at[:, columns], piece_hbm.at[:, deep + width :]),
        ):
            late.append(
                pltpu.make_async_copy(source, target, out_sems.at[len(outs) + len(late)])
            )
    for each in late:
        each.start()
    tables[3].wait()
    raw = mm(hidden[...], out_w[...])
    norms = jnp.sqrt(jnp.sum(raw * raw, axis=1, keepdims=True) + 1e-06)
    norm_ref[...] = jnp.broadcast_to(norms, norm_ref.shape)
    unit32 = raw / norms
    unit32_ref[...] = unit32
    units_ref[...] = unit32.astype(BF16)
    for each in outs + late:
        each.wait()


def piece_columns(feats, width, size):
    wide = width // size
    return feats // size, width, wide if wide % 128 == 0 else width


def encode(patches, w_mix, w_in, w_out, size):
    count, length, lanes = patches.shape
    filters = w_mix.shape[1]
    feats, width = w_in.shape
    embed = w_out.shape[1]
    freqs = feats // filters
    rounds = 4
    assert count % (rounds * SUB) == 0
    groups = count // SUB
    rows = 2 * freqs * SUB
    piece = (count, sum(piece_columns(feats, width, size)))
    kept = [pltpu.MemorySpace.HBM(piece, BF16)] * size
    near = [
        shape((groups, rows, lanes), BF16),
        shape((groups, rows, filters), F32),
        shape((count, feats), BF16),
        shape(w_in.shape, BF16),
        shape(w_out.shape, BF16),
        shape((count, width), BF16),
        shape((count, embed), BF16),
        shape((count, embed), F32),
        shape((count, 128), F32),
        shape((count, 128), F32),
    ]
    return pl.pallas_call(
        functools.partial(encode_kernel, freqs, size, rounds),
        in_specs=[ANY] * 5,
        out_shape=kept + near,
        out_specs=[ANY] * len(kept) + [VMEM] * len(near),
        scratch_shapes=[
            pltpu.VMEM(patches.shape, BF16),
            pltpu.VMEM((rows, SUB * length), BF16),
            pltpu.VMEM(w_mix.shape, BF16),
            pltpu.VMEM((count, feats), F32),
            pltpu.VMEM((count, width), BF16),
            pltpu.SemaphoreType.DMA((4,)),
            pltpu.SemaphoreType.DMA((rounds,)),
            pltpu.SemaphoreType.DMA((3 * size,)),
        ],
        compiler_params=params(24),
        cost_estimate=cost(3e9, 14e6),
    )(*map(hbm, (patches, angle_basis(length, freqs), w_mix, w_out, w_in)))


def exponentials(units, keys, own):
    expo = jnp.exp(SCALE * mm_nt(units, keys))
    if own:
        row = lax.broadcasted_iota(jnp.int32, expo.shape, 0)
        col = lax.broadcasted_iota(jnp.int32, expo.shape, 1)
        expo = jnp.where(row == col, 0.0, expo)
    return expo


def pair_up_kernel(own_ref, other_ref, out_ref):
    rows = own_ref.shape[0]
    own, other = own_ref[...], other_ref[...]
    first = lax.axis_index("dp") % 2 == 0
    out_ref[:rows, :] = jnp.where(first, own, other)
    out_ref[rows:, :] = jnp.where(first, other, own)


def pair_up(own, other):
    rows, width = own.shape
    return pl.pallas_call(
        pair_up_kernel,
        in_specs=[VMEM] * 2,
        out_shape=shape((2 * rows, width), own.dtype),
        out_specs=VMEM,
        compiler_params=params(8),
        cost_estimate=cost(1e3, 1e5),
    )(own, other)


def cross(pair):
    size, peers = lax.axis_size("blk"), lax.axis_size("dp")
    got = []
    for k in range(1, max(size, peers // 2)):
        routes = []
        for blk in range(size):
            for dp in range(peers):
                if dp % 2 == 0 and 2 * k < peers:
                    routes.append((blk * peers + dp, blk * peers + (dp ^ (2 * k))))
                if dp % 2 == 1 and k < size:
                    routes.append((blk * peers + dp, (blk ^ k) * peers + dp))
        got.append(lax.ppermute(pair, ("blk", "dp"), routes))
    return got


def crossed(got_ref, swapped_ref, rows):
    first = lax.axis_index("dp") % 2 == 0

    def along(k, core):
        at = (2 * (k - 1) + core) * rows
        return jnp.where(first, got_ref[at : at + rows, :], swapped_ref[at : at + rows, :])

    def across(k):
        at = 2 * (k - 1) * rows
        low = jnp.where(first, swapped_ref[at : at + rows, :], got_ref[at + rows : at + 2 * rows, :])
        return low

    return along, across


def as_rows(column, count):
    return jnp.broadcast_to(column, (column.shape[0], count)).T


def scores_kernel(
    size,
    peers,
    dev_ref,
    row_ref,
    units_ref,
    pair_ref,
    got_ref,
    swapped_ref,
    local_ref,
    stats_ref,
    loss_ref,
    group_ref,
    around_ref,
):
    units = units_ref[...]
    count = units.shape[0]
    along, across = crossed(got_ref, swapped_ref, count)
    zneg = numer = None
    for i in range(size):
        keys = across(i) if i else units
        group_ref[i * count : (i + 1) * count, :] = keys
        expo = exponentials(units, keys, i == 0)
        total = jnp.sum(expo, axis=1, keepdims=True)
        term = mm(expo.astype(BF16), keys)
        zneg = total if zneg is None else zneg + total
        numer = term if numer is None else numer + term
    me = lax.axis_index("dp")
    dev = dev_ref[...]
    place = (2 * ((dev ^ me) >> 1) + (dev & 1)) * count + row_ref[...]
    place = jnp.broadcast_to(place.astype(F32), (count, count)).T
    lane = lax.broadcasted_iota(jnp.int32, (count, count), 1).astype(F32)
    positive = None
    for i in range(peers):
        k, core = i // 2, i % 2
        source = along(k, core) if k else pair_ref[core * count : (core + 1) * count, :]
        around_ref[i * count : (i + 1) * count, :] = source
        hit = jnp.where(place - float(i * count) == lane, 1.0, 0.0).astype(BF16)
        term = mm(hit, source)
        positive = term if positive is None else positive + term
    spos = SCALE * jnp.sum(units.astype(F32) * positive, axis=1, keepdims=True)
    top = jnp.exp(spos)
    totals = top + zneg
    less = top / totals - 1.0
    coef = SCALE / count
    local_ref[...] = coef * (less * positive + numer / totals)
    loss_ref[...] = as_rows(jnp.log(totals) - spos, count)[:1]
    stats_ref[...] = jnp.zeros(stats_ref.shape, F32)
    stats_ref[0:1, :] = as_rows(totals, count)[:1]
    stats_ref[1:2, :] = as_rows(coef * less, count)[:1]
    stats_ref[2:3, :] = (dev * count + row_ref[...]).astype(F32)


def scores(partner_dev, partner_row, units, pair, got, swapped, size, peers):
    count, embed = units.shape
    return pl.pallas_call(
        functools.partial(scores_kernel, size, peers),
        in_specs=[VMEM] * 6,
        out_shape=[
            shape((count, embed), F32),
            shape((SUB, count), F32),
            shape((1, count), F32),
            shape((size * count, embed), BF16),
            shape((peers * count, embed), BF16),
        ],
        out_specs=[VMEM] * 5,
        compiler_params=params(16),
        cost_estimate=cost(4e8, 1e6),
    )(partner_dev.reshape(1, count), partner_row.reshape(1, count), units, pair, got, swapped)


def upper_kernel(
    size,
    peers,
    group_ref,
    around_ref,
    stats_ref,
    pair_ref,
    got_ref,
    swapped_ref,
    local_ref,
    unit32_ref,
    norm_ref,
    out_ref,
):
    count, _ = local_ref.shape
    coef = SCALE / count
    along, across = crossed(got_ref, swapped_ref, SUB)
    units = group_ref[:count, :]
    keyterm = None
    for i in range(size):
        keys = group_ref[i * count : (i + 1) * count, :]
        expo = exponentials(units, keys, i == 0)
        totals = (across(i) if i else stats_ref[...])[0:1, :]
        term = mm((expo / totals).astype(BF16), keys)
        keyterm = term if keyterm is None else keyterm + term
    mine = lax.axis_index("dp") * count + lax.broadcasted_iota(jnp.int32, (count, count), 0)
    mine = mine.astype(F32)
    chosen = amount = None
    for i in range(peers):
        k, core = i // 2, i % 2
        table = along(k, core) if k else pair_ref[core * SUB : (core + 1) * SUB, :]
        hit = table[2:3, :] == mine
        share = jnp.where(hit, table[1:2, :], 0.0)
        term = mm(jnp.where(hit, 1.0, 0.0).astype(BF16), around_ref[i * count : (i + 1) * count, :])
        chosen = term if chosen is None else chosen + term
        amount = share if amount is None else amount + share
    back = jnp.sum(amount, axis=1, keepdims=True) * chosen
    grad_units = local_ref[...] + coef * keyterm + back
    unit32 = unit32_ref[...]
    tilt = jnp.sum(unit32 * grad_units, axis=1, keepdims=True)
    out_ref[...] = ((grad_units - unit32 * tilt) / norm_ref[:, :1]).astype(BF16)


def upper(group, around, stats, pair, got, swapped, local, unit32, norms, size, peers):
    count, embed = local.shape
    args = [group, around, stats, pair, got, swapped, local, unit32, norms]
    return pl.pallas_call(
        functools.partial(upper_kernel, size, peers),
        in_specs=[VMEM] * len(args),
        out_shape=shape((count, embed), BF16),
        out_specs=VMEM,
        compiler_params=params(16),
        cost_estimate=cost(4e8, 2e6),
    )(*args)


def pre_grads(grad_raw, out_w, slope):
    return (mm_nt(grad_raw, out_w) * slope.astype(F32)).astype(BF16)


def lower_kernel(
    freqs, raw_ref, rscale_ref, in_w, out_w, slope, normed, mixed, spec, g_mix_ref, grad_feat
):
    grad_pre = pre_grads(raw_ref[...], out_w[...], slope[...])
    grad_norm = mm_nt(grad_pre, in_w[...])
    xhat = normed[...].astype(F32)
    mean = jnp.mean(grad_norm, axis=1, keepdims=True)
    tilt = jnp.mean(grad_norm * xhat, axis=1, keepdims=True)
    grad_feat[...] = rscale_ref[:, :1] * (grad_norm - mean - xhat * tilt)
    groups, _, filters = mixed.shape
    half = freqs * SUB

    def one(g, total):
        base = pl.multiple_of(g * SUB, SUB)
        grads = jnp.concatenate(
            [grad_feat[pl.ds(base, SUB), k * filters : (k + 1) * filters] for k in range(freqs)],
            axis=0,
        )
        grad_mixed = jnp.concatenate(
            [mixed[g, :half] * grads, mixed[g, half:] * grads], axis=0
        ).astype(BF16)
        return total + mm_tn(grad_mixed, spec[g])

    total = lax.fori_loop(0, groups, one, jnp.zeros((filters, spec.shape[2]), F32), unroll=16)
    g_mix_ref[...] = total.T


def lower(grad_raw, rscale, in_w, out_w, slope, normed, mixed, spec, freqs):
    filters, lanes = mixed.shape[2], spec.shape[2]
    return pl.pallas_call(
        functools.partial(lower_kernel, freqs),
        in_specs=[VMEM] * 8,
        out_shape=shape((lanes, filters), F32),
        out_specs=VMEM,
        scratch_shapes=[pltpu.VMEM(normed.shape, F32)],
        compiler_params=params(20),
        cost_estimate=cost(1e9, 7e6),
    )(grad_raw, rscale, in_w, out_w, slope, normed, mixed, spec)


def up_to(rows, unit):
    return -(-rows // unit) * unit


class Layout:
    def __init__(self, lanes, filters, feats, width, embed, size, peers):
        self.size, self.peers = size, peers
        self.in_rows = feats // size // peers
        self.out_rows = width // size // peers
        self.mix_rows = lanes // peers
        self.top = up_to(self.in_rows, 16)
        self.strip = max(16, up_to(self.out_rows, 16))
        self.mix_blocks = -(-self.mix_rows // self.strip)
        self.rows = self.top + self.strip
        self.width = width
        assert embed == 128 and filters == 128 and (1 + self.mix_blocks) * 128 <= width

    def mix_parts(self):
        for block in range(self.mix_blocks):
            start = block * self.strip
            yield start, min(self.strip, self.mix_rows - start), slice(128 * (block + 1), 128 * (block + 2))


def weights_kernel(lay, columns, *refs):
    size, peers = lay.size, lay.peers
    pieces, raws, rest = refs[:size], refs[size : 2 * size], refs[2 * size :]
    out_w_ref, mix_ref, keep_ref, away_ref, g_in, g_out = rest
    deep, width, wide = columns
    share = width // size
    for i in range(size):
        raw = raws[i][...]
        grad_pre = pre_grads(raw, out_w_ref[...], pieces[i][:, deep : deep + width])
        term_in = mm_tn(pieces[i][:, :deep], grad_pre)
        term_out = mm_tn(pieces[i][:, deep + width :], raw)
        if i == 0:
            g_in[...] = term_in
            g_out[...] = term_out
        else:
            g_in[...] += term_in
            g_out[...] += term_out
    me = lax.axis_index("dp")
    first = 0 if wide == share else lax.axis_index("blk") * share
    keep_ref[...] = jnp.zeros(keep_ref.shape, F32)
    away_ref[...] = jnp.zeros(away_ref.shape, BF16)
    for slot in range(peers):
        owner = me ^ slot
        target = away_ref if slot & 1 else keep_ref
        at = slot >> 1
        target[at, : lay.in_rows, :] = g_in[pl.ds(owner * lay.in_rows, lay.in_rows), :].astype(target.dtype)
        target[at, lay.top : lay.top + lay.out_rows, :128] = g_out[
            pl.ds(first + owner * lay.out_rows, lay.out_rows), :
        ].astype(target.dtype)
        for start, rows, cols in lay.mix_parts():
            target[at, lay.top : lay.top + rows, cols] = mix_ref[
                pl.ds(owner * lay.mix_rows + start, rows), :
            ].astype(target.dtype)


def weight_grads(lay, columns, pieces, raws, w_out, g_mix):
    deep, width, wide = columns
    block = (lay.peers // 2, lay.rows, lay.width)
    args = [*pieces, *raws, w_out, g_mix]
    return pl.pallas_call(
        functools.partial(weights_kernel, lay, columns),
        in_specs=[VMEM] * len(args),
        out_shape=[shape(block, F32), shape(block, BF16)],
        out_specs=[VMEM] * 2,
        scratch_shapes=[pltpu.VMEM((deep, width), F32), pltpu.VMEM((wide, 128), F32)],
        compiler_params=params(16),
        cost_estimate=cost(6e8, 4e6),
    )(*args)


def pair_kernel(keep_ref, got_ref, own_ref, *out_refs):
    own_ref[...] = keep_ref[0] + got_ref[0].astype(F32)
    for i, out_ref in enumerate(out_refs):
        out_ref[...] = (keep_ref[i + 1] + got_ref[i + 1].astype(F32)).astype(BF16)


def pair_sum(keep, got):
    slots, rows, width = keep.shape
    return pl.pallas_call(
        pair_kernel,
        in_specs=[VMEM] * 2,
        out_shape=[shape((rows, width), F32)] + [shape((rows, width), BF16)] * (slots - 1),
        out_specs=[VMEM] * slots,
        compiler_params=params(8),
        cost_estimate=cost(1e6, 2e6),
    )(keep, got)


def total_kernel(own_ref, *refs):
    total = own_ref[...]
    for each in refs[:-1]:
        total = total + each[...].astype(F32)
    refs[-1][...] = total.astype(BF16)


def total_sum(own, got):
    return pl.pallas_call(
        total_kernel,
        in_specs=[VMEM] * (1 + len(got)),
        out_shape=shape(own.shape, BF16),
        out_specs=VMEM,
        compiler_params=params(8),
        cost_estimate=cost(1e6, 1e6),
    )(own, *got)


def finish_kernel(lay, parts, done, closing, *refs):
    slots = lay.peers // 2
    part_refs, refs = dict(zip(parts, refs)), refs[len(parts) :]
    if done:
        refs = refs[2:]
    g_in_hbm, g_out_hbm, *refs = refs
    if closing:
        g_mix_ref, *refs = refs
    stage, strip_stage, sems, strip_sems = refs
    me_blk, me_dp = lax.axis_index("blk"), lax.axis_index("dp")
    copies = []
    slot = 0
    for (hop, core, half), source in part_refs.items():
        if closing and (hop, core, half) not in closing:
            continue
        for z in range(slots // 2):
            at = z * lay.rows
            owner = (me_blk ^ hop) * lay.peers + (me_dp ^ (half * slots + 2 * z + core))
            stage[slot] = source[at : at + lay.in_rows, :].astype(F32)
            strip = at + lay.top
            strip_stage[slot] = source[strip : strip + lay.out_rows, :128].astype(F32)
            for kept, target, rows, sem in (
                (stage, g_in_hbm, lay.in_rows, sems),
                (strip_stage, g_out_hbm, lay.out_rows, strip_sems),
            ):
                copy = pltpu.make_async_copy(
                    kept.at[slot], target.at[pl.ds(owner * rows, rows), :], sem.at[slot]
                )
                copy.start()
                copies.append(copy)
            slot += 1
    if closing:
        for core in range(2):
            for half in range(2):
                for z in range(slots // 2):
                    strip = z * lay.rows + lay.top
                    owner = me_dp ^ (half * slots + 2 * z + core)
                    for start, rows, cols in lay.mix_parts():
                        terms = [
                            part_refs[hop, core, half][strip : strip + rows, cols].astype(F32)
                            for hop in range(lay.size)
                        ]
                        while len(terms) > 1:
                            terms = [terms[t] + terms[t + 1] for t in range(0, len(terms), 2)]
                        g_mix_ref[pl.ds(owner * lay.mix_rows + start, rows), :] = terms[0]
    for copy in copies:
        copy.wait()


def finish(lay, parts, done, closing, lanes, feats, width):
    slots = (len(closing) if closing else len(parts)) * lay.peers // 4
    outs = [shape((feats, width), F32), shape((width, 128), F32)]
    specs = [ANY, ANY]
    if closing:
        outs.append(shape((lanes, 128), F32))
        specs.append(VMEM)
    return pl.pallas_call(
        functools.partial(finish_kernel, lay, tuple(parts), bool(done), closing),
        in_specs=[VMEM] * len(parts) + [ANY] * len(done),
        out_shape=outs,
        out_specs=specs,
        scratch_shapes=[
            pltpu.VMEM((slots, lay.in_rows, lay.width), F32),
            pltpu.VMEM((slots, lay.out_rows, 128), F32),
            pltpu.SemaphoreType.DMA((slots,)),
            pltpu.SemaphoreType.DMA((slots,)),
        ],
        input_output_aliases={len(parts) + i: i for i in range(len(done))},
        compiler_params=params(24),
        cost_estimate=cost(1e6, 8e6),
    )(*parts.values(), *done)


def stack_kernel(*refs):
    rows = refs[0].shape[0]
    for i, each in enumerate(refs[:-1]):
        refs[-1][i * rows : (i + 1) * rows, :] = each[...]


def stack(blocks):
    rows, width = blocks[0].shape
    return pl.pallas_call(
        stack_kernel,
        in_specs=[VMEM] * len(blocks),
        out_shape=shape((len(blocks) * rows, width), blocks[0].dtype),
        out_specs=VMEM,
        compiler_params=params(8),
        cost_estimate=cost(1e3, 1e5),
    )(*blocks)


def swap(block, axis, bit):
    size = lax.axis_size(axis)
    return lax.ppermute(block, axis, [(src, src ^ bit) for src in range(size)])


def spread(block, axis, hops):
    return [block] + [swap(block, axis, hop) for hop in hops]


def on_device(patches, w_mix, w_in, w_out, partner_dev, partner_row):
    count, _, lanes = patches.shape
    filters = w_mix.shape[1]
    feats, width = w_in.shape
    embed = w_out.shape[1]
    freqs = feats // filters
    size, peers = lax.axis_size("blk"), lax.axis_size("dp")
    assert size & (size - 1) == 0 and peers & (peers - 1) == 0 and peers > 1
    across, along = range(1, size), range(2, peers, 2)
    single = [hop for hop in across if hop & (hop - 1) == 0]
    several = [hop for hop in across if hop & (hop - 1)]
    columns = piece_columns(feats, width, size)
    lay = Layout(lanes, filters, feats, width, embed, size, peers)

    *early, spec, mixed, normed, in_w, out_w, slope, units, unit32, norms, rscale = encode(
        patches, w_mix, w_in, w_out, size
    )
    other = swap(units, "dp", 1)
    pair = pair_up(units, other)
    got = stack(lax.optimization_barrier(cross(pair)))
    factors = {hop: swap(early[hop], "blk", hop) for hop in single}
    swapped = swap(got, "dp", 1)
    local, stats, loss, group, around = scores(
        partner_dev, partner_row, units, pair, got, swapped, size, peers
    )
    other = swap(stats, "dp", 1)
    pair = pair_up(stats, other)
    got = stack(lax.optimization_barrier(cross(pair)))
    factors.update({hop: swap(early[hop], "blk", hop) for hop in several})
    factors = [early[0]] + [factors[hop] for hop in across]
    swapped = swap(got, "dp", 1)
    grad_raw = upper(group, around, stats, pair, got, swapped, local, unit32, norms, size, peers)
    raws = spread(grad_raw, "blk", across)
    g_mix = lower(grad_raw, rscale, in_w, out_w, slope, normed, mixed, spec, freqs)
    keep, away = weight_grads(lay, columns, factors, raws, out_w, g_mix)
    got = swap(away, "dp", 1)
    own, *sends = pair_sum(keep, got)
    got = [swap(block, "dp", hop) for block, hop in zip(sends, along)]
    share = total_sum(own, got)
    shares = spread(share, "dp", along)
    middle = len(shares) // 2
    planes = {(0, 0): stack(shares[:middle]), (0, 1): stack(shares[middle:])}
    for half in range(2):
        for hop in single:
            planes[hop, half] = swap(planes[0, half], "blk", hop)
        for hop in several:
            bit = hop & -hop if half else 1 << (hop.bit_length() - 1)
            planes[hop, half] = swap(planes[hop ^ bit, half], "blk", bit)
    parts, done = {}, []
    groups = [group for group in ([0], single, several) if group]
    for order, group in enumerate(groups):
        fresh = {}
        for hop in group:
            for half in range(2):
                fresh[hop, 0, half] = planes[hop, half]
                fresh[hop, 1, half] = swap(planes[hop, half], "dp", 1)
        parts.update(fresh)
        last = order == len(groups) - 1
        done = finish(
            lay, parts if last else fresh, done, tuple(fresh) if last else (), lanes, feats, width
        )
    g_in, g_out, g_mix = done
    return (loss.reshape(count), g_mix, g_in, g_out)


def solution(mesh):
    placed = (P(("blk", "dp"), None, None), P(), P(), P(), P(("blk", "dp")), P(("blk", "dp")))
    return jax.shard_map(
        on_device,
        mesh=mesh,
        in_specs=placed,
        out_specs=(P(("blk", "dp")), P(), P(), P()),
        check_vma=False,
    )
```

```python
import functools
import math

import jax
import jax.numpy as jnp
import numpy as np
from jax import lax
from jax.experimental import pallas as pl
from jax.experimental.pallas import tpu as pltpu
from jax.sharding import PartitionSpec as P


SCALE = 10.0
SUB = 8
BF16 = jnp.bfloat16
F32 = jnp.float32
VMEM = pl.BlockSpec(memory_space=pltpu.VMEM)
ANY = pl.BlockSpec(memory_space=pl.ANY)


def shape(dims, dtype):
    return jax.ShapeDtypeStruct(tuple(dims), dtype)


def hbm(value):
    return pltpu.with_memory_space_constraint(value, pltpu.MemorySpace.HBM)


def mm(left, right):
    return jnp.dot(left, right, preferred_element_type=F32)


def mm_nt(left, right):
    return lax.dot_general(left, right, (((1,), (1,)), ((), ())), preferred_element_type=F32)


def mm_tn(left, right):
    return lax.dot_general(left, right, (((0,), (0,)), ((), ())), preferred_element_type=F32)


def params(mib):
    return pltpu.CompilerParams(vmem_limit_bytes=mib << 20)


def cost(flops, nbytes):
    return pl.CostEstimate(flops=int(flops), bytes_accessed=int(nbytes), transcendentals=0)


def angle_basis(length, freqs):
    phase = np.mod(np.outer(np.arange(freqs), np.arange(length)), length).astype(np.float32)
    phase = phase * np.float32(2.0 * math.pi / length)
    table = np.concatenate([np.cos(phase), -np.sin(phase)], axis=0).astype(np.float32)
    basis = np.einsum("ka,pq->kpqa", table, np.eye(SUB, dtype=np.float32))
    return jnp.asarray(basis.reshape(2 * freqs * SUB, SUB * length), BF16)


def encode_kernel(freqs, size, rounds, patch_hbm, basis_hbm, mix_hbm, out_hbm, in_hbm, *rest):
    piece_hbms, rest = rest[:size], rest[size:]
    spec, mixed, normed, in_w, out_w, slope, units_ref, unit32_ref, norm_ref, rscale_ref, *rest = rest
    patches, basis, mix, feat, hidden, *sems = rest
    table_sems, patch_sems, out_sems = sems
    count, length, lanes = patches.shape
    filters = mix.shape[1]
    half = freqs * SUB
    per = count // rounds
    groups = per // SUB

    def table(i, source, target):
        return pltpu.make_async_copy(source, target, table_sems.at[i])

    tables = [
        table(i, *pair)
        for i, pair in enumerate(
            [(basis_hbm, basis), (mix_hbm, mix), (in_hbm, in_w), (out_hbm, out_w)]
        )
    ]

    def fetch(r):
        rows = pl.ds(r * per, per)
        return pltpu.make_async_copy(patch_hbm.at[rows], patches.at[rows], patch_sems.at[r])

    tables[0].start()
    fetch(0).start()
    tables[1].start()
    for r in range(1, rounds):
        fetch(r).start()
    tables[2].start()
    tables[3].start()
    tables[0].wait()
    tables[1].wait()

    def one(r, carry):
        fetch(r).wait()
        for s in range(groups):
            g = r * groups + s
            base = pl.multiple_of(g * SUB, SUB)
            block = patches[pl.ds(base, SUB)].reshape(SUB * length, lanes)
            part = mm(basis[...], block).astype(BF16)
            spec[g] = part
            both = mm(part, mix[...])
            real_part, imag_part = both[:half], both[half:]
            powers = real_part * real_part + imag_part * imag_part
            share = 2.0 / (1.0 + powers)
            mixed[g, :half] = real_part * share
            mixed[g, half:] = imag_part * share
            piece = jnp.log1p(powers)
            for k in range(freqs):
                feat[pl.ds(base, SUB), k * filters : (k + 1) * filters] = piece[
                    k * SUB : (k + 1) * SUB
                ]
        return carry

    lax.fori_loop(0, rounds, one, 0)
    features = feat[...]
    removed = features - jnp.mean(features, axis=1, keepdims=True)
    rscale = lax.rsqrt(jnp.mean(removed * removed, axis=1, keepdims=True) + 1e-05)
    normed[...] = (removed * rscale).astype(BF16)
    rscale_ref[...] = jnp.broadcast_to(rscale, rscale_ref.shape)
    deep, width, wide = piece_columns(normed.shape[1], hidden.shape[1], size)
    me = lax.axis_index("blk")
    outs = []
    for i, piece_hbm in enumerate(piece_hbms):
        columns = pl.ds(pl.multiple_of((me ^ i) * deep, 128), deep)
        outs.append(
            pltpu.make_async_copy(
                normed.at[:, columns], piece_hbm.at[:, :deep], out_sems.at[len(outs)]
            )
        )
    for each in outs:
        each.start()
    tables[2].wait()
    preact = mm(normed[...], in_w[...])
    sigm = jax.nn.sigmoid(preact)
    hidden[...] = (preact * sigm).astype(BF16)
    slope[...] = (sigm * (1.0 + preact * (1.0 - sigm))).astype(BF16)
    late = []
    for i, piece_hbm in enumerate(piece_hbms):
        if wide == hidden.shape[1]:
            columns = pl.ds(0, wide)
        else:
            columns = pl.ds(pl.multiple_of((me ^ i) * wide, 128), wide)
        for source, target in (
            (slope, piece_hbm.at[:, deep : deep + width]),
            (hidden.at[:, columns], piece_hbm.at[:, deep + width :]),
        ):
            late.append(
                pltpu.make_async_copy(source, target, out_sems.at[len(outs) + len(late)])
            )
    for each in late:
        each.start()
    tables[3].wait()
    raw = mm(hidden[...], out_w[...])
    norms = jnp.sqrt(jnp.sum(raw * raw, axis=1, keepdims=True) + 1e-06)
    norm_ref[...] = jnp.broadcast_to(norms, norm_ref.shape)
    unit32 = raw / norms
    unit32_ref[...] = unit32
    units_ref[...] = unit32.astype(BF16)
    for each in outs + late:
        each.wait()


def piece_columns(feats, width, size):
    wide = width // size
    return feats // size, width, wide if wide % 128 == 0 else width


def encode(patches, w_mix, w_in, w_out, size):
    count, length, lanes = patches.shape
    filters = w_mix.shape[1]
    feats, width = w_in.shape
    embed = w_out.shape[1]
    freqs = feats // filters
    rounds = 4
    assert count % (rounds * SUB) == 0
    groups = count // SUB
    rows = 2 * freqs * SUB
    piece = (count, sum(piece_columns(feats, width, size)))
    kept = [pltpu.MemorySpace.HBM(piece, BF16)] * size
    near = [
        shape((groups, rows, lanes), BF16),
        shape((groups, rows, filters), F32),
        shape((count, feats), BF16),
        shape(w_in.shape, BF16),
        shape(w_out.shape, BF16),
        shape((count, width), BF16),
        shape((count, embed), BF16),
        shape((count, embed), F32),
        shape((count, 128), F32),
        shape((count, 128), F32),
    ]
    return pl.pallas_call(
        functools.partial(encode_kernel, freqs, size, rounds),
        in_specs=[ANY] * 5,
        out_shape=kept + near,
        out_specs=[ANY] * len(kept) + [VMEM] * len(near),
        scratch_shapes=[
            pltpu.VMEM(patches.shape, BF16),
            pltpu.VMEM((rows, SUB * length), BF16),
            pltpu.VMEM(w_mix.shape, BF16),
            pltpu.VMEM((count, feats), F32),
            pltpu.VMEM((count, width), BF16),
            pltpu.SemaphoreType.DMA((4,)),
            pltpu.SemaphoreType.DMA((rounds,)),
            pltpu.SemaphoreType.DMA((3 * size,)),
        ],
        compiler_params=params(24),
        cost_estimate=cost(3e9, 14e6),
    )(*map(hbm, (patches, angle_basis(length, freqs), w_mix, w_out, w_in)))


def exponentials(units, keys, own):
    expo = jnp.exp(SCALE * mm_nt(units, keys))
    if own:
        row = lax.broadcasted_iota(jnp.int32, expo.shape, 0)
        col = lax.broadcasted_iota(jnp.int32, expo.shape, 1)
        expo = jnp.where(row == col, 0.0, expo)
    return expo


def pair_up_kernel(own_ref, other_ref, out_ref):
    rows = own_ref.shape[0]
    own, other = own_ref[...], other_ref[...]
    first = lax.axis_index("dp") % 2 == 0
    out_ref[:rows, :] = jnp.where(first, own, other)
    out_ref[rows:, :] = jnp.where(first, other, own)


def pair_up(own, other):
    rows, width = own.shape
    return pl.pallas_call(
        pair_up_kernel,
        in_specs=[VMEM] * 2,
        out_shape=shape((2 * rows, width), own.dtype),
        out_specs=VMEM,
        compiler_params=params(8),
        cost_estimate=cost(1e3, 1e5),
    )(own, other)


def cross(pair):
    size, peers = lax.axis_size("blk"), lax.axis_size("dp")
    got = []
    for k in range(1, max(size, peers // 2)):
        routes = []
        for blk in range(size):
            for dp in range(peers):
                if dp % 2 == 0 and 2 * k < peers:
                    routes.append((blk * peers + dp, blk * peers + (dp ^ (2 * k))))
                if dp % 2 == 1 and k < size:
                    routes.append((blk * peers + dp, (blk ^ k) * peers + dp))
        got.append(lax.ppermute(pair, ("blk", "dp"), routes))
    return got


def crossed(got_ref, swapped_ref, rows):
    first = lax.axis_index("dp") % 2 == 0

    def along(k, core):
        at = (2 * (k - 1) + core) * rows
        return jnp.where(first, got_ref[at : at + rows, :], swapped_ref[at : at + rows, :])

    def across(k):
        at = 2 * (k - 1) * rows
        low = jnp.where(first, swapped_ref[at : at + rows, :], got_ref[at + rows : at + 2 * rows, :])
        return low

    return along, across


def as_rows(column, count):
    return jnp.broadcast_to(column, (column.shape[0], count)).T


def scores_kernel(
    size,
    peers,
    dev_ref,
    row_ref,
    units_ref,
    pair_ref,
    got_ref,
    swapped_ref,
    local_ref,
    stats_ref,
    loss_ref,
    group_ref,
    around_ref,
):
    units = units_ref[...]
    count = units.shape[0]
    along, across = crossed(got_ref, swapped_ref, count)
    zneg = numer = None
    for i in range(size):
        keys = across(i) if i else units
        group_ref[i * count : (i + 1) * count, :] = keys
        expo = exponentials(units, keys, i == 0)
        total = jnp.sum(expo, axis=1, keepdims=True)
        term = mm(expo.astype(BF16), keys)
        zneg = total if zneg is None else zneg + total
        numer = term if numer is None else numer + term
    me = lax.axis_index("dp")
    dev = dev_ref[...]
    place = (2 * ((dev ^ me) >> 1) + (dev & 1)) * count + row_ref[...]
    place = jnp.broadcast_to(place.astype(F32), (count, count)).T
    lane = lax.broadcasted_iota(jnp.int32, (count, count), 1).astype(F32)
    positive = None
    for i in range(peers):
        k, core = i // 2, i % 2
        source = along(k, core) if k else pair_ref[core * count : (core + 1) * count, :]
        around_ref[i * count : (i + 1) * count, :] = source
        hit = jnp.where(place - float(i * count) == lane, 1.0, 0.0).astype(BF16)
        term = mm(hit, source)
        positive = term if positive is None else positive + term
    spos = SCALE * jnp.sum(units.astype(F32) * positive, axis=1, keepdims=True)
    top = jnp.exp(spos)
    totals = top + zneg
    less = top / totals - 1.0
    coef = SCALE / count
    local_ref[...] = coef * (less * positive + numer / totals)
    loss_ref[...] = as_rows(jnp.log(totals) - spos, count)[:1]
    stats_ref[...] = jnp.zeros(stats_ref.shape, F32)
    stats_ref[0:1, :] = as_rows(totals, count)[:1]
    stats_ref[1:2, :] = as_rows(coef * less, count)[:1]
    stats_ref[2:3, :] = (dev * count + row_ref[...]).astype(F32)


def scores(partner_dev, partner_row, units, pair, got, swapped, size, peers):
    count, embed = units.shape
    return pl.pallas_call(
        functools.partial(scores_kernel, size, peers),
        in_specs=[VMEM] * 6,
        out_shape=[
            shape((count, embed), F32),
            shape((SUB, count), F32),
            shape((1, count), F32),
            shape((size * count, embed), BF16),
            shape((peers * count, embed), BF16),
        ],
        out_specs=[VMEM] * 5,
        compiler_params=params(16),
        cost_estimate=cost(4e8, 1e6),
    )(partner_dev.reshape(1, count), partner_row.reshape(1, count), units, pair, got, swapped)


def upper_kernel(
    size,
    peers,
    group_ref,
    around_ref,
    stats_ref,
    pair_ref,
    got_ref,
    swapped_ref,
    local_ref,
    unit32_ref,
    norm_ref,
    out_ref,
):
    count, _ = local_ref.shape
    coef = SCALE / count
    along, across = crossed(got_ref, swapped_ref, SUB)
    units = group_ref[:count, :]
    keyterm = None
    for i in range(size):
        keys = group_ref[i * count : (i + 1) * count, :]
        expo = exponentials(units, keys, i == 0)
        totals = (across(i) if i else stats_ref[...])[0:1, :]
        term = mm((expo / totals).astype(BF16), keys)
        keyterm = term if keyterm is None else keyterm + term
    mine = lax.axis_index("dp") * count + lax.broadcasted_iota(jnp.int32, (count, count), 0)
    mine = mine.astype(F32)
    chosen = amount = None
    for i in range(peers):
        k, core = i // 2, i % 2
        table = along(k, core) if k else pair_ref[core * SUB : (core + 1) * SUB, :]
        hit = table[2:3, :] == mine
        share = jnp.where(hit, table[1:2, :], 0.0)
        term = mm(jnp.where(hit, 1.0, 0.0).astype(BF16), around_ref[i * count : (i + 1) * count, :])
        chosen = term if chosen is None else chosen + term
        amount = share if amount is None else amount + share
    back = jnp.sum(amount, axis=1, keepdims=True) * chosen
    grad_units = local_ref[...] + coef * keyterm + back
    unit32 = unit32_ref[...]
    tilt = jnp.sum(unit32 * grad_units, axis=1, keepdims=True)
    out_ref[...] = ((grad_units - unit32 * tilt) / norm_ref[:, :1]).astype(BF16)


def upper(group, around, stats, pair, got, swapped, local, unit32, norms, size, peers):
    count, embed = local.shape
    args = [group, around, stats, pair, got, swapped, local, unit32, norms]
    return pl.pallas_call(
        functools.partial(upper_kernel, size, peers),
        in_specs=[VMEM] * len(args),
        out_shape=shape((count, embed), BF16),
        out_specs=VMEM,
        compiler_params=params(16),
        cost_estimate=cost(4e8, 2e6),
    )(*args)


def pre_grads(grad_raw, out_w, slope):
    return (mm_nt(grad_raw, out_w) * slope.astype(F32)).astype(BF16)


def lower_kernel(
    freqs, raw_ref, rscale_ref, in_w, out_w, slope, normed, mixed, spec, g_mix_ref, grad_feat
):
    grad_pre = pre_grads(raw_ref[...], out_w[...], slope[...])
    grad_norm = mm_nt(grad_pre, in_w[...])
    xhat = normed[...].astype(F32)
    mean = jnp.mean(grad_norm, axis=1, keepdims=True)
    tilt = jnp.mean(grad_norm * xhat, axis=1, keepdims=True)
    grad_feat[...] = rscale_ref[:, :1] * (grad_norm - mean - xhat * tilt)
    groups, _, filters = mixed.shape
    half = freqs * SUB

    def one(g, total):
        base = pl.multiple_of(g * SUB, SUB)
        grads = jnp.concatenate(
            [grad_feat[pl.ds(base, SUB), k * filters : (k + 1) * filters] for k in range(freqs)],
            axis=0,
        )
        grad_mixed = jnp.concatenate(
            [mixed[g, :half] * grads, mixed[g, half:] * grads], axis=0
        ).astype(BF16)
        return total + mm_tn(grad_mixed, spec[g])

    total = lax.fori_loop(0, groups, one, jnp.zeros((filters, spec.shape[2]), F32), unroll=16)
    g_mix_ref[...] = total.T


def lower(grad_raw, rscale, in_w, out_w, slope, normed, mixed, spec, freqs):
    filters, lanes = mixed.shape[2], spec.shape[2]
    return pl.pallas_call(
        functools.partial(lower_kernel, freqs),
        in_specs=[VMEM] * 8,
        out_shape=shape((lanes, filters), F32),
        out_specs=VMEM,
        scratch_shapes=[pltpu.VMEM(normed.shape, F32)],
        compiler_params=params(20),
        cost_estimate=cost(1e9, 7e6),
    )(grad_raw, rscale, in_w, out_w, slope, normed, mixed, spec)


def up_to(rows, unit):
    return -(-rows // unit) * unit


class Layout:
    def __init__(self, lanes, filters, feats, width, embed, size, peers):
        self.size, self.peers = size, peers
        self.in_rows = feats // size // peers
        self.out_rows = width // size // peers
        self.mix_rows = lanes // peers
        self.top = up_to(self.in_rows, 16)
        self.strip = max(16, up_to(self.out_rows, 16))
        self.mix_blocks = -(-self.mix_rows // self.strip)
        self.rows = self.top + self.strip
        self.width = width
        assert embed == 128 and filters == 128 and (1 + self.mix_blocks) * 128 <= width

    def mix_parts(self):
        for block in range(self.mix_blocks):
            start = block * self.strip
            yield start, min(self.strip, self.mix_rows - start), slice(128 * (block + 1), 128 * (block + 2))


def weights_kernel(lay, columns, *refs):
    size, peers = lay.size, lay.peers
    pieces, raws, rest = refs[:size], refs[size : 2 * size], refs[2 * size :]
    out_w_ref, mix_ref, keep_ref, away_ref, g_in, g_out = rest
    deep, width, wide = columns
    share = width // size
    for i in range(size):
        raw = raws[i][...]
        grad_pre = pre_grads(raw, out_w_ref[...], pieces[i][:, deep : deep + width])
        term_in = mm_tn(pieces[i][:, :deep], grad_pre)
        term_out = mm_tn(pieces[i][:, deep + width :], raw)
        if i == 0:
            g_in[...] = term_in
            g_out[...] = term_out
        else:
            g_in[...] += term_in
            g_out[...] += term_out
    me = lax.axis_index("dp")
    first = 0 if wide == share else lax.axis_index("blk") * share
    keep_ref[:, lay.top :, :] = jnp.zeros((peers // 2, lay.strip, width), F32)
    away_ref[:, lay.top :, :] = jnp.zeros((peers // 2, lay.strip, width), BF16)
    if lay.top > lay.in_rows:
        keep_ref[:, : lay.top, :] = jnp.zeros((peers // 2, lay.top, width), F32)
        away_ref[:, : lay.top, :] = jnp.zeros((peers // 2, lay.top, width), BF16)
    for slot in range(peers):
        owner = me ^ slot
        target = away_ref if slot & 1 else keep_ref
        at = slot >> 1
        target[at, : lay.in_rows, :] = g_in[pl.ds(owner * lay.in_rows, lay.in_rows), :].astype(target.dtype)
        target[at, lay.top : lay.top + lay.out_rows, :128] = g_out[
            pl.ds(first + owner * lay.out_rows, lay.out_rows), :
        ].astype(target.dtype)
        for start, rows, cols in lay.mix_parts():
            target[at, lay.top : lay.top + rows, cols] = mix_ref[
                pl.ds(owner * lay.mix_rows + start, rows), :
            ].astype(target.dtype)


def weight_grads(lay, columns, pieces, raws, w_out, g_mix):
    deep, width, wide = columns
    block = (lay.peers // 2, lay.rows, lay.width)
    args = [*pieces, *raws, w_out, g_mix]
    return pl.pallas_call(
        functools.partial(weights_kernel, lay, columns),
        in_specs=[VMEM] * len(args),
        out_shape=[shape(block, F32), shape(block, BF16)],
        out_specs=[VMEM] * 2,
        scratch_shapes=[pltpu.VMEM((deep, width), F32), pltpu.VMEM((wide, 128), F32)],
        compiler_params=params(16),
        cost_estimate=cost(6e8, 4e6),
    )(*args)


HALVES = 2


def pair_kernel(keep_ref, got_ref, *out_refs):
    slots, _, width = keep_ref.shape
    part = width // HALVES
    for half in range(HALVES):
        cols = slice(half * part, (half + 1) * part)
        for i in range(slots):
            out_ref = out_refs[half * slots + i]
            total = keep_ref[i, :, cols] + got_ref[i, :, cols].astype(F32)
            out_ref[...] = total.astype(out_ref.dtype)


def pair_sum(keep, got):
    slots, rows, width = keep.shape
    part = (rows, width // HALVES)
    outs = [shape(part, F32)] + [shape(part, BF16)] * (slots - 1)
    sums = pl.pallas_call(
        pair_kernel,
        in_specs=[VMEM] * 2,
        out_shape=outs * HALVES,
        out_specs=[VMEM] * (slots * HALVES),
        compiler_params=params(8),
        cost_estimate=cost(1e6, 2e6),
    )(keep, got)
    return [sums[half * slots : (half + 1) * slots] for half in range(HALVES)]


def total_kernel(own_ref, *refs):
    total = own_ref[...]
    for each in refs[:-1]:
        total = total + each[...].astype(F32)
    refs[-1][...] = total.astype(BF16)


def total_sum(own, got):
    return pl.pallas_call(
        total_kernel,
        in_specs=[VMEM] * (1 + len(got)),
        out_shape=shape(own.shape, BF16),
        out_specs=VMEM,
        compiler_params=params(8),
        cost_estimate=cost(1e6, 1e6),
    )(own, *got)


def finish_kernel(lay, parts, done, fresh, closing, *refs):
    slots = lay.peers // 2
    part_cols = lay.width // HALVES
    part_refs, refs = dict(zip(parts, refs)), refs[len(parts) :]
    if done:
        refs = refs[2:]
    g_in_hbm, g_out_hbm, *refs = refs
    if closing:
        g_mix_ref, *refs = refs
    stage, strip_stage, sems, strip_sems = refs
    me_blk, me_dp = lax.axis_index("blk"), lax.axis_index("dp")
    copies = []

    def send(kept, slot, target, sem):
        copy = pltpu.make_async_copy(kept.at[slot], target, sem.at[slot])
        copy.start()
        copies.append(copy)

    for n, (hop, core, half) in enumerate(fresh):
        source = part_refs[hop, core, half]
        cols = slice(half * part_cols, (half + 1) * part_cols)
        for z in range(slots):
            slot = n * slots + z
            at = z * lay.rows
            owner = (me_blk ^ hop) * lay.peers + (me_dp ^ (2 * z + core))
            stage[slot] = source[at : at + lay.in_rows, :].astype(F32)
            send(stage, slot, g_in_hbm.at[pl.ds(owner * lay.in_rows, lay.in_rows), cols], sems)
            if half == 0:
                strip = at + lay.top
                strip_stage[slot] = source[strip : strip + lay.out_rows, :128].astype(F32)
                send(
                    strip_stage,
                    slot,
                    g_out_hbm.at[pl.ds(owner * lay.out_rows, lay.out_rows), :],
                    strip_sems,
                )
    if closing:
        for core in range(2):
            for z in range(slots):
                strip = z * lay.rows + lay.top
                owner = me_dp ^ (2 * z + core)
                for start, rows, cols in lay.mix_parts():
                    half, first = divmod(cols.start, part_cols)
                    terms = [
                        part_refs[hop, core, half][strip : strip + rows, first : first + 128].astype(F32)
                        for hop in range(lay.size)
                    ]
                    while len(terms) > 1:
                        terms = [terms[t] + terms[t + 1] for t in range(0, len(terms), 2)]
                    g_mix_ref[pl.ds(owner * lay.mix_rows + start, rows), :] = terms[0]
    for copy in copies:
        copy.wait()


def finish(lay, parts, done, fresh, closing, lanes, feats, width):
    slots = len(fresh) * lay.peers // 2
    outs = [shape((feats, width), F32), shape((width, 128), F32)]
    specs = [ANY, ANY]
    if closing:
        outs.append(shape((lanes, 128), F32))
        specs.append(VMEM)
    return pl.pallas_call(
        functools.partial(finish_kernel, lay, tuple(parts), bool(done), tuple(fresh), closing),
        in_specs=[VMEM] * len(parts) + [ANY] * len(done),
        out_shape=outs,
        out_specs=specs,
        scratch_shapes=[
            pltpu.VMEM((slots, lay.in_rows, lay.width // HALVES), F32),
            pltpu.VMEM((slots, lay.out_rows, 128), F32),
            pltpu.SemaphoreType.DMA((slots,)),
            pltpu.SemaphoreType.DMA((slots,)),
        ],
        input_output_aliases={len(parts) + i: i for i in range(len(done))},
        compiler_params=params(24),
        cost_estimate=cost(1e6, 8e6),
    )(*parts.values(), *done)


def stack_kernel(*refs):
    rows = refs[0].shape[0]
    for i, each in enumerate(refs[:-1]):
        refs[-1][i * rows : (i + 1) * rows, :] = each[...]


def stack(blocks):
    rows, width = blocks[0].shape
    return pl.pallas_call(
        stack_kernel,
        in_specs=[VMEM] * len(blocks),
        out_shape=shape((len(blocks) * rows, width), blocks[0].dtype),
        out_specs=VMEM,
        compiler_params=params(8),
        cost_estimate=cost(1e3, 1e5),
    )(*blocks)


def swap(block, axis, bit):
    size = lax.axis_size(axis)
    return lax.ppermute(block, axis, [(src, src ^ bit) for src in range(size)])


def spread(block, axis, hops):
    return [block] + [swap(block, axis, hop) for hop in hops]


def on_device(patches, w_mix, w_in, w_out, partner_dev, partner_row):
    count, _, lanes = patches.shape
    filters = w_mix.shape[1]
    feats, width = w_in.shape
    embed = w_out.shape[1]
    freqs = feats // filters
    size, peers = lax.axis_size("blk"), lax.axis_size("dp")
    assert size & (size - 1) == 0 and peers & (peers - 1) == 0 and peers > 1
    across, along = range(1, size), range(2, peers, 2)
    single = [hop for hop in across if hop & (hop - 1) == 0]
    several = [hop for hop in across if hop & (hop - 1)]
    columns = piece_columns(feats, width, size)
    lay = Layout(lanes, filters, feats, width, embed, size, peers)

    *early, spec, mixed, normed, in_w, out_w, slope, units, unit32, norms, rscale = encode(
        patches, w_mix, w_in, w_out, size
    )
    other = swap(units, "dp", 1)
    pair = pair_up(units, other)
    got = stack(lax.optimization_barrier(cross(pair)))
    factors = {hop: swap(early[hop], "blk", hop) for hop in single}
    swapped = swap(got, "dp", 1)
    local, stats, loss, group, around = scores(
        partner_dev, partner_row, units, pair, got, swapped, size, peers
    )
    other = swap(stats, "dp", 1)
    pair = pair_up(stats, other)
    got = stack(lax.optimization_barrier(cross(pair)))
    factors.update({hop: swap(early[hop], "blk", hop) for hop in several})
    factors = [early[0]] + [factors[hop] for hop in across]
    swapped = swap(got, "dp", 1)
    grad_raw = upper(group, around, stats, pair, got, swapped, local, unit32, norms, size, peers)
    raws = spread(grad_raw, "blk", across)
    g_mix = lower(grad_raw, rscale, in_w, out_w, slope, normed, mixed, spec, freqs)
    keep, away = weight_grads(lay, columns, factors, raws, out_w, g_mix)
    got = swap(away, "dp", 1)
    planes = {}
    for half, (own, *sends) in enumerate(pair_sum(keep, got)):
        got = [swap(block, "dp", hop) for block, hop in zip(sends, along)]
        share = total_sum(own, got)
        shares = spread(share, "dp", along)
        planes[0, half] = stack(shares)
        for hop in single:
            planes[hop, half] = swap(planes[0, half], "blk", hop)
        for hop in several:
            bit = hop & -hop if half else 1 << (hop.bit_length() - 1)
            planes[hop, half] = swap(planes[hop ^ bit, half], "blk", bit)
    parts, done = {}, []
    stages = [[(0, 0), (0, 1)], [(hop, 0) for hop in single], [(hop, 1) for hop in single]]
    stages += [[(hop, half) for hop in several] for half in range(HALVES)]
    stages = [stage for stage in stages if stage]
    for order, stage in enumerate(stages):
        fresh = {}
        for hop, half in stage:
            fresh[hop, 0, half] = planes[hop, half]
            fresh[hop, 1, half] = swap(planes[hop, half], "dp", 1)
        parts.update(fresh)
        last = order == len(stages) - 1
        done = finish(
            lay, parts if last else fresh, done, fresh, last, lanes, feats, width
        )
    g_in, g_out, g_mix = done
    return (loss.reshape(count), g_mix, g_in, g_out)


def solution(mesh):
    placed = (P(("blk", "dp"), None, None), P(), P(), P(), P(("blk", "dp")), P(("blk", "dp")))
    return jax.shard_map(
        on_device,
        mesh=mesh,
        in_specs=placed,
        out_specs=(P(("blk", "dp")), P(), P(), P()),
        check_vma=False,
    )
```

```python
import functools
import math

import jax
import jax.numpy as jnp
import numpy as np
from jax import lax
from jax.experimental import pallas as pl
from jax.experimental.pallas import tpu as pltpu
from jax.sharding import PartitionSpec as P


SCALE = 10.0
SUB = 8
BF16 = jnp.bfloat16
F32 = jnp.float32
VMEM = pl.BlockSpec(memory_space=pltpu.VMEM)
ANY = pl.BlockSpec(memory_space=pl.ANY)


def shape(dims, dtype):
    return jax.ShapeDtypeStruct(tuple(dims), dtype)


def hbm(value):
    return pltpu.with_memory_space_constraint(value, pltpu.MemorySpace.HBM)


def mm(left, right):
    return jnp.dot(left, right, preferred_element_type=F32)


def mm_nt(left, right):
    return lax.dot_general(left, right, (((1,), (1,)), ((), ())), preferred_element_type=F32)


def mm_tn(left, right):
    return lax.dot_general(left, right, (((0,), (0,)), ((), ())), preferred_element_type=F32)


def params(mib):
    return pltpu.CompilerParams(vmem_limit_bytes=mib << 20)


def cost(flops, nbytes):
    return pl.CostEstimate(flops=int(flops), bytes_accessed=int(nbytes), transcendentals=0)


def angle_basis(length, freqs):
    phase = np.mod(np.outer(np.arange(freqs), np.arange(length)), length).astype(np.float32)
    phase = phase * np.float32(2.0 * math.pi / length)
    table = np.concatenate([np.cos(phase), -np.sin(phase)], axis=0).astype(np.float32)
    basis = np.einsum("ka,pq->kpqa", table, np.eye(SUB, dtype=np.float32))
    return jnp.asarray(basis.reshape(2 * freqs * SUB, SUB * length), BF16)


def encode_kernel(freqs, size, rounds, patch_hbm, basis_hbm, mix_hbm, out_hbm, in_hbm, *rest):
    piece_hbms, rest = rest[:size], rest[size:]
    spec, mixed, normed, in_w, out_w, slope, units_ref, unit32_ref, norm_ref, rscale_ref, *rest = rest
    patches, basis, mix, feat, hidden, *sems = rest
    table_sems, patch_sems, out_sems = sems
    count, length, lanes = patches.shape
    filters = mix.shape[1]
    half = freqs * SUB
    per = count // rounds
    groups = per // SUB

    def table(i, source, target):
        return pltpu.make_async_copy(source, target, table_sems.at[i])

    tables = [
        table(i, *pair)
        for i, pair in enumerate(
            [(basis_hbm, basis), (mix_hbm, mix), (in_hbm, in_w), (out_hbm, out_w)]
        )
    ]

    def fetch(r):
        rows = pl.ds(r * per, per)
        return pltpu.make_async_copy(patch_hbm.at[rows], patches.at[rows], patch_sems.at[r])

    tables[0].start()
    fetch(0).start()
    tables[1].start()
    for r in range(1, rounds):
        fetch(r).start()
    tables[2].start()
    tables[3].start()
    tables[0].wait()
    tables[1].wait()

    def one(r, carry):
        fetch(r).wait()
        for s in range(groups):
            g = r * groups + s
            base = pl.multiple_of(g * SUB, SUB)
            block = patches[pl.ds(base, SUB)].reshape(SUB * length, lanes)
            part = mm(basis[...], block).astype(BF16)
            spec[g] = part
            both = mm(part, mix[...])
            real_part, imag_part = both[:half], both[half:]
            powers = real_part * real_part + imag_part * imag_part
            share = 2.0 / (1.0 + powers)
            mixed[g, :half] = real_part * share
            mixed[g, half:] = imag_part * share
            piece = jnp.log1p(powers)
            for k in range(freqs):
                feat[pl.ds(base, SUB), k * filters : (k + 1) * filters] = piece[
                    k * SUB : (k + 1) * SUB
                ]
        return carry

    lax.fori_loop(0, rounds, one, 0)
    features = feat[...]
    removed = features - jnp.mean(features, axis=1, keepdims=True)
    rscale = lax.rsqrt(jnp.mean(removed * removed, axis=1, keepdims=True) + 1e-05)
    normed[...] = (removed * rscale).astype(BF16)
    rscale_ref[...] = jnp.broadcast_to(rscale, rscale_ref.shape)
    deep, width, wide = piece_columns(normed.shape[1], hidden.shape[1], size)
    me = lax.axis_index("blk")
    outs = []
    for i, piece_hbm in enumerate(piece_hbms):
        columns = pl.ds(pl.multiple_of((me ^ i) * deep, 128), deep)
        outs.append(
            pltpu.make_async_copy(
                normed.at[:, columns], piece_hbm.at[:, :deep], out_sems.at[len(outs)]
            )
        )
    for each in outs:
        each.start()
    tables[2].wait()
    preact = mm(normed[...], in_w[...])
    sigm = jax.nn.sigmoid(preact)
    hidden[...] = (preact * sigm).astype(BF16)
    slope[...] = (sigm * (1.0 + preact * (1.0 - sigm))).astype(BF16)
    late = []
    for i, piece_hbm in enumerate(piece_hbms):
        if wide == hidden.shape[1]:
            columns = pl.ds(0, wide)
        else:
            columns = pl.ds(pl.multiple_of((me ^ i) * wide, 128), wide)
        for source, target in (
            (slope, piece_hbm.at[:, deep : deep + width]),
            (hidden.at[:, columns], piece_hbm.at[:, deep + width :]),
        ):
            late.append(
                pltpu.make_async_copy(source, target, out_sems.at[len(outs) + len(late)])
            )
    for each in late:
        each.start()
    tables[3].wait()
    raw = mm(hidden[...], out_w[...])
    norms = jnp.sqrt(jnp.sum(raw * raw, axis=1, keepdims=True) + 1e-06)
    norm_ref[...] = jnp.broadcast_to(norms, norm_ref.shape)
    unit32 = raw / norms
    unit32_ref[...] = unit32
    units_ref[...] = unit32.astype(BF16)
    for each in outs + late:
        each.wait()


def piece_columns(feats, width, size):
    wide = width // size
    return feats // size, width, wide if wide % 128 == 0 else width


def encode(patches, w_mix, w_in, w_out, size):
    count, length, lanes = patches.shape
    filters = w_mix.shape[1]
    feats, width = w_in.shape
    embed = w_out.shape[1]
    freqs = feats // filters
    rounds = 4
    assert count % (rounds * SUB) == 0
    groups = count // SUB
    rows = 2 * freqs * SUB
    piece = (count, sum(piece_columns(feats, width, size)))
    kept = [pltpu.MemorySpace.HBM(piece, BF16)] * size
    near = [
        shape((groups, rows, lanes), BF16),
        shape((groups, rows, filters), F32),
        shape((count, feats), BF16),
        shape(w_in.shape, BF16),
        shape(w_out.shape, BF16),
        shape((count, width), BF16),
        shape((count, embed), BF16),
        shape((count, embed), F32),
        shape((count, 128), F32),
        shape((count, 128), F32),
    ]
    return pl.pallas_call(
        functools.partial(encode_kernel, freqs, size, rounds),
        in_specs=[ANY] * 5,
        out_shape=kept + near,
        out_specs=[ANY] * len(kept) + [VMEM] * len(near),
        scratch_shapes=[
            pltpu.VMEM(patches.shape, BF16),
            pltpu.VMEM((rows, SUB * length), BF16),
            pltpu.VMEM(w_mix.shape, BF16),
            pltpu.VMEM((count, feats), F32),
            pltpu.VMEM((count, width), BF16),
            pltpu.SemaphoreType.DMA((4,)),
            pltpu.SemaphoreType.DMA((rounds,)),
            pltpu.SemaphoreType.DMA((3 * size,)),
        ],
        compiler_params=params(24),
        cost_estimate=cost(3e9, 14e6),
    )(*map(hbm, (patches, angle_basis(length, freqs), w_mix, w_out, w_in)))


def exponentials(units, keys, own):
    expo = jnp.exp(SCALE * mm_nt(units, keys))
    if own:
        row = lax.broadcasted_iota(jnp.int32, expo.shape, 0)
        col = lax.broadcasted_iota(jnp.int32, expo.shape, 1)
        expo = jnp.where(row == col, 0.0, expo)
    return expo


def pair_up_kernel(own_ref, other_ref, out_ref):
    rows = own_ref.shape[0]
    own, other = own_ref[...], other_ref[...]
    first = lax.axis_index("dp") % 2 == 0
    out_ref[:rows, :] = jnp.where(first, own, other)
    out_ref[rows:, :] = jnp.where(first, other, own)


def pair_up(own, other):
    rows, width = own.shape
    return pl.pallas_call(
        pair_up_kernel,
        in_specs=[VMEM] * 2,
        out_shape=shape((2 * rows, width), own.dtype),
        out_specs=VMEM,
        compiler_params=params(8),
        cost_estimate=cost(1e3, 1e5),
    )(own, other)


def cross(pair):
    size, peers = lax.axis_size("blk"), lax.axis_size("dp")
    got = []
    for k in range(1, max(size, peers // 2)):
        routes = []
        for blk in range(size):
            for dp in range(peers):
                if dp % 2 == 0 and 2 * k < peers:
                    routes.append((blk * peers + dp, blk * peers + (dp ^ (2 * k))))
                if dp % 2 == 1 and k < size:
                    routes.append((blk * peers + dp, (blk ^ k) * peers + dp))
        got.append(lax.ppermute(pair, ("blk", "dp"), routes))
    return got


def crossed(got_ref, swapped_ref, rows):
    first = lax.axis_index("dp") % 2 == 0

    def along(k, core):
        at = (2 * (k - 1) + core) * rows
        return jnp.where(first, got_ref[at : at + rows, :], swapped_ref[at : at + rows, :])

    def across(k):
        at = 2 * (k - 1) * rows
        low = jnp.where(first, swapped_ref[at : at + rows, :], got_ref[at + rows : at + 2 * rows, :])
        return low

    return along, across


def as_rows(column, count):
    return jnp.broadcast_to(column, (column.shape[0], count)).T


def scores_kernel(
    size,
    peers,
    dev_ref,
    row_ref,
    units_ref,
    pair_ref,
    got_ref,
    swapped_ref,
    local_ref,
    stats_ref,
    loss_ref,
    group_ref,
    around_ref,
):
    units = units_ref[...]
    count = units.shape[0]
    along, across = crossed(got_ref, swapped_ref, count)
    zneg = numer = None
    for i in range(size):
        keys = across(i) if i else units
        group_ref[i * count : (i + 1) * count, :] = keys
        expo = exponentials(units, keys, i == 0)
        total = jnp.sum(expo, axis=1, keepdims=True)
        term = mm(expo.astype(BF16), keys)
        zneg = total if zneg is None else zneg + total
        numer = term if numer is None else numer + term
    me = lax.axis_index("dp")
    dev = dev_ref[...]
    place = (2 * ((dev ^ me) >> 1) + (dev & 1)) * count + row_ref[...]
    place = jnp.broadcast_to(place.astype(F32), (count, count)).T
    lane = lax.broadcasted_iota(jnp.int32, (count, count), 1).astype(F32)
    positive = None
    for i in range(peers):
        k, core = i // 2, i % 2
        source = along(k, core) if k else pair_ref[core * count : (core + 1) * count, :]
        around_ref[i * count : (i + 1) * count, :] = source
        hit = jnp.where(place - float(i * count) == lane, 1.0, 0.0).astype(BF16)
        term = mm(hit, source)
        positive = term if positive is None else positive + term
    spos = SCALE * jnp.sum(units.astype(F32) * positive, axis=1, keepdims=True)
    top = jnp.exp(spos)
    totals = top + zneg
    less = top / totals - 1.0
    coef = SCALE / count
    local_ref[...] = coef * (less * positive + numer / totals)
    loss_ref[...] = as_rows(jnp.log(totals) - spos, count)[:1]
    stats_ref[...] = jnp.zeros(stats_ref.shape, F32)
    stats_ref[0:1, :] = as_rows(totals, count)[:1]
    stats_ref[1:2, :] = as_rows(coef * less, count)[:1]
    stats_ref[2:3, :] = (dev * count + row_ref[...]).astype(F32)


def scores(partner_dev, partner_row, units, pair, got, swapped, size, peers):
    count, embed = units.shape
    return pl.pallas_call(
        functools.partial(scores_kernel, size, peers),
        in_specs=[VMEM] * 6,
        out_shape=[
            shape((count, embed), F32),
            shape((SUB, count), F32),
            shape((1, count), F32),
            shape((size * count, embed), BF16),
            shape((peers * count, embed), BF16),
        ],
        out_specs=[VMEM] * 5,
        compiler_params=params(16),
        cost_estimate=cost(4e8, 1e6),
    )(partner_dev.reshape(1, count), partner_row.reshape(1, count), units, pair, got, swapped)


def upper_kernel(
    size,
    peers,
    group_ref,
    around_ref,
    stats_ref,
    pair_ref,
    got_ref,
    swapped_ref,
    local_ref,
    unit32_ref,
    norm_ref,
    out_ref,
):
    count, _ = local_ref.shape
    coef = SCALE / count
    along, across = crossed(got_ref, swapped_ref, SUB)
    units = group_ref[:count, :]
    keyterm = None
    for i in range(size):
        keys = group_ref[i * count : (i + 1) * count, :]
        expo = exponentials(units, keys, i == 0)
        totals = (across(i) if i else stats_ref[...])[0:1, :]
        term = mm((expo / totals).astype(BF16), keys)
        keyterm = term if keyterm is None else keyterm + term
    mine = lax.axis_index("dp") * count + lax.broadcasted_iota(jnp.int32, (count, count), 0)
    mine = mine.astype(F32)
    chosen = amount = None
    for i in range(peers):
        k, core = i // 2, i % 2
        table = along(k, core) if k else pair_ref[core * SUB : (core + 1) * SUB, :]
        hit = table[2:3, :] == mine
        share = jnp.where(hit, table[1:2, :], 0.0)
        term = mm(jnp.where(hit, 1.0, 0.0).astype(BF16), around_ref[i * count : (i + 1) * count, :])
        chosen = term if chosen is None else chosen + term
        amount = share if amount is None else amount + share
    back = jnp.sum(amount, axis=1, keepdims=True) * chosen
    grad_units = local_ref[...] + coef * keyterm + back
    unit32 = unit32_ref[...]
    tilt = jnp.sum(unit32 * grad_units, axis=1, keepdims=True)
    out_ref[...] = ((grad_units - unit32 * tilt) / norm_ref[:, :1]).astype(BF16)


def upper(group, around, stats, pair, got, swapped, local, unit32, norms, size, peers):
    count, embed = local.shape
    args = [group, around, stats, pair, got, swapped, local, unit32, norms]
    return pl.pallas_call(
        functools.partial(upper_kernel, size, peers),
        in_specs=[VMEM] * len(args),
        out_shape=shape((count, embed), BF16),
        out_specs=VMEM,
        compiler_params=params(16),
        cost_estimate=cost(4e8, 2e6),
    )(*args)


def pre_grads(grad_raw, out_w, slope):
    return (mm_nt(grad_raw, out_w) * slope.astype(F32)).astype(BF16)


def lower_kernel(
    freqs, raw_ref, rscale_ref, in_w, out_w, slope, normed, mixed, spec, g_mix_ref, grad_feat
):
    grad_pre = pre_grads(raw_ref[...], out_w[...], slope[...])
    grad_norm = mm_nt(grad_pre, in_w[...])
    xhat = normed[...].astype(F32)
    mean = jnp.mean(grad_norm, axis=1, keepdims=True)
    tilt = jnp.mean(grad_norm * xhat, axis=1, keepdims=True)
    grad_feat[...] = rscale_ref[:, :1] * (grad_norm - mean - xhat * tilt)
    groups, _, filters = mixed.shape
    half = freqs * SUB

    def one(g, total):
        base = pl.multiple_of(g * SUB, SUB)
        grads = jnp.concatenate(
            [grad_feat[pl.ds(base, SUB), k * filters : (k + 1) * filters] for k in range(freqs)],
            axis=0,
        )
        grad_mixed = jnp.concatenate(
            [mixed[g, :half] * grads, mixed[g, half:] * grads], axis=0
        ).astype(BF16)
        return total + mm_tn(grad_mixed, spec[g])

    total = lax.fori_loop(0, groups, one, jnp.zeros((filters, spec.shape[2]), F32), unroll=16)
    g_mix_ref[...] = total.T


def lower(grad_raw, rscale, in_w, out_w, slope, normed, mixed, spec, freqs):
    filters, lanes = mixed.shape[2], spec.shape[2]
    return pl.pallas_call(
        functools.partial(lower_kernel, freqs),
        in_specs=[VMEM] * 8,
        out_shape=shape((lanes, filters), F32),
        out_specs=VMEM,
        scratch_shapes=[pltpu.VMEM(normed.shape, F32)],
        compiler_params=params(20),
        cost_estimate=cost(1e9, 7e6),
    )(grad_raw, rscale, in_w, out_w, slope, normed, mixed, spec)


def up_to(rows, unit):
    return -(-rows // unit) * unit


class Layout:
    def __init__(self, lanes, filters, feats, width, embed, size, peers):
        self.size, self.peers = size, peers
        self.in_rows = feats // size // peers
        self.out_rows = width // size // peers
        self.mix_rows = lanes // peers
        self.top = up_to(self.in_rows, 16)
        self.strip = max(16, up_to(self.out_rows, 16))
        self.mix_blocks = -(-self.mix_rows // self.strip)
        self.rows = self.top + self.strip
        self.width = width
        assert embed == 128 and filters == 128 and (1 + self.mix_blocks) * 128 <= width

    def mix_parts(self):
        for block in range(self.mix_blocks):
            start = block * self.strip
            yield start, min(self.strip, self.mix_rows - start), slice(128 * (block + 1), 128 * (block + 2))


def weights_kernel(lay, columns, *refs):
    size, peers = lay.size, lay.peers
    pieces, raws, rest = refs[:size], refs[size : 2 * size], refs[2 * size :]
    out_w_ref, mix_ref, keep_ref, away_ref, g_in, g_out = rest
    deep, width, wide = columns
    share = width // size
    for i in range(size):
        raw = raws[i][...]
        grad_pre = pre_grads(raw, out_w_ref[...], pieces[i][:, deep : deep + width])
        term_in = mm_tn(pieces[i][:, :deep], grad_pre)
        term_out = mm_tn(pieces[i][:, deep + width :], raw)
        if i == 0:
            g_in[...] = term_in
            g_out[...] = term_out
        else:
            g_in[...] += term_in
            g_out[...] += term_out
    me = lax.axis_index("dp")
    first = 0 if wide == share else lax.axis_index("blk") * share
    keep_ref[:, lay.top :, :] = jnp.zeros((peers // 2, lay.strip, width), F32)
    away_ref[:, lay.top :, :] = jnp.zeros((peers // 2, lay.strip, width), BF16)
    if lay.top > lay.in_rows:
        keep_ref[:, : lay.top, :] = jnp.zeros((peers // 2, lay.top, width), F32)
        away_ref[:, : lay.top, :] = jnp.zeros((peers // 2, lay.top, width), BF16)
    for slot in range(peers):
        owner = me ^ slot
        target = away_ref if slot & 1 else keep_ref
        at = slot >> 1
        target[at, : lay.in_rows, :] = g_in[pl.ds(owner * lay.in_rows, lay.in_rows), :].astype(target.dtype)
        target[at, lay.top : lay.top + lay.out_rows, :128] = g_out[
            pl.ds(first + owner * lay.out_rows, lay.out_rows), :
        ].astype(target.dtype)
        for start, rows, cols in lay.mix_parts():
            target[at, lay.top : lay.top + rows, cols] = mix_ref[
                pl.ds(owner * lay.mix_rows + start, rows), :
            ].astype(target.dtype)


def weight_grads(lay, columns, pieces, raws, w_out, g_mix):
    deep, width, wide = columns
    block = (lay.peers // 2, lay.rows, lay.width)
    args = [*pieces, *raws, w_out, g_mix]
    return pl.pallas_call(
        functools.partial(weights_kernel, lay, columns),
        in_specs=[VMEM] * len(args),
        out_shape=[shape(block, F32), shape(block, BF16)],
        out_specs=[VMEM] * 2,
        scratch_shapes=[pltpu.VMEM((deep, width), F32), pltpu.VMEM((wide, 128), F32)],
        compiler_params=params(16),
        cost_estimate=cost(6e8, 4e6),
    )(*args)


HALVES = 2


def fold_kernel(halves, keep_ref, got_ref, *out_refs):
    slots, rows, width = keep_ref.shape
    part = width // halves
    for half in range(halves):
        cols = slice(half * part, (half + 1) * part)
        outs = out_refs[half * (len(out_refs) // halves) :]
        for i in range(slots):
            total = keep_ref[i, :, cols] + got_ref[i * rows : (i + 1) * rows, cols].astype(F32)
            if slots == 1:
                outs[0][...] = total.astype(BF16)
            elif i % 2 == 0:
                outs[0][i // 2] = total
            else:
                outs[1][i // 2 * rows : (i // 2 + 1) * rows, :] = total.astype(BF16)


def fold(keep, got, halves=1):
    slots, rows, width = keep.shape
    part = width // halves
    outs = [shape((rows, part), BF16)]
    if slots > 1:
        outs = [shape((slots // 2, rows, part), F32), shape((slots // 2 * rows, part), BF16)]
    outs = outs * halves
    return pl.pallas_call(
        functools.partial(fold_kernel, halves),
        in_specs=[VMEM] * 2,
        out_shape=outs,
        out_specs=[VMEM] * len(outs),
        compiler_params=params(8),
        cost_estimate=cost(1e6, 2e6),
    )(keep, got)


def plane_order(slots):
    order, step = [0], slots // 2
    while step:
        order += [z ^ step for z in order]
        step //= 2
    return order


def finish_kernel(lay, parts, done, fresh, closing, *refs):
    slots = lay.peers // 2
    part_cols = lay.width // HALVES
    part_refs, refs = dict(zip(parts, refs)), refs[len(parts) :]
    if done:
        refs = refs[2:]
    g_in_hbm, g_out_hbm, *refs = refs
    if closing:
        g_mix_ref, *refs = refs
    stage, strip_stage, sems, strip_sems = refs
    me_blk, me_dp = lax.axis_index("blk"), lax.axis_index("dp")
    copies = []

    def send(kept, slot, target, sem):
        copy = pltpu.make_async_copy(kept.at[slot], target, sem.at[slot])
        copy.start()
        copies.append(copy)

    for n, (hop, core, half) in enumerate(fresh):
        source = part_refs[hop, core, half]
        cols = slice(half * part_cols, (half + 1) * part_cols)
        for block, z in enumerate(plane_order(slots)):
            slot = n * slots + block
            at = block * lay.rows
            owner = (me_blk ^ hop) * lay.peers + (me_dp ^ (2 * z + core))
            stage[slot] = source[at : at + lay.in_rows, :].astype(F32)
            send(stage, slot, g_in_hbm.at[pl.ds(owner * lay.in_rows, lay.in_rows), cols], sems)
            if half == 0:
                strip = at + lay.top
                strip_stage[slot] = source[strip : strip + lay.out_rows, :128].astype(F32)
                send(
                    strip_stage,
                    slot,
                    g_out_hbm.at[pl.ds(owner * lay.out_rows, lay.out_rows), :],
                    strip_sems,
                )
    if closing:
        for core in range(2):
            for block, z in enumerate(plane_order(slots)):
                strip = block * lay.rows + lay.top
                owner = me_dp ^ (2 * z + core)
                for start, rows, cols in lay.mix_parts():
                    half, first = divmod(cols.start, part_cols)
                    terms = [
                        part_refs[hop, core, half][strip : strip + rows, first : first + 128].astype(F32)
                        for hop in range(lay.size)
                    ]
                    while len(terms) > 1:
                        terms = [terms[t] + terms[t + 1] for t in range(0, len(terms), 2)]
                    g_mix_ref[pl.ds(owner * lay.mix_rows + start, rows), :] = terms[0]
    for copy in copies:
        copy.wait()


def finish(lay, parts, done, fresh, closing, lanes, feats, width):
    slots = len(fresh) * lay.peers // 2
    outs = [shape((feats, width), F32), shape((width, 128), F32)]
    specs = [ANY, ANY]
    if closing:
        outs.append(shape((lanes, 128), F32))
        specs.append(VMEM)
    return pl.pallas_call(
        functools.partial(finish_kernel, lay, tuple(parts), bool(done), tuple(fresh), closing),
        in_specs=[VMEM] * len(parts) + [ANY] * len(done),
        out_shape=outs,
        out_specs=specs,
        scratch_shapes=[
            pltpu.VMEM((slots, lay.in_rows, lay.width // HALVES), F32),
            pltpu.VMEM((slots, lay.out_rows, 128), F32),
            pltpu.SemaphoreType.DMA((slots,)),
            pltpu.SemaphoreType.DMA((slots,)),
        ],
        input_output_aliases={len(parts) + i: i for i in range(len(done))},
        compiler_params=params(24),
        cost_estimate=cost(1e6, 8e6),
    )(*parts.values(), *done)


def stack_kernel(*refs):
    rows = refs[0].shape[0]
    for i, each in enumerate(refs[:-1]):
        refs[-1][i * rows : (i + 1) * rows, :] = each[...]


def stack(blocks):
    rows, width = blocks[0].shape
    return pl.pallas_call(
        stack_kernel,
        in_specs=[VMEM] * len(blocks),
        out_shape=shape((len(blocks) * rows, width), blocks[0].dtype),
        out_specs=VMEM,
        compiler_params=params(8),
        cost_estimate=cost(1e3, 1e5),
    )(*blocks)


def swap(block, axis, bit):
    size = lax.axis_size(axis)
    return lax.ppermute(block, axis, [(src, src ^ bit) for src in range(size)])


def spread(block, axis, hops):
    return [block] + [swap(block, axis, hop) for hop in hops]


def on_device(patches, w_mix, w_in, w_out, partner_dev, partner_row):
    count, _, lanes = patches.shape
    filters = w_mix.shape[1]
    feats, width = w_in.shape
    embed = w_out.shape[1]
    freqs = feats // filters
    size, peers = lax.axis_size("blk"), lax.axis_size("dp")
    assert size & (size - 1) == 0 and peers & (peers - 1) == 0 and peers > 2
    across = range(1, size)
    single = [hop for hop in across if hop & (hop - 1) == 0]
    several = [hop for hop in across if hop & (hop - 1)]
    columns = piece_columns(feats, width, size)
    lay = Layout(lanes, filters, feats, width, embed, size, peers)

    *early, spec, mixed, normed, in_w, out_w, slope, units, unit32, norms, rscale = encode(
        patches, w_mix, w_in, w_out, size
    )
    other = swap(units, "dp", 1)
    pair = pair_up(units, other)
    got = stack(lax.optimization_barrier(cross(pair)))
    factors = {hop: swap(early[hop], "blk", hop) for hop in single}
    swapped = swap(got, "dp", 1)
    local, stats, loss, group, around = scores(
        partner_dev, partner_row, units, pair, got, swapped, size, peers
    )
    other = swap(stats, "dp", 1)
    pair = pair_up(stats, other)
    got = stack(lax.optimization_barrier(cross(pair)))
    factors.update({hop: swap(early[hop], "blk", hop) for hop in several})
    factors = [early[0]] + [factors[hop] for hop in across]
    swapped = swap(got, "dp", 1)
    grad_raw = upper(group, around, stats, pair, got, swapped, local, unit32, norms, size, peers)
    raws = spread(grad_raw, "blk", across)
    g_mix = lower(grad_raw, rscale, in_w, out_w, slope, normed, mixed, spec, freqs)
    keep, away = weight_grads(lay, columns, factors, raws, out_w, g_mix)
    got = swap(away.reshape(-1, away.shape[2]), "dp", 1)
    planes, first = {}, fold(keep, got, HALVES)
    turns = range((peers // 2).bit_length() - 1)
    halves = range(HALVES)
    kept = {half: first[2 * half : 2 * half + 2] for half in halves}
    for turn in turns:
        for half in halves:
            got = swap(kept[half][1], "dp", 2 << turn)
            kept[half] = fold(kept[half][0], got)
    for half in halves:
        planes[0, half] = kept[half][0]
    for turn in reversed(turns):
        for half in halves:
            got = swap(planes[0, half], "dp", 2 << turn)
            planes[0, half] = stack([planes[0, half], got])
    for half in halves:
        for hop in single:
            planes[hop, half] = swap(planes[0, half], "blk", hop)
        for hop in several:
            bit = hop & -hop if half else 1 << (hop.bit_length() - 1)
            planes[hop, half] = swap(planes[hop ^ bit, half], "blk", bit)
    parts, done = {}, []
    stages = [[(0, 0), (0, 1)], [(hop, 0) for hop in single], [(hop, 1) for hop in single]]
    stages += [[(hop, half) for hop in several] for half in range(HALVES)]
    stages = [stage for stage in stages if stage]
    for order, stage in enumerate(stages):
        fresh = {}
        for hop, half in stage:
            fresh[hop, 0, half] = planes[hop, half]
            fresh[hop, 1, half] = swap(planes[hop, half], "dp", 1)
        parts.update(fresh)
        last = order == len(stages) - 1
        done = finish(
            lay, parts if last else fresh, done, fresh, last, lanes, feats, width
        )
    g_in, g_out, g_mix = done
    return (loss.reshape(count), g_mix, g_in, g_out)


def solution(mesh):
    placed = (P(("blk", "dp"), None, None), P(), P(), P(), P(("blk", "dp")), P(("blk", "dp")))
    return jax.shard_map(
        on_device,
        mesh=mesh,
        in_specs=placed,
        out_specs=(P(("blk", "dp")), P(), P(), P()),
        check_vma=False,
    )
```

```python
import functools
import math

import jax
import jax.numpy as jnp
import numpy as np
from jax import lax
from jax.experimental import pallas as pl
from jax.experimental.pallas import tpu as pltpu
from jax.sharding import PartitionSpec as P


SCALE = 10.0
SUB = 8
BF16 = jnp.bfloat16
F32 = jnp.float32
VMEM = pl.BlockSpec(memory_space=pltpu.VMEM)
ANY = pl.BlockSpec(memory_space=pl.ANY)


def shape(dims, dtype):
    return jax.ShapeDtypeStruct(tuple(dims), dtype)


def hbm(value):
    return pltpu.with_memory_space_constraint(value, pltpu.MemorySpace.HBM)


def mm(left, right):
    return jnp.dot(left, right, preferred_element_type=F32)


def mm_nt(left, right):
    return lax.dot_general(left, right, (((1,), (1,)), ((), ())), preferred_element_type=F32)


def mm_tn(left, right):
    return lax.dot_general(left, right, (((0,), (0,)), ((), ())), preferred_element_type=F32)


def params(mib):
    return pltpu.CompilerParams(vmem_limit_bytes=mib << 20)


def cost(flops, nbytes):
    return pl.CostEstimate(flops=int(flops), bytes_accessed=int(nbytes), transcendentals=0)


def angle_basis(length, freqs):
    phase = np.mod(np.outer(np.arange(freqs), np.arange(length)), length).astype(np.float32)
    phase = phase * np.float32(2.0 * math.pi / length)
    table = np.concatenate([np.cos(phase), -np.sin(phase)], axis=0).astype(np.float32)
    basis = np.einsum("ka,pq->kpqa", table, np.eye(SUB, dtype=np.float32))
    return jnp.asarray(basis.reshape(2 * freqs * SUB, SUB * length), BF16)


def encode_kernel(freqs, size, rounds, patch_hbm, basis_hbm, mix_hbm, out_hbm, in_hbm, *rest):
    piece_hbms, rest = rest[:size], rest[size:]
    spec, mixed, normed, in_w, out_w, slope, units_ref, unit32_ref, norm_ref, rscale_ref, *rest = rest
    patches, basis, mix, feat, hidden, *sems = rest
    table_sems, patch_sems, out_sems = sems
    count, length, lanes = patches.shape
    filters = mix.shape[1]
    half = freqs * SUB
    per = count // rounds
    groups = per // SUB

    def table(i, source, target):
        return pltpu.make_async_copy(source, target, table_sems.at[i])

    tables = [
        table(i, *pair)
        for i, pair in enumerate(
            [(basis_hbm, basis), (mix_hbm, mix), (in_hbm, in_w), (out_hbm, out_w)]
        )
    ]

    def fetch(r):
        rows = pl.ds(r * per, per)
        return pltpu.make_async_copy(patch_hbm.at[rows], patches.at[rows], patch_sems.at[r])

    tables[0].start()
    fetch(0).start()
    tables[1].start()
    for r in range(1, rounds):
        fetch(r).start()
    tables[2].start()
    tables[3].start()
    tables[0].wait()
    tables[1].wait()

    def one(r, carry):
        fetch(r).wait()
        for s in range(groups):
            g = r * groups + s
            base = pl.multiple_of(g * SUB, SUB)
            block = patches[pl.ds(base, SUB)].reshape(SUB * length, lanes)
            part = mm(basis[...], block).astype(BF16)
            spec[g] = part
            both = mm(part, mix[...])
            real_part, imag_part = both[:half], both[half:]
            powers = real_part * real_part + imag_part * imag_part
            share = 2.0 / (1.0 + powers)
            mixed[g, :half] = real_part * share
            mixed[g, half:] = imag_part * share
            piece = jnp.log1p(powers)
            for k in range(freqs):
                feat[pl.ds(base, SUB), k * filters : (k + 1) * filters] = piece[
                    k * SUB : (k + 1) * SUB
                ]
        return carry

    lax.fori_loop(0, rounds, one, 0)
    features = feat[...]
    removed = features - jnp.mean(features, axis=1, keepdims=True)
    rscale = lax.rsqrt(jnp.mean(removed * removed, axis=1, keepdims=True) + 1e-05)
    normed[...] = (removed * rscale).astype(BF16)
    rscale_ref[...] = jnp.broadcast_to(rscale, rscale_ref.shape)
    deep, width, wide = piece_columns(normed.shape[1], hidden.shape[1], size)
    me = lax.axis_index("blk")
    outs = []
    for i, piece_hbm in enumerate(piece_hbms):
        columns = pl.ds(pl.multiple_of((me ^ i) * deep, 128), deep)
        outs.append(
            pltpu.make_async_copy(
                normed.at[:, columns], piece_hbm.at[:, :deep], out_sems.at[len(outs)]
            )
        )
    for each in outs:
        each.start()
    tables[2].wait()
    preact = mm(normed[...], in_w[...])
    sigm = jax.nn.sigmoid(preact)
    hidden[...] = (preact * sigm).astype(BF16)
    slope[...] = (sigm * (1.0 + preact * (1.0 - sigm))).astype(BF16)
    late = []
    for i, piece_hbm in enumerate(piece_hbms):
        if wide == hidden.shape[1]:
            columns = pl.ds(0, wide)
        else:
            columns = pl.ds(pl.multiple_of((me ^ i) * wide, 128), wide)
        for source, target in (
            (slope, piece_hbm.at[:, deep : deep + width]),
            (hidden.at[:, columns], piece_hbm.at[:, deep + width :]),
        ):
            late.append(
                pltpu.make_async_copy(source, target, out_sems.at[len(outs) + len(late)])
            )
    for each in late:
        each.start()
    tables[3].wait()
    raw = mm(hidden[...], out_w[...])
    norms = jnp.sqrt(jnp.sum(raw * raw, axis=1, keepdims=True) + 1e-06)
    norm_ref[...] = jnp.broadcast_to(norms, norm_ref.shape)
    unit32 = raw / norms
    unit32_ref[...] = unit32
    units_ref[...] = unit32.astype(BF16)
    for each in outs + late:
        each.wait()


def piece_columns(feats, width, size):
    wide = width // size
    return feats // size, width, wide if wide % 128 == 0 else width


def encode(patches, w_mix, w_in, w_out, size):
    count, length, lanes = patches.shape
    filters = w_mix.shape[1]
    feats, width = w_in.shape
    embed = w_out.shape[1]
    freqs = feats // filters
    rounds = 4
    assert count % (rounds * SUB) == 0
    groups = count // SUB
    rows = 2 * freqs * SUB
    piece = (count, sum(piece_columns(feats, width, size)))
    kept = [pltpu.MemorySpace.HBM(piece, BF16)] * size
    near = [
        shape((groups, rows, lanes), BF16),
        shape((groups, rows, filters), F32),
        shape((count, feats), BF16),
        shape(w_in.shape, BF16),
        shape(w_out.shape, BF16),
        shape((count, width), BF16),
        shape((count, embed), BF16),
        shape((count, embed), F32),
        shape((count, 128), F32),
        shape((count, 128), F32),
    ]
    return pl.pallas_call(
        functools.partial(encode_kernel, freqs, size, rounds),
        in_specs=[ANY] * 5,
        out_shape=kept + near,
        out_specs=[ANY] * len(kept) + [VMEM] * len(near),
        scratch_shapes=[
            pltpu.VMEM(patches.shape, BF16),
            pltpu.VMEM((rows, SUB * length), BF16),
            pltpu.VMEM(w_mix.shape, BF16),
            pltpu.VMEM((count, feats), F32),
            pltpu.VMEM((count, width), BF16),
            pltpu.SemaphoreType.DMA((4,)),
            pltpu.SemaphoreType.DMA((rounds,)),
            pltpu.SemaphoreType.DMA((3 * size,)),
        ],
        compiler_params=params(24),
        cost_estimate=cost(3e9, 14e6),
    )(*map(hbm, (patches, angle_basis(length, freqs), w_mix, w_out, w_in)))


def exponentials(units, keys, own):
    expo = jnp.exp(SCALE * mm_nt(units, keys))
    if own:
        row = lax.broadcasted_iota(jnp.int32, expo.shape, 0)
        col = lax.broadcasted_iota(jnp.int32, expo.shape, 1)
        expo = jnp.where(row == col, 0.0, expo)
    return expo


def pair_up_kernel(own_ref, other_ref, out_ref):
    rows = own_ref.shape[0]
    own, other = own_ref[...], other_ref[...]
    first = lax.axis_index("dp") % 2 == 0
    out_ref[:rows, :] = jnp.where(first, own, other)
    out_ref[rows:, :] = jnp.where(first, other, own)


def pair_up(own, other):
    rows, width = own.shape
    return pl.pallas_call(
        pair_up_kernel,
        in_specs=[VMEM] * 2,
        out_shape=shape((2 * rows, width), own.dtype),
        out_specs=VMEM,
        compiler_params=params(8),
        cost_estimate=cost(1e3, 1e5),
    )(own, other)


def cross(pair):
    size, peers = lax.axis_size("blk"), lax.axis_size("dp")
    got = []
    for k in range(1, max(size, peers // 2)):
        routes = []
        for blk in range(size):
            for dp in range(peers):
                if dp % 2 == 0 and 2 * k < peers:
                    routes.append((blk * peers + dp, blk * peers + (dp ^ (2 * k))))
                if dp % 2 == 1 and k < size:
                    routes.append((blk * peers + dp, (blk ^ k) * peers + dp))
        got.append(lax.ppermute(pair, ("blk", "dp"), routes))
    return got


def crossed(got_ref, swapped_ref, rows):
    first = lax.axis_index("dp") % 2 == 0

    def along(k, core):
        at = (2 * (k - 1) + core) * rows
        return jnp.where(first, got_ref[at : at + rows, :], swapped_ref[at : at + rows, :])

    def across(k):
        at = 2 * (k - 1) * rows
        low = jnp.where(first, swapped_ref[at : at + rows, :], got_ref[at + rows : at + 2 * rows, :])
        return low

    return along, across


def as_rows(column, count):
    return jnp.broadcast_to(column, (column.shape[0], count)).T


def scores_kernel(
    size,
    peers,
    dev_ref,
    row_ref,
    units_ref,
    pair_ref,
    got_ref,
    swapped_ref,
    local_ref,
    stats_ref,
    loss_ref,
    group_ref,
    around_ref,
):
    units = units_ref[...]
    count = units.shape[0]
    along, across = crossed(got_ref, swapped_ref, count)
    zneg = numer = None
    for i in range(size):
        keys = across(i) if i else units
        group_ref[i * count : (i + 1) * count, :] = keys
        expo = exponentials(units, keys, i == 0)
        total = jnp.sum(expo, axis=1, keepdims=True)
        term = mm(expo.astype(BF16), keys)
        zneg = total if zneg is None else zneg + total
        numer = term if numer is None else numer + term
    me = lax.axis_index("dp")
    dev = dev_ref[...]
    place = (2 * ((dev ^ me) >> 1) + (dev & 1)) * count + row_ref[...]
    place = jnp.broadcast_to(place.astype(F32), (count, count)).T
    lane = lax.broadcasted_iota(jnp.int32, (count, count), 1).astype(F32)
    positive = None
    for i in range(peers):
        k, core = i // 2, i % 2
        source = along(k, core) if k else pair_ref[core * count : (core + 1) * count, :]
        around_ref[i * count : (i + 1) * count, :] = source
        hit = jnp.where(place - float(i * count) == lane, 1.0, 0.0).astype(BF16)
        term = mm(hit, source)
        positive = term if positive is None else positive + term
    spos = SCALE * jnp.sum(units.astype(F32) * positive, axis=1, keepdims=True)
    top = jnp.exp(spos)
    totals = top + zneg
    less = top / totals - 1.0
    coef = SCALE / count
    local_ref[...] = coef * (less * positive + numer / totals)
    loss_ref[...] = as_rows(jnp.log(totals) - spos, count)[:1]
    stats_ref[...] = jnp.zeros(stats_ref.shape, F32)
    stats_ref[0:1, :] = as_rows(totals, count)[:1]
    stats_ref[1:2, :] = as_rows(coef * less, count)[:1]
    stats_ref[2:3, :] = (dev * count + row_ref[...]).astype(F32)


def scores(partner_dev, partner_row, units, pair, got, swapped, size, peers):
    count, embed = units.shape
    return pl.pallas_call(
        functools.partial(scores_kernel, size, peers),
        in_specs=[VMEM] * 6,
        out_shape=[
            shape((count, embed), F32),
            shape((SUB, count), F32),
            shape((1, count), F32),
            shape((size * count, embed), BF16),
            shape((peers * count, embed), BF16),
        ],
        out_specs=[VMEM] * 5,
        compiler_params=params(16),
        cost_estimate=cost(4e8, 1e6),
    )(partner_dev.reshape(1, count), partner_row.reshape(1, count), units, pair, got, swapped)


def upper_kernel(
    size,
    peers,
    group_ref,
    around_ref,
    stats_ref,
    pair_ref,
    got_ref,
    swapped_ref,
    local_ref,
    unit32_ref,
    norm_ref,
    out_ref,
):
    count, _ = local_ref.shape
    coef = SCALE / count
    along, across = crossed(got_ref, swapped_ref, SUB)
    units = group_ref[:count, :]
    keyterm = None
    for i in range(size):
        keys = group_ref[i * count : (i + 1) * count, :]
        expo = exponentials(units, keys, i == 0)
        totals = (across(i) if i else stats_ref[...])[0:1, :]
        term = mm((expo / totals).astype(BF16), keys)
        keyterm = term if keyterm is None else keyterm + term
    mine = lax.axis_index("dp") * count + lax.broadcasted_iota(jnp.int32, (count, count), 0)
    mine = mine.astype(F32)
    chosen = amount = None
    for i in range(peers):
        k, core = i // 2, i % 2
        table = along(k, core) if k else pair_ref[core * SUB : (core + 1) * SUB, :]
        hit = table[2:3, :] == mine
        share = jnp.where(hit, table[1:2, :], 0.0)
        term = mm(jnp.where(hit, 1.0, 0.0).astype(BF16), around_ref[i * count : (i + 1) * count, :])
        chosen = term if chosen is None else chosen + term
        amount = share if amount is None else amount + share
    back = jnp.sum(amount, axis=1, keepdims=True) * chosen
    grad_units = local_ref[...] + coef * keyterm + back
    unit32 = unit32_ref[...]
    tilt = jnp.sum(unit32 * grad_units, axis=1, keepdims=True)
    out_ref[...] = ((grad_units - unit32 * tilt) / norm_ref[:, :1]).astype(BF16)


def upper(group, around, stats, pair, got, swapped, local, unit32, norms, size, peers):
    count, embed = local.shape
    args = [group, around, stats, pair, got, swapped, local, unit32, norms]
    return pl.pallas_call(
        functools.partial(upper_kernel, size, peers),
        in_specs=[VMEM] * len(args),
        out_shape=shape((count, embed), BF16),
        out_specs=VMEM,
        compiler_params=params(16),
        cost_estimate=cost(4e8, 2e6),
    )(*args)


def pre_grads(grad_raw, out_w, slope):
    return (mm_nt(grad_raw, out_w) * slope.astype(F32)).astype(BF16)


def lower_kernel(
    freqs, raw_ref, rscale_ref, in_w, out_w, slope, normed, mixed, spec, g_mix_ref, grad_feat
):
    grad_pre = pre_grads(raw_ref[...], out_w[...], slope[...])
    grad_norm = mm_nt(grad_pre, in_w[...])
    xhat = normed[...].astype(F32)
    mean = jnp.mean(grad_norm, axis=1, keepdims=True)
    tilt = jnp.mean(grad_norm * xhat, axis=1, keepdims=True)
    grad_feat[...] = rscale_ref[:, :1] * (grad_norm - mean - xhat * tilt)
    groups, _, filters = mixed.shape
    half = freqs * SUB

    def one(g, total):
        base = pl.multiple_of(g * SUB, SUB)
        grads = jnp.concatenate(
            [grad_feat[pl.ds(base, SUB), k * filters : (k + 1) * filters] for k in range(freqs)],
            axis=0,
        )
        grad_mixed = jnp.concatenate(
            [mixed[g, :half] * grads, mixed[g, half:] * grads], axis=0
        ).astype(BF16)
        return total + mm_tn(grad_mixed, spec[g])

    total = lax.fori_loop(0, groups, one, jnp.zeros((filters, spec.shape[2]), F32), unroll=16)
    g_mix_ref[...] = total.T


def lower(grad_raw, rscale, in_w, out_w, slope, normed, mixed, spec, freqs):
    filters, lanes = mixed.shape[2], spec.shape[2]
    return pl.pallas_call(
        functools.partial(lower_kernel, freqs),
        in_specs=[VMEM] * 8,
        out_shape=shape((lanes, filters), F32),
        out_specs=VMEM,
        scratch_shapes=[pltpu.VMEM(normed.shape, F32)],
        compiler_params=params(20),
        cost_estimate=cost(1e9, 7e6),
    )(grad_raw, rscale, in_w, out_w, slope, normed, mixed, spec)


def up_to(rows, unit):
    return -(-rows // unit) * unit


class Layout:
    def __init__(self, lanes, filters, feats, width, embed, size, peers):
        self.size, self.peers = size, peers
        self.in_rows = feats // size // peers
        self.out_rows = width // size // peers
        self.mix_rows = lanes // peers
        self.top = up_to(self.in_rows, 16)
        self.strip = max(16, up_to(self.out_rows, 16))
        self.mix_blocks = -(-self.mix_rows // self.strip)
        self.rows = self.top + self.strip
        self.width = width
        assert embed == 128 and filters == 128 and (1 + self.mix_blocks) * 128 <= width

    def mix_parts(self):
        for block in range(self.mix_blocks):
            start = block * self.strip
            yield start, min(self.strip, self.mix_rows - start), slice(128 * (block + 1), 128 * (block + 2))


def weights_kernel(lay, columns, *refs):
    size, peers = lay.size, lay.peers
    pieces, raws, rest = refs[:size], refs[size : 2 * size], refs[2 * size :]
    out_w_ref, mix_ref, keep_ref, away_ref, g_in, g_out = rest
    deep, width, wide = columns
    share = width // size
    for i in range(size):
        raw = raws[i][...]
        grad_pre = pre_grads(raw, out_w_ref[...], pieces[i][:, deep : deep + width])
        term_in = mm_tn(pieces[i][:, :deep], grad_pre)
        term_out = mm_tn(pieces[i][:, deep + width :], raw)
        if i == 0:
            g_in[...] = term_in
            g_out[...] = term_out
        else:
            g_in[...] += term_in
            g_out[...] += term_out
    me = lax.axis_index("dp")
    first = 0 if wide == share else lax.axis_index("blk") * share
    keep_ref[:, lay.top :, :] = jnp.zeros((peers // 2, lay.strip, width), F32)
    away_ref[:, lay.top :, :] = jnp.zeros((peers // 2, lay.strip, width), BF16)
    if lay.top > lay.in_rows:
        keep_ref[:, : lay.top, :] = jnp.zeros((peers // 2, lay.top, width), F32)
        away_ref[:, : lay.top, :] = jnp.zeros((peers // 2, lay.top, width), BF16)
    for slot in range(peers):
        owner = me ^ slot
        target = away_ref if slot & 1 else keep_ref
        at = slot >> 1
        target[at, : lay.in_rows, :] = g_in[pl.ds(owner * lay.in_rows, lay.in_rows), :].astype(target.dtype)
        target[at, lay.top : lay.top + lay.out_rows, :128] = g_out[
            pl.ds(first + owner * lay.out_rows, lay.out_rows), :
        ].astype(target.dtype)
        for start, rows, cols in lay.mix_parts():
            target[at, lay.top : lay.top + rows, cols] = mix_ref[
                pl.ds(owner * lay.mix_rows + start, rows), :
            ].astype(target.dtype)


def weight_grads(lay, columns, pieces, raws, w_out, g_mix):
    deep, width, wide = columns
    block = (lay.peers // 2, lay.rows, lay.width)
    args = [*pieces, *raws, w_out, g_mix]
    return pl.pallas_call(
        functools.partial(weights_kernel, lay, columns),
        in_specs=[VMEM] * len(args),
        out_shape=[shape(block, F32), shape(block, BF16)],
        out_specs=[VMEM] * 2,
        scratch_shapes=[pltpu.VMEM((deep, width), F32), pltpu.VMEM((wide, 128), F32)],
        compiler_params=params(16),
        cost_estimate=cost(6e8, 4e6),
    )(*args)


HALVES = 2


def pair_kernel(keep_ref, got_ref, *out_refs):
    slots, _, width = keep_ref.shape
    part = width // HALVES
    for half in range(HALVES):
        cols = slice(half * part, (half + 1) * part)
        for i in range(slots):
            out_ref = out_refs[half * slots + i]
            total = keep_ref[i, :, cols] + got_ref[i, :, cols].astype(F32)
            out_ref[...] = total.astype(out_ref.dtype)


def pair_sum(keep, got):
    slots, rows, width = keep.shape
    part = (rows, width // HALVES)
    outs = [shape(part, F32)] + [shape(part, BF16)] * (slots - 1)
    sums = pl.pallas_call(
        pair_kernel,
        in_specs=[VMEM] * 2,
        out_shape=outs * HALVES,
        out_specs=[VMEM] * (slots * HALVES),
        compiler_params=params(8),
        cost_estimate=cost(1e6, 2e6),
    )(keep, got)
    return [sums[half * slots : (half + 1) * slots] for half in range(HALVES)]


def total_kernel(own_ref, *refs):
    total = own_ref[...]
    for each in refs[:-1]:
        total = total + each[...].astype(F32)
    refs[-1][...] = total.astype(BF16)


def total_sum(own, got):
    return pl.pallas_call(
        total_kernel,
        in_specs=[VMEM] * (1 + len(got)),
        out_shape=shape(own.shape, BF16),
        out_specs=VMEM,
        compiler_params=params(8),
        cost_estimate=cost(1e6, 1e6),
    )(own, *got)


def finish_kernel(lay, parts, done, fresh, closing, *refs):
    slots = lay.peers // 2
    part_cols = lay.width // HALVES
    part_refs, refs = dict(zip(parts, refs)), refs[len(parts) :]
    if done > 2:
        mix_ref = refs[2]
    g_in_hbm, g_out_hbm, *refs = refs[done:]
    if closing is not None:
        g_mix_ref, *refs = refs
    stage, strip_stage, sems, strip_sems = refs
    me_blk, me_dp = lax.axis_index("blk"), lax.axis_index("dp")
    copies = []

    def send(kept, slot, target, sem):
        copy = pltpu.make_async_copy(kept.at[slot], target, sem.at[slot])
        copy.start()
        copies.append(copy)

    for n, (hop, core, half) in enumerate(fresh):
        source = part_refs[hop, core, half]
        cols = slice(half * part_cols, (half + 1) * part_cols)
        for z in range(slots):
            slot = n * slots + z
            at = z * lay.rows
            owner = (me_blk ^ hop) * lay.peers + (me_dp ^ (2 * z + core))
            stage[slot] = source[at : at + lay.in_rows, :].astype(F32)
            send(stage, slot, g_in_hbm.at[pl.ds(owner * lay.in_rows, lay.in_rows), cols], sems)
            if half == 0:
                strip = at + lay.top
                strip_stage[slot] = source[strip : strip + lay.out_rows, :128].astype(F32)
                send(
                    strip_stage,
                    slot,
                    g_out_hbm.at[pl.ds(owner * lay.out_rows, lay.out_rows), :],
                    strip_sems,
                )
    if closing is not None:
        for core in range(2):
            for z in range(slots):
                strip = z * lay.rows + lay.top
                owner = me_dp ^ (2 * z + core)
                for start, rows, cols in lay.mix_parts():
                    half, first = divmod(cols.start, part_cols)
                    at = pl.ds(owner * lay.mix_rows + start, rows)
                    if half < closing:
                        g_mix_ref[at, :] = mix_ref[at, :]
                    if half != closing:
                        continue
                    terms = [
                        part_refs[hop, core, half][strip : strip + rows, first : first + 128].astype(F32)
                        for hop in range(lay.size)
                    ]
                    while len(terms) > 1:
                        terms = [terms[t] + terms[t + 1] for t in range(0, len(terms), 2)]
                    g_mix_ref[at, :] = terms[0]
    for copy in copies:
        copy.wait()


def finish(lay, parts, done, fresh, closing, lanes, feats, width):
    slots = len(fresh) * lay.peers // 2
    outs = [shape((feats, width), F32), shape((width, 128), F32)]
    specs = [ANY, ANY]
    if closing is not None:
        outs.append(shape((lanes, 128), F32))
        specs.append(VMEM)
    return pl.pallas_call(
        functools.partial(finish_kernel, lay, tuple(parts), len(done), tuple(fresh), closing),
        in_specs=[VMEM] * len(parts) + [ANY, ANY, VMEM][: len(done)],
        out_shape=outs,
        out_specs=specs,
        scratch_shapes=[
            pltpu.VMEM((slots, lay.in_rows, lay.width // HALVES), F32),
            pltpu.VMEM((slots, lay.out_rows, 128), F32),
            pltpu.SemaphoreType.DMA((slots,)),
            pltpu.SemaphoreType.DMA((slots,)),
        ],
        input_output_aliases={len(parts) + i: i for i in range(min(2, len(done)))},
        compiler_params=params(24),
        cost_estimate=cost(1e6, 8e6),
    )(*parts.values(), *done)


def stack_kernel(*refs):
    rows = refs[0].shape[0]
    for i, each in enumerate(refs[:-1]):
        refs[-1][i * rows : (i + 1) * rows, :] = each[...]


def stack(blocks):
    rows, width = blocks[0].shape
    return pl.pallas_call(
        stack_kernel,
        in_specs=[VMEM] * len(blocks),
        out_shape=shape((len(blocks) * rows, width), blocks[0].dtype),
        out_specs=VMEM,
        compiler_params=params(8),
        cost_estimate=cost(1e3, 1e5),
    )(*blocks)


def swap(block, axis, bit):
    size = lax.axis_size(axis)
    return lax.ppermute(block, axis, [(src, src ^ bit) for src in range(size)])


def spread(block, axis, hops):
    return [block] + [swap(block, axis, hop) for hop in hops]


def on_device(patches, w_mix, w_in, w_out, partner_dev, partner_row):
    count, _, lanes = patches.shape
    filters = w_mix.shape[1]
    feats, width = w_in.shape
    embed = w_out.shape[1]
    freqs = feats // filters
    size, peers = lax.axis_size("blk"), lax.axis_size("dp")
    assert size & (size - 1) == 0 and peers & (peers - 1) == 0 and peers > 1
    across, along = range(1, size), range(2, peers, 2)
    single = [hop for hop in across if hop & (hop - 1) == 0]
    several = [hop for hop in across if hop & (hop - 1)]
    columns = piece_columns(feats, width, size)
    lay = Layout(lanes, filters, feats, width, embed, size, peers)

    *early, spec, mixed, normed, in_w, out_w, slope, units, unit32, norms, rscale = encode(
        patches, w_mix, w_in, w_out, size
    )
    other = swap(units, "dp", 1)
    pair = pair_up(units, other)
    got = stack(lax.optimization_barrier(cross(pair)))
    factors = {hop: swap(early[hop], "blk", hop) for hop in single}
    swapped = swap(got, "dp", 1)
    local, stats, loss, group, around = scores(
        partner_dev, partner_row, units, pair, got, swapped, size, peers
    )
    other = swap(stats, "dp", 1)
    pair = pair_up(stats, other)
    got = stack(lax.optimization_barrier(cross(pair)))
    factors.update({hop: swap(early[hop], "blk", hop) for hop in several})
    factors = [early[0]] + [factors[hop] for hop in across]
    swapped = swap(got, "dp", 1)
    grad_raw = upper(group, around, stats, pair, got, swapped, local, unit32, norms, size, peers)
    raws = spread(grad_raw, "blk", across)
    g_mix = lower(grad_raw, rscale, in_w, out_w, slope, normed, mixed, spec, freqs)
    keep, away = weight_grads(lay, columns, factors, raws, out_w, g_mix)
    got = swap(away, "dp", 1)
    planes = {}
    for half, (own, *sends) in enumerate(pair_sum(keep, got)):
        got = [swap(block, "dp", hop) for block, hop in zip(sends, along)]
        share = total_sum(own, got)
        shares = spread(share, "dp", along)
        planes[0, half] = stack(shares)
        for hop in single:
            planes[hop, half] = swap(planes[0, half], "blk", hop)
        for hop in several:
            bit = hop & -hop if half else 1 << (hop.bit_length() - 1)
            planes[hop, half] = swap(planes[hop ^ bit, half], "blk", bit)
    parts, done = {}, []
    stages = [[(0, 0), (0, 1)], [(hop, 0) for hop in single], [(hop, 1) for hop in single]]
    stages += [[(hop, half) for hop in several] for half in range(HALVES)]
    stages = [stage for stage in stages if stage]
    for order, stage in enumerate(stages):
        fresh = {}
        for hop, half in stage:
            fresh[hop, 0, half] = planes[hop, half]
            fresh[hop, 1, half] = swap(planes[hop, half], "dp", 1)
        parts.update(fresh)
        closing = order - len(stages) + HALVES
        taken = fresh
        if closing >= 0:
            taken = {part: block for part, block in parts.items() if part[2] == closing}
        done = finish(
            lay, taken, done, fresh, closing if closing >= 0 else None, lanes, feats, width
        )
    g_in, g_out, g_mix = done
    return (loss.reshape(count), g_mix, g_in, g_out)


def solution(mesh):
    placed = (P(("blk", "dp"), None, None), P(), P(), P(), P(("blk", "dp")), P(("blk", "dp")))
    return jax.shard_map(
        on_device,
        mesh=mesh,
        in_specs=placed,
        out_specs=(P(("blk", "dp")), P(), P(), P()),
        check_vma=False,
    )
```

```python
import functools
import math

import jax
import jax.numpy as jnp
import numpy as np
from jax import lax
from jax.experimental import pallas as pl
from jax.experimental.pallas import tpu as pltpu
from jax.sharding import PartitionSpec as P


SCALE = 10.0
SUB = 8
BF16 = jnp.bfloat16
F32 = jnp.float32
VMEM = pl.BlockSpec(memory_space=pltpu.VMEM)
ANY = pl.BlockSpec(memory_space=pl.ANY)


def shape(dims, dtype):
    return jax.ShapeDtypeStruct(tuple(dims), dtype)


def hbm(value):
    return pltpu.with_memory_space_constraint(value, pltpu.MemorySpace.HBM)


def mm(left, right):
    return jnp.dot(left, right, preferred_element_type=F32)


def mm_nt(left, right):
    return lax.dot_general(left, right, (((1,), (1,)), ((), ())), preferred_element_type=F32)


def mm_tn(left, right):
    return lax.dot_general(left, right, (((0,), (0,)), ((), ())), preferred_element_type=F32)


def params(mib):
    return pltpu.CompilerParams(vmem_limit_bytes=mib << 20)


def cost(flops, nbytes):
    return pl.CostEstimate(flops=int(flops), bytes_accessed=int(nbytes), transcendentals=0)


def angle_basis(length, freqs):
    phase = np.mod(np.outer(np.arange(freqs), np.arange(length)), length).astype(np.float32)
    phase = phase * np.float32(2.0 * math.pi / length)
    table = np.concatenate([np.cos(phase), -np.sin(phase)], axis=0).astype(np.float32)
    basis = np.einsum("ka,pq->kpqa", table, np.eye(SUB, dtype=np.float32))
    return jnp.asarray(basis.reshape(2 * freqs * SUB, SUB * length), BF16)


def encode_kernel(freqs, size, rounds, patch_hbm, basis_hbm, mix_hbm, out_hbm, in_hbm, *rest):
    piece_hbms, rest = rest[:size], rest[size:]
    spec, mixed, normed, in_w, out_w, slope, units_ref, unit32_ref, norm_ref, rscale_ref, *rest = rest
    patches, basis, mix, feat, hidden, *sems = rest
    table_sems, patch_sems, out_sems = sems
    count, length, lanes = patches.shape
    filters = mix.shape[1]
    half = freqs * SUB
    per = count // rounds
    groups = per // SUB

    def table(i, source, target):
        return pltpu.make_async_copy(source, target, table_sems.at[i])

    tables = [
        table(i, *pair)
        for i, pair in enumerate(
            [(basis_hbm, basis), (mix_hbm, mix), (in_hbm, in_w), (out_hbm, out_w)]
        )
    ]

    def fetch(r):
        rows = pl.ds(r * per, per)
        return pltpu.make_async_copy(patch_hbm.at[rows], patches.at[rows], patch_sems.at[r])

    tables[0].start()
    fetch(0).start()
    tables[1].start()
    for r in range(1, rounds):
        fetch(r).start()
    tables[2].start()
    tables[3].start()
    tables[0].wait()
    tables[1].wait()

    def one(r, carry):
        fetch(r).wait()
        for s in range(groups):
            g = r * groups + s
            base = pl.multiple_of(g * SUB, SUB)
            block = patches[pl.ds(base, SUB)].reshape(SUB * length, lanes)
            part = mm(basis[...], block).astype(BF16)
            spec[g] = part
            both = mm(part, mix[...])
            real_part, imag_part = both[:half], both[half:]
            powers = real_part * real_part + imag_part * imag_part
            share = 2.0 / (1.0 + powers)
            mixed[g, :half] = real_part * share
            mixed[g, half:] = imag_part * share
            piece = jnp.log1p(powers)
            for k in range(freqs):
                feat[pl.ds(base, SUB), k * filters : (k + 1) * filters] = piece[
                    k * SUB : (k + 1) * SUB
                ]
        return carry

    lax.fori_loop(0, rounds, one, 0)
    features = feat[...]
    removed = features - jnp.mean(features, axis=1, keepdims=True)
    rscale = lax.rsqrt(jnp.mean(removed * removed, axis=1, keepdims=True) + 1e-05)
    normed[...] = (removed * rscale).astype(BF16)
    rscale_ref[...] = jnp.broadcast_to(rscale, rscale_ref.shape)
    deep, width, wide = piece_columns(normed.shape[1], hidden.shape[1], size)
    me = lax.axis_index("blk")
    outs = []
    for i, piece_hbm in enumerate(piece_hbms):
        columns = pl.ds(pl.multiple_of((me ^ i) * deep, 128), deep)
        outs.append(
            pltpu.make_async_copy(
                normed.at[:, columns], piece_hbm.at[:, :deep], out_sems.at[len(outs)]
            )
        )
    for each in outs:
        each.start()
    tables[2].wait()
    preact = mm(normed[...], in_w[...])
    sigm = jax.nn.sigmoid(preact)
    hidden[...] = (preact * sigm).astype(BF16)
    slope[...] = (sigm * (1.0 + preact * (1.0 - sigm))).astype(BF16)
    late = []
    for i, piece_hbm in enumerate(piece_hbms):
        if wide == hidden.shape[1]:
            columns = pl.ds(0, wide)
        else:
            columns = pl.ds(pl.multiple_of((me ^ i) * wide, 128), wide)
        for source, target in (
            (slope, piece_hbm.at[:, deep : deep + width]),
            (hidden.at[:, columns], piece_hbm.at[:, deep + width :]),
        ):
            late.append(
                pltpu.make_async_copy(source, target, out_sems.at[len(outs) + len(late)])
            )
    for each in late:
        each.start()
    tables[3].wait()
    raw = mm(hidden[...], out_w[...])
    norms = jnp.sqrt(jnp.sum(raw * raw, axis=1, keepdims=True) + 1e-06)
    norm_ref[...] = jnp.broadcast_to(norms, norm_ref.shape)
    unit32 = raw / norms
    unit32_ref[...] = unit32
    units_ref[...] = unit32.astype(BF16)
    for each in outs + late:
        each.wait()


def piece_columns(feats, width, size):
    wide = width // size
    return feats // size, width, wide if wide % 128 == 0 else width


def encode(patches, w_mix, w_in, w_out, size):
    count, length, lanes = patches.shape
    filters = w_mix.shape[1]
    feats, width = w_in.shape
    embed = w_out.shape[1]
    freqs = feats // filters
    rounds = 4
    assert count % (rounds * SUB) == 0
    groups = count // SUB
    rows = 2 * freqs * SUB
    piece = (count, sum(piece_columns(feats, width, size)))
    kept = [pltpu.MemorySpace.HBM(piece, BF16)] * size
    near = [
        shape((groups, rows, lanes), BF16),
        shape((groups, rows, filters), F32),
        shape((count, feats), BF16),
        shape(w_in.shape, BF16),
        shape(w_out.shape, BF16),
        shape((count, width), BF16),
        shape((count, embed), BF16),
        shape((count, embed), F32),
        shape((count, 128), F32),
        shape((count, 128), F32),
    ]
    return pl.pallas_call(
        functools.partial(encode_kernel, freqs, size, rounds),
        in_specs=[ANY] * 5,
        out_shape=kept + near,
        out_specs=[ANY] * len(kept) + [VMEM] * len(near),
        scratch_shapes=[
            pltpu.VMEM(patches.shape, BF16),
            pltpu.VMEM((rows, SUB * length), BF16),
            pltpu.VMEM(w_mix.shape, BF16),
            pltpu.VMEM((count, feats), F32),
            pltpu.VMEM((count, width), BF16),
            pltpu.SemaphoreType.DMA((4,)),
            pltpu.SemaphoreType.DMA((rounds,)),
            pltpu.SemaphoreType.DMA((3 * size,)),
        ],
        compiler_params=params(24),
        cost_estimate=cost(3e9, 14e6),
    )(*map(hbm, (patches, angle_basis(length, freqs), w_mix, w_out, w_in)))


def exponentials(units, keys, own):
    expo = jnp.exp(SCALE * mm_nt(units, keys))
    if own:
        row = lax.broadcasted_iota(jnp.int32, expo.shape, 0)
        col = lax.broadcasted_iota(jnp.int32, expo.shape, 1)
        expo = jnp.where(row == col, 0.0, expo)
    return expo


def pair_up_kernel(own_ref, other_ref, out_ref):
    rows = own_ref.shape[0]
    own, other = own_ref[...], other_ref[...]
    first = lax.axis_index("dp") % 2 == 0
    out_ref[:rows, :] = jnp.where(first, own, other)
    out_ref[rows:, :] = jnp.where(first, other, own)


def pair_up(own, other):
    rows, width = own.shape
    return pl.pallas_call(
        pair_up_kernel,
        in_specs=[VMEM] * 2,
        out_shape=shape((2 * rows, width), own.dtype),
        out_specs=VMEM,
        compiler_params=params(8),
        cost_estimate=cost(1e3, 1e5),
    )(own, other)


def cross(pair):
    size, peers = lax.axis_size("blk"), lax.axis_size("dp")
    got = []
    for k in range(1, max(size, peers // 2)):
        routes = []
        for blk in range(size):
            for dp in range(peers):
                if dp % 2 == 0 and 2 * k < peers:
                    routes.append((blk * peers + dp, blk * peers + (dp ^ (2 * k))))
                if dp % 2 == 1 and k < size:
                    routes.append((blk * peers + dp, (blk ^ k) * peers + dp))
        got.append(lax.ppermute(pair, ("blk", "dp"), routes))
    return got


def crossed(got_ref, swapped_ref, rows):
    first = lax.axis_index("dp") % 2 == 0

    def along(k, core):
        at = (2 * (k - 1) + core) * rows
        return jnp.where(first, got_ref[at : at + rows, :], swapped_ref[at : at + rows, :])

    def across(k):
        at = 2 * (k - 1) * rows
        low = jnp.where(first, swapped_ref[at : at + rows, :], got_ref[at + rows : at + 2 * rows, :])
        return low

    return along, across


def as_rows(column, count):
    return jnp.broadcast_to(column, (column.shape[0], count)).T


def scores_kernel(
    size,
    peers,
    dev_ref,
    row_ref,
    units_ref,
    pair_ref,
    got_ref,
    swapped_ref,
    local_ref,
    stats_ref,
    loss_ref,
    group_ref,
    around_ref,
):
    units = units_ref[...]
    count = units.shape[0]
    along, across = crossed(got_ref, swapped_ref, count)
    zneg = numer = None
    for i in range(size):
        keys = across(i) if i else units
        group_ref[i * count : (i + 1) * count, :] = keys
        expo = exponentials(units, keys, i == 0)
        total = jnp.sum(expo, axis=1, keepdims=True)
        term = mm(expo.astype(BF16), keys)
        zneg = total if zneg is None else zneg + total
        numer = term if numer is None else numer + term
    me = lax.axis_index("dp")
    dev = dev_ref[...]
    place = (2 * ((dev ^ me) >> 1) + (dev & 1)) * count + row_ref[...]
    place = jnp.broadcast_to(place.astype(F32), (count, count)).T
    lane = lax.broadcasted_iota(jnp.int32, (count, count), 1).astype(F32)
    positive = None
    for i in range(peers):
        k, core = i // 2, i % 2
        source = along(k, core) if k else pair_ref[core * count : (core + 1) * count, :]
        around_ref[i * count : (i + 1) * count, :] = source
        hit = jnp.where(place - float(i * count) == lane, 1.0, 0.0).astype(BF16)
        term = mm(hit, source)
        positive = term if positive is None else positive + term
    spos = SCALE * jnp.sum(units.astype(F32) * positive, axis=1, keepdims=True)
    top = jnp.exp(spos)
    totals = top + zneg
    less = top / totals - 1.0
    coef = SCALE / count
    local_ref[...] = coef * (less * positive + numer / totals)
    loss_ref[...] = as_rows(jnp.log(totals) - spos, count)[:1]
    stats_ref[...] = jnp.zeros(stats_ref.shape, F32)
    stats_ref[0:1, :] = as_rows(totals, count)[:1]
    stats_ref[1:2, :] = as_rows(coef * less, count)[:1]
    stats_ref[2:3, :] = (dev * count + row_ref[...]).astype(F32)


def scores(partner_dev, partner_row, units, pair, got, swapped, size, peers):
    count, embed = units.shape
    return pl.pallas_call(
        functools.partial(scores_kernel, size, peers),
        in_specs=[VMEM] * 6,
        out_shape=[
            shape((count, embed), F32),
            shape((SUB, count), F32),
            shape((1, count), F32),
            shape((size * count, embed), BF16),
            shape((peers * count, embed), BF16),
        ],
        out_specs=[VMEM] * 5,
        compiler_params=params(16),
        cost_estimate=cost(4e8, 1e6),
    )(partner_dev.reshape(1, count), partner_row.reshape(1, count), units, pair, got, swapped)


def upper_kernel(
    size,
    peers,
    group_ref,
    around_ref,
    stats_ref,
    pair_ref,
    got_ref,
    swapped_ref,
    local_ref,
    unit32_ref,
    norm_ref,
    out_ref,
):
    count, _ = local_ref.shape
    coef = SCALE / count
    along, across = crossed(got_ref, swapped_ref, SUB)
    units = group_ref[:count, :]
    keyterm = None
    for i in range(size):
        keys = group_ref[i * count : (i + 1) * count, :]
        expo = exponentials(units, keys, i == 0)
        totals = (across(i) if i else stats_ref[...])[0:1, :]
        term = mm((expo / totals).astype(BF16), keys)
        keyterm = term if keyterm is None else keyterm + term
    mine = lax.axis_index("dp") * count + lax.broadcasted_iota(jnp.int32, (count, count), 0)
    mine = mine.astype(F32)
    chosen = amount = None
    for i in range(peers):
        k, core = i // 2, i % 2
        table = along(k, core) if k else pair_ref[core * SUB : (core + 1) * SUB, :]
        hit = table[2:3, :] == mine
        share = jnp.where(hit, table[1:2, :], 0.0)
        term = mm(jnp.where(hit, 1.0, 0.0).astype(BF16), around_ref[i * count : (i + 1) * count, :])
        chosen = term if chosen is None else chosen + term
        amount = share if amount is None else amount + share
    back = jnp.sum(amount, axis=1, keepdims=True) * chosen
    grad_units = local_ref[...] + coef * keyterm + back
    unit32 = unit32_ref[...]
    tilt = jnp.sum(unit32 * grad_units, axis=1, keepdims=True)
    out_ref[...] = ((grad_units - unit32 * tilt) / norm_ref[:, :1]).astype(BF16)


def upper(group, around, stats, pair, got, swapped, local, unit32, norms, size, peers):
    count, embed = local.shape
    args = [group, around, stats, pair, got, swapped, local, unit32, norms]
    return pl.pallas_call(
        functools.partial(upper_kernel, size, peers),
        in_specs=[VMEM] * len(args),
        out_shape=shape((count, embed), BF16),
        out_specs=VMEM,
        compiler_params=params(16),
        cost_estimate=cost(4e8, 2e6),
    )(*args)


def pre_grads(grad_raw, out_w, slope):
    return (mm_nt(grad_raw, out_w) * slope.astype(F32)).astype(BF16)


def lower_kernel(
    freqs, raw_ref, rscale_ref, in_w, out_w, slope, normed, mixed, spec, g_mix_ref, grad_feat
):
    grad_pre = pre_grads(raw_ref[...], out_w[...], slope[...])
    grad_norm = mm_nt(grad_pre, in_w[...])
    xhat = normed[...].astype(F32)
    mean = jnp.mean(grad_norm, axis=1, keepdims=True)
    tilt = jnp.mean(grad_norm * xhat, axis=1, keepdims=True)
    grad_feat[...] = rscale_ref[:, :1] * (grad_norm - mean - xhat * tilt)
    groups, _, filters = mixed.shape
    half = freqs * SUB

    def one(g, total):
        base = pl.multiple_of(g * SUB, SUB)
        grads = jnp.concatenate(
            [grad_feat[pl.ds(base, SUB), k * filters : (k + 1) * filters] for k in range(freqs)],
            axis=0,
        )
        grad_mixed = jnp.concatenate(
            [mixed[g, :half] * grads, mixed[g, half:] * grads], axis=0
        ).astype(BF16)
        return total + mm_tn(grad_mixed, spec[g])

    total = lax.fori_loop(0, groups, one, jnp.zeros((filters, spec.shape[2]), F32), unroll=16)
    g_mix_ref[...] = total.T


def lower(grad_raw, rscale, in_w, out_w, slope, normed, mixed, spec, freqs):
    filters, lanes = mixed.shape[2], spec.shape[2]
    return pl.pallas_call(
        functools.partial(lower_kernel, freqs),
        in_specs=[VMEM] * 8,
        out_shape=shape((lanes, filters), F32),
        out_specs=VMEM,
        scratch_shapes=[pltpu.VMEM(normed.shape, F32)],
        compiler_params=params(20),
        cost_estimate=cost(1e9, 7e6),
    )(grad_raw, rscale, in_w, out_w, slope, normed, mixed, spec)


def up_to(rows, unit):
    return -(-rows // unit) * unit


class Layout:
    def __init__(self, lanes, filters, feats, width, embed, size, peers):
        self.size, self.peers = size, peers
        self.in_rows = feats // size // peers
        self.out_rows = width // size // peers
        self.mix_rows = lanes // peers
        self.top = up_to(self.in_rows, 16)
        self.strip = max(16, up_to(self.out_rows, 16))
        self.mix_blocks = -(-self.mix_rows // self.strip)
        self.rows = self.top + self.strip
        self.width = width
        assert embed == 128 and filters == 128 and (1 + self.mix_blocks) * 128 <= width

    def mix_parts(self):
        for block in range(self.mix_blocks):
            start = block * self.strip
            yield start, min(self.strip, self.mix_rows - start), slice(128 * (block + 1), 128 * (block + 2))


def weights_kernel(lay, columns, *refs):
    size, peers = lay.size, lay.peers
    pieces, raws, rest = refs[:size], refs[size : 2 * size], refs[2 * size :]
    out_w_ref, mix_ref, keep_ref, away_ref, g_in, g_out = rest
    deep, width, wide = columns
    share = width // size
    for i in range(size):
        raw = raws[i][...]
        grad_pre = pre_grads(raw, out_w_ref[...], pieces[i][:, deep : deep + width])
        term_in = mm_tn(pieces[i][:, :deep], grad_pre)
        term_out = mm_tn(pieces[i][:, deep + width :], raw)
        if i == 0:
            g_in[...] = term_in
            g_out[...] = term_out
        else:
            g_in[...] += term_in
            g_out[...] += term_out
    me = lax.axis_index("dp")
    first = 0 if wide == share else lax.axis_index("blk") * share
    keep_ref[:, lay.top :, :] = jnp.zeros((peers // 2, lay.strip, width), F32)
    away_ref[:, lay.top :, :] = jnp.zeros((peers // 2, lay.strip, width), BF16)
    if lay.top > lay.in_rows:
        keep_ref[:, : lay.top, :] = jnp.zeros((peers // 2, lay.top, width), F32)
        away_ref[:, : lay.top, :] = jnp.zeros((peers // 2, lay.top, width), BF16)
    for slot in range(peers):
        owner = me ^ slot
        target = away_ref if slot & 1 else keep_ref
        at = slot >> 1
        target[at, : lay.in_rows, :] = g_in[pl.ds(owner * lay.in_rows, lay.in_rows), :].astype(target.dtype)
        target[at, lay.top : lay.top + lay.out_rows, :128] = g_out[
            pl.ds(first + owner * lay.out_rows, lay.out_rows), :
        ].astype(target.dtype)
        for start, rows, cols in lay.mix_parts():
            target[at, lay.top : lay.top + rows, cols] = mix_ref[
                pl.ds(owner * lay.mix_rows + start, rows), :
            ].astype(target.dtype)


def weight_grads(lay, columns, pieces, raws, w_out, g_mix):
    deep, width, wide = columns
    block = (lay.peers // 2, lay.rows, lay.width)
    args = [*pieces, *raws, w_out, g_mix]
    return pl.pallas_call(
        functools.partial(weights_kernel, lay, columns),
        in_specs=[VMEM] * len(args),
        out_shape=[shape(block, F32), shape(block, BF16)],
        out_specs=[VMEM] * 2,
        scratch_shapes=[pltpu.VMEM((deep, width), F32), pltpu.VMEM((wide, 128), F32)],
        compiler_params=params(16),
        cost_estimate=cost(6e8, 4e6),
    )(*args)


HALVES = 2


def pair_kernel(keep_ref, got_ref, *out_refs):
    slots, _, width = keep_ref.shape
    part = width // HALVES
    for half in range(HALVES):
        cols = slice(half * part, (half + 1) * part)
        for i in range(slots):
            out_ref = out_refs[half * slots + i]
            total = keep_ref[i, :, cols] + got_ref[i, :, cols].astype(F32)
            out_ref[...] = total.astype(out_ref.dtype)


def pair_sum(keep, got):
    slots, rows, width = keep.shape
    part = (rows, width // HALVES)
    outs = [shape(part, F32)] + [shape(part, BF16)] * (slots - 1)
    sums = pl.pallas_call(
        pair_kernel,
        in_specs=[VMEM] * 2,
        out_shape=outs * HALVES,
        out_specs=[VMEM] * (slots * HALVES),
        compiler_params=params(8),
        cost_estimate=cost(1e6, 2e6),
    )(keep, got)
    return [sums[half * slots : (half + 1) * slots] for half in range(HALVES)]


def total_kernel(own_ref, *refs):
    total = own_ref[...]
    for each in refs[:-1]:
        total = total + each[...].astype(F32)
    refs[-1][...] = total.astype(BF16)


def total_sum(own, got):
    return pl.pallas_call(
        total_kernel,
        in_specs=[VMEM] * (1 + len(got)),
        out_shape=shape(own.shape, BF16),
        out_specs=VMEM,
        compiler_params=params(8),
        cost_estimate=cost(1e6, 1e6),
    )(own, *got)


def finish_kernel(lay, parts, done, fresh, closing, *refs):
    slots = lay.peers // 2
    part_cols = lay.width // HALVES
    part_refs, refs = dict(zip(parts, refs)), refs[len(parts) :]
    g_in_hbm, g_out_hbm, *refs = refs[done:]
    if closing is not None:
        g_mix_hbm, *refs = refs
    stage, strip_stage, mix_stage, sems, strip_sems, mix_sems = refs
    me_blk, me_dp = lax.axis_index("blk"), lax.axis_index("dp")
    copies = []

    def send(kept, slot, target, sem):
        copy = pltpu.make_async_copy(kept.at[slot], target, sem.at[slot])
        copy.start()
        copies.append(copy)

    if closing is not None:
        slot = 0
        for core in range(2):
            for z in range(slots):
                strip = z * lay.rows + lay.top
                owner = me_dp ^ (2 * z + core)
                for start, rows, cols in lay.mix_parts():
                    half, first = divmod(cols.start, part_cols)
                    if half != closing:
                        continue
                    terms = [
                        part_refs[hop, core, half][strip : strip + rows, first : first + 128].astype(F32)
                        for hop in range(lay.size)
                    ]
                    while len(terms) > 1:
                        terms = [terms[t] + terms[t + 1] for t in range(0, len(terms), 2)]
                    mix_stage[slot, :rows, :] = terms[0]
                    copy = pltpu.make_async_copy(
                        mix_stage.at[slot, :rows],
                        g_mix_hbm.at[pl.ds(owner * lay.mix_rows + start, rows), :],
                        mix_sems.at[slot],
                    )
                    copy.start()
                    copies.append(copy)
                    slot += 1
    for n, (hop, core, half) in enumerate(fresh):
        source = part_refs[hop, core, half]
        cols = slice(half * part_cols, (half + 1) * part_cols)
        for z in range(slots):
            slot = n * slots + z
            at = z * lay.rows
            owner = (me_blk ^ hop) * lay.peers + (me_dp ^ (2 * z + core))
            stage[slot] = source[at : at + lay.in_rows, :].astype(F32)
            send(stage, slot, g_in_hbm.at[pl.ds(owner * lay.in_rows, lay.in_rows), cols], sems)
            if half == 0:
                strip = at + lay.top
                strip_stage[slot] = source[strip : strip + lay.out_rows, :128].astype(F32)
                send(
                    strip_stage,
                    slot,
                    g_out_hbm.at[pl.ds(owner * lay.out_rows, lay.out_rows), :],
                    strip_sems,
                )
    for copy in copies:
        copy.wait()


def finish(lay, parts, done, fresh, closing, lanes, feats, width):
    slots = len(fresh) * lay.peers // 2
    outs = [shape((feats, width), F32), shape((width, 128), F32)]
    specs = [ANY, ANY]
    if closing is not None:
        outs.append(shape((lanes, 128), F32))
        specs.append(ANY)
    blocks = lay.peers * lay.mix_blocks
    return pl.pallas_call(
        functools.partial(finish_kernel, lay, tuple(parts), len(done), tuple(fresh), closing),
        in_specs=[VMEM] * len(parts) + [ANY] * len(done),
        out_shape=outs,
        out_specs=specs,
        scratch_shapes=[
            pltpu.VMEM((slots, lay.in_rows, lay.width // HALVES), F32),
            pltpu.VMEM((slots, lay.out_rows, 128), F32),
            pltpu.VMEM((blocks, lay.strip, 128), F32),
            pltpu.SemaphoreType.DMA((slots,)),
            pltpu.SemaphoreType.DMA((slots,)),
            pltpu.SemaphoreType.DMA((blocks,)),
        ],
        input_output_aliases={len(parts) + i: i for i in range(len(done))},
        compiler_params=params(24),
        cost_estimate=cost(1e6, 8e6),
    )(*parts.values(), *done)


def stack_kernel(*refs):
    rows = refs[0].shape[0]
    for i, each in enumerate(refs[:-1]):
        refs[-1][i * rows : (i + 1) * rows, :] = each[...]


def stack(blocks):
    rows, width = blocks[0].shape
    return pl.pallas_call(
        stack_kernel,
        in_specs=[VMEM] * len(blocks),
        out_shape=shape((len(blocks) * rows, width), blocks[0].dtype),
        out_specs=VMEM,
        compiler_params=params(8),
        cost_estimate=cost(1e3, 1e5),
    )(*blocks)


def swap(block, axis, bit):
    size = lax.axis_size(axis)
    return lax.ppermute(block, axis, [(src, src ^ bit) for src in range(size)])


def spread(block, axis, hops):
    return [block] + [swap(block, axis, hop) for hop in hops]


def on_device(patches, w_mix, w_in, w_out, partner_dev, partner_row):
    count, _, lanes = patches.shape
    filters = w_mix.shape[1]
    feats, width = w_in.shape
    embed = w_out.shape[1]
    freqs = feats // filters
    size, peers = lax.axis_size("blk"), lax.axis_size("dp")
    assert size & (size - 1) == 0 and peers & (peers - 1) == 0 and peers > 1
    across, along = range(1, size), range(2, peers, 2)
    single = [hop for hop in across if hop & (hop - 1) == 0]
    several = [hop for hop in across if hop & (hop - 1)]
    columns = piece_columns(feats, width, size)
    lay = Layout(lanes, filters, feats, width, embed, size, peers)

    *early, spec, mixed, normed, in_w, out_w, slope, units, unit32, norms, rscale = encode(
        patches, w_mix, w_in, w_out, size
    )
    other = swap(units, "dp", 1)
    pair = pair_up(units, other)
    got = stack(lax.optimization_barrier(cross(pair)))
    factors = {hop: swap(early[hop], "blk", hop) for hop in single}
    swapped = swap(got, "dp", 1)
    local, stats, loss, group, around = scores(
        partner_dev, partner_row, units, pair, got, swapped, size, peers
    )
    other = swap(stats, "dp", 1)
    pair = pair_up(stats, other)
    got = stack(lax.optimization_barrier(cross(pair)))
    factors.update({hop: swap(early[hop], "blk", hop) for hop in several})
    factors = [early[0]] + [factors[hop] for hop in across]
    swapped = swap(got, "dp", 1)
    grad_raw = upper(group, around, stats, pair, got, swapped, local, unit32, norms, size, peers)
    raws = spread(grad_raw, "blk", across)
    g_mix = lower(grad_raw, rscale, in_w, out_w, slope, normed, mixed, spec, freqs)
    keep, away = weight_grads(lay, columns, factors, raws, out_w, g_mix)
    got = swap(away, "dp", 1)
    planes = {}
    for half, (own, *sends) in enumerate(pair_sum(keep, got)):
        got = [swap(block, "dp", hop) for block, hop in zip(sends, along)]
        share = total_sum(own, got)
        shares = spread(share, "dp", along)
        planes[0, half] = stack(shares)
        for hop in single:
            planes[hop, half] = swap(planes[0, half], "blk", hop)
        for hop in several:
            bit = hop & -hop if half else 1 << (hop.bit_length() - 1)
            planes[hop, half] = swap(planes[hop ^ bit, half], "blk", bit)
    parts, done = {}, []
    stages = [[(0, 0), (0, 1)], [(hop, 0) for hop in single], [(hop, 1) for hop in single]]
    stages += [[(hop, half) for hop in several] for half in range(HALVES)]
    stages = [stage for stage in stages if stage]
    for order, stage in enumerate(stages):
        fresh = {}
        for hop, half in stage:
            fresh[hop, 0, half] = planes[hop, half]
            fresh[hop, 1, half] = swap(planes[hop, half], "dp", 1)
        parts.update(fresh)
        closing = order - len(stages) + HALVES
        taken = fresh
        if closing >= 0:
            taken = {part: block for part, block in parts.items() if part[2] == closing}
        done = finish(
            lay, taken, done, fresh, closing if closing >= 0 else None, lanes, feats, width
        )
    g_in, g_out, g_mix = done
    return (loss.reshape(count), g_mix, g_in, g_out)


def solution(mesh):
    placed = (P(("blk", "dp"), None, None), P(), P(), P(), P(("blk", "dp")), P(("blk", "dp")))
    return jax.shard_map(
        on_device,
        mesh=mesh,
        in_specs=placed,
        out_specs=(P(("blk", "dp")), P(), P(), P()),
        check_vma=False,
    )
```

```python
import functools
import math

import jax
import jax.numpy as jnp
import numpy as np
from jax import lax
from jax.experimental import pallas as pl
from jax.experimental.pallas import tpu as pltpu
from jax.sharding import PartitionSpec as P


SCALE = 10.0
SUB = 8
BF16 = jnp.bfloat16
F32 = jnp.float32
VMEM = pl.BlockSpec(memory_space=pltpu.VMEM)
ANY = pl.BlockSpec(memory_space=pl.ANY)


def shape(dims, dtype):
    return jax.ShapeDtypeStruct(tuple(dims), dtype)


def hbm(value):
    return pltpu.with_memory_space_constraint(value, pltpu.MemorySpace.HBM)


def mm(left, right):
    return jnp.dot(left, right, preferred_element_type=F32)


def mm_nt(left, right):
    return lax.dot_general(left, right, (((1,), (1,)), ((), ())), preferred_element_type=F32)


def mm_tn(left, right):
    return lax.dot_general(left, right, (((0,), (0,)), ((), ())), preferred_element_type=F32)


def params(mib):
    return pltpu.CompilerParams(vmem_limit_bytes=mib << 20)


def cost(flops, nbytes):
    return pl.CostEstimate(flops=int(flops), bytes_accessed=int(nbytes), transcendentals=0)


def angle_basis(length, freqs):
    phase = np.mod(np.outer(np.arange(freqs), np.arange(length)), length).astype(np.float32)
    phase = phase * np.float32(2.0 * math.pi / length)
    table = np.concatenate([np.cos(phase), -np.sin(phase)], axis=0).astype(np.float32)
    basis = np.einsum("ka,pq->kpqa", table, np.eye(SUB, dtype=np.float32))
    return jnp.asarray(basis.reshape(2 * freqs * SUB, SUB * length), BF16)


def encode_kernel(freqs, size, rounds, patch_hbm, basis_hbm, mix_hbm, out_hbm, in_hbm, *rest):
    piece_hbms, rest = rest[:size], rest[size:]
    spec, mixed, normed, in_w, out_w, slope, units_ref, unit32_ref, norm_ref, rscale_ref, *rest = rest
    patches, basis, mix, feat, hidden, *sems = rest
    table_sems, patch_sems, out_sems = sems
    count, length, lanes = patches.shape
    filters = mix.shape[1]
    half = freqs * SUB
    per = count // rounds
    groups = per // SUB

    def table(i, source, target):
        return pltpu.make_async_copy(source, target, table_sems.at[i])

    tables = [
        table(i, *pair)
        for i, pair in enumerate(
            [(basis_hbm, basis), (mix_hbm, mix), (in_hbm, in_w), (out_hbm, out_w)]
        )
    ]

    def fetch(r):
        rows = pl.ds(r * per, per)
        return pltpu.make_async_copy(patch_hbm.at[rows], patches.at[rows], patch_sems.at[r])

    tables[0].start()
    fetch(0).start()
    tables[1].start()
    for r in range(1, rounds):
        fetch(r).start()
    tables[2].start()
    tables[3].start()
    tables[0].wait()
    tables[1].wait()

    def one(r, carry):
        fetch(r).wait()
        for s in range(groups):
            g = r * groups + s
            base = pl.multiple_of(g * SUB, SUB)
            block = patches[pl.ds(base, SUB)].reshape(SUB * length, lanes)
            part = mm(basis[...], block).astype(BF16)
            spec[g] = part
            both = mm(part, mix[...])
            real_part, imag_part = both[:half], both[half:]
            powers = real_part * real_part + imag_part * imag_part
            share = 2.0 / (1.0 + powers)
            mixed[g, :half] = real_part * share
            mixed[g, half:] = imag_part * share
            piece = jnp.log1p(powers)
            for k in range(freqs):
                feat[pl.ds(base, SUB), k * filters : (k + 1) * filters] = piece[
                    k * SUB : (k + 1) * SUB
                ]
        return carry

    lax.fori_loop(0, rounds, one, 0)
    features = feat[...]
    removed = features - jnp.mean(features, axis=1, keepdims=True)
    rscale = lax.rsqrt(jnp.mean(removed * removed, axis=1, keepdims=True) + 1e-05)
    normed[...] = (removed * rscale).astype(BF16)
    rscale_ref[...] = jnp.broadcast_to(rscale, rscale_ref.shape)
    deep, width, wide = piece_columns(normed.shape[1], hidden.shape[1], size)
    me = lax.axis_index("blk")
    outs = []
    for i, piece_hbm in enumerate(piece_hbms):
        columns = pl.ds(pl.multiple_of((me ^ i) * deep, 128), deep)
        outs.append(
            pltpu.make_async_copy(
                normed.at[:, columns], piece_hbm.at[:, :deep], out_sems.at[len(outs)]
            )
        )
    for each in outs:
        each.start()
    tables[2].wait()
    preact = mm(normed[...], in_w[...])
    sigm = jax.nn.sigmoid(preact)
    hidden[...] = (preact * sigm).astype(BF16)
    slope[...] = (sigm * (1.0 + preact * (1.0 - sigm))).astype(BF16)
    late = []
    for i, piece_hbm in enumerate(piece_hbms):
        if wide == hidden.shape[1]:
            columns = pl.ds(0, wide)
        else:
            columns = pl.ds(pl.multiple_of((me ^ i) * wide, 128), wide)
        for source, target in (
            (slope, piece_hbm.at[:, deep : deep + width]),
            (hidden.at[:, columns], piece_hbm.at[:, deep + width :]),
        ):
            late.append(
                pltpu.make_async_copy(source, target, out_sems.at[len(outs) + len(late)])
            )
    for each in late:
        each.start()
    tables[3].wait()
    raw = mm(hidden[...], out_w[...])
    norms = jnp.sqrt(jnp.sum(raw * raw, axis=1, keepdims=True) + 1e-06)
    norm_ref[...] = jnp.broadcast_to(norms, norm_ref.shape)
    unit32 = raw / norms
    unit32_ref[...] = unit32
    units_ref[...] = unit32.astype(BF16)
    for each in outs + late:
        each.wait()


def piece_columns(feats, width, size):
    wide = width // size
    return feats // size, width, wide if wide % 128 == 0 else width


def encode(patches, w_mix, w_in, w_out, size):
    count, length, lanes = patches.shape
    filters = w_mix.shape[1]
    feats, width = w_in.shape
    embed = w_out.shape[1]
    freqs = feats // filters
    rounds = 4
    assert count % (rounds * SUB) == 0
    groups = count // SUB
    rows = 2 * freqs * SUB
    piece = (count, sum(piece_columns(feats, width, size)))
    kept = [pltpu.MemorySpace.HBM(piece, BF16)] * size
    near = [
        shape((groups, rows, lanes), BF16),
        shape((groups, rows, filters), F32),
        shape((count, feats), BF16),
        shape(w_in.shape, BF16),
        shape(w_out.shape, BF16),
        shape((count, width), BF16),
        shape((count, embed), BF16),
        shape((count, embed), F32),
        shape((count, 128), F32),
        shape((count, 128), F32),
    ]
    return pl.pallas_call(
        functools.partial(encode_kernel, freqs, size, rounds),
        in_specs=[ANY] * 5,
        out_shape=kept + near,
        out_specs=[ANY] * len(kept) + [VMEM] * len(near),
        scratch_shapes=[
            pltpu.VMEM(patches.shape, BF16),
            pltpu.VMEM((rows, SUB * length), BF16),
            pltpu.VMEM(w_mix.shape, BF16),
            pltpu.VMEM((count, feats), F32),
            pltpu.VMEM((count, width), BF16),
            pltpu.SemaphoreType.DMA((4,)),
            pltpu.SemaphoreType.DMA((rounds,)),
            pltpu.SemaphoreType.DMA((3 * size,)),
        ],
        compiler_params=params(24),
        cost_estimate=cost(3e9, 14e6),
    )(*map(hbm, (patches, angle_basis(length, freqs), w_mix, w_out, w_in)))


def exponentials(units, keys, own):
    expo = jnp.exp(SCALE * mm_nt(units, keys))
    if own:
        row = lax.broadcasted_iota(jnp.int32, expo.shape, 0)
        col = lax.broadcasted_iota(jnp.int32, expo.shape, 1)
        expo = jnp.where(row == col, 0.0, expo)
    return expo


def pair_up_kernel(own_ref, other_ref, out_ref):
    rows = own_ref.shape[0]
    own, other = own_ref[...], other_ref[...]
    first = lax.axis_index("dp") % 2 == 0
    out_ref[:rows, :] = jnp.where(first, own, other)
    out_ref[rows:, :] = jnp.where(first, other, own)


def pair_up(own, other):
    rows, width = own.shape
    return pl.pallas_call(
        pair_up_kernel,
        in_specs=[VMEM] * 2,
        out_shape=shape((2 * rows, width), own.dtype),
        out_specs=VMEM,
        compiler_params=params(8),
        cost_estimate=cost(1e3, 1e5),
    )(own, other)


def cross(pair):
    size, peers = lax.axis_size("blk"), lax.axis_size("dp")
    got = []
    for k in range(1, max(size, peers // 2)):
        routes = []
        for blk in range(size):
            for dp in range(peers):
                if dp % 2 == 0 and 2 * k < peers:
                    routes.append((blk * peers + dp, blk * peers + (dp ^ (2 * k))))
                if dp % 2 == 1 and k < size:
                    routes.append((blk * peers + dp, (blk ^ k) * peers + dp))
        got.append(lax.ppermute(pair, ("blk", "dp"), routes))
    return got


def crossed(got_ref, swapped_ref, rows):
    first = lax.axis_index("dp") % 2 == 0

    def along(k, core):
        at = (2 * (k - 1) + core) * rows
        return jnp.where(first, got_ref[at : at + rows, :], swapped_ref[at : at + rows, :])

    def across(k):
        at = 2 * (k - 1) * rows
        low = jnp.where(first, swapped_ref[at : at + rows, :], got_ref[at + rows : at + 2 * rows, :])
        return low

    return along, across


def as_rows(column, count):
    return jnp.broadcast_to(column, (column.shape[0], count)).T


def scores_kernel(
    size,
    peers,
    dev_ref,
    row_ref,
    units_ref,
    pair_ref,
    got_ref,
    swapped_ref,
    local_ref,
    stats_ref,
    loss_ref,
    group_ref,
    around_ref,
):
    units = units_ref[...]
    count = units.shape[0]
    along, across = crossed(got_ref, swapped_ref, count)
    zneg = numer = None
    for i in range(size):
        keys = across(i) if i else units
        group_ref[i * count : (i + 1) * count, :] = keys
        expo = exponentials(units, keys, i == 0)
        total = jnp.sum(expo, axis=1, keepdims=True)
        term = mm(expo.astype(BF16), keys)
        zneg = total if zneg is None else zneg + total
        numer = term if numer is None else numer + term
    me = lax.axis_index("dp")
    dev = dev_ref[...]
    place = (2 * ((dev ^ me) >> 1) + (dev & 1)) * count + row_ref[...]
    place = jnp.broadcast_to(place.astype(F32), (count, count)).T
    lane = lax.broadcasted_iota(jnp.int32, (count, count), 1).astype(F32)
    positive = None
    for i in range(peers):
        k, core = i // 2, i % 2
        source = along(k, core) if k else pair_ref[core * count : (core + 1) * count, :]
        around_ref[i * count : (i + 1) * count, :] = source
        hit = jnp.where(place - float(i * count) == lane, 1.0, 0.0).astype(BF16)
        term = mm(hit, source)
        positive = term if positive is None else positive + term
    spos = SCALE * jnp.sum(units.astype(F32) * positive, axis=1, keepdims=True)
    top = jnp.exp(spos)
    totals = top + zneg
    less = top / totals - 1.0
    coef = SCALE / count
    local_ref[...] = coef * (less * positive + numer / totals)
    loss_ref[...] = as_rows(jnp.log(totals) - spos, count)[:1]
    stats_ref[...] = jnp.zeros(stats_ref.shape, F32)
    stats_ref[0:1, :] = as_rows(totals, count)[:1]
    stats_ref[1:2, :] = as_rows(coef * less, count)[:1]
    stats_ref[2:3, :] = (dev * count + row_ref[...]).astype(F32)


def scores(partner_dev, partner_row, units, pair, got, swapped, size, peers):
    count, embed = units.shape
    return pl.pallas_call(
        functools.partial(scores_kernel, size, peers),
        in_specs=[VMEM] * 6,
        out_shape=[
            shape((count, embed), F32),
            shape((SUB, count), F32),
            shape((1, count), F32),
            shape((size * count, embed), BF16),
            shape((peers * count, embed), BF16),
        ],
        out_specs=[VMEM] * 5,
        compiler_params=params(16),
        cost_estimate=cost(4e8, 1e6),
    )(partner_dev.reshape(1, count), partner_row.reshape(1, count), units, pair, got, swapped)


def upper_kernel(
    size,
    peers,
    group_ref,
    around_ref,
    stats_ref,
    pair_ref,
    got_ref,
    swapped_ref,
    local_ref,
    unit32_ref,
    norm_ref,
    out_ref,
):
    count, _ = local_ref.shape
    coef = SCALE / count
    along, across = crossed(got_ref, swapped_ref, SUB)
    units = group_ref[:count, :]
    keyterm = None
    for i in range(size):
        keys = group_ref[i * count : (i + 1) * count, :]
        expo = exponentials(units, keys, i == 0)
        totals = (across(i) if i else stats_ref[...])[0:1, :]
        term = mm((expo / totals).astype(BF16), keys)
        keyterm = term if keyterm is None else keyterm + term
    mine = lax.axis_index("dp") * count + lax.broadcasted_iota(jnp.int32, (count, count), 0)
    mine = mine.astype(F32)
    chosen = amount = None
    for i in range(peers):
        k, core = i // 2, i % 2
        table = along(k, core) if k else pair_ref[core * SUB : (core + 1) * SUB, :]
        hit = table[2:3, :] == mine
        share = jnp.where(hit, table[1:2, :], 0.0)
        term = mm(jnp.where(hit, 1.0, 0.0).astype(BF16), around_ref[i * count : (i + 1) * count, :])
        chosen = term if chosen is None else chosen + term
        amount = share if amount is None else amount + share
    back = jnp.sum(amount, axis=1, keepdims=True) * chosen
    grad_units = local_ref[...] + coef * keyterm + back
    unit32 = unit32_ref[...]
    tilt = jnp.sum(unit32 * grad_units, axis=1, keepdims=True)
    out_ref[...] = ((grad_units - unit32 * tilt) / norm_ref[:, :1]).astype(BF16)


def upper(group, around, stats, pair, got, swapped, local, unit32, norms, size, peers):
    count, embed = local.shape
    args = [group, around, stats, pair, got, swapped, local, unit32, norms]
    return pl.pallas_call(
        functools.partial(upper_kernel, size, peers),
        in_specs=[VMEM] * len(args),
        out_shape=shape((count, embed), BF16),
        out_specs=VMEM,
        compiler_params=params(16),
        cost_estimate=cost(4e8, 2e6),
    )(*args)


def pre_grads(grad_raw, out_w, slope):
    return (mm_nt(grad_raw, out_w) * slope.astype(F32)).astype(BF16)


def lower_kernel(
    freqs, raw_ref, rscale_ref, in_w, out_w, slope, normed, mixed, spec, g_mix_ref, grad_feat
):
    grad_pre = pre_grads(raw_ref[...], out_w[...], slope[...])
    grad_norm = mm_nt(grad_pre, in_w[...])
    xhat = normed[...].astype(F32)
    mean = jnp.mean(grad_norm, axis=1, keepdims=True)
    tilt = jnp.mean(grad_norm * xhat, axis=1, keepdims=True)
    grad_feat[...] = rscale_ref[:, :1] * (grad_norm - mean - xhat * tilt)
    groups, _, filters = mixed.shape
    half = freqs * SUB

    def one(g, total):
        base = pl.multiple_of(g * SUB, SUB)
        grads = jnp.concatenate(
            [grad_feat[pl.ds(base, SUB), k * filters : (k + 1) * filters] for k in range(freqs)],
            axis=0,
        )
        grad_mixed = jnp.concatenate(
            [mixed[g, :half] * grads, mixed[g, half:] * grads], axis=0
        ).astype(BF16)
        return total + mm_tn(grad_mixed, spec[g])

    total = lax.fori_loop(0, groups, one, jnp.zeros((filters, spec.shape[2]), F32), unroll=16)
    g_mix_ref[...] = total.T


def lower(grad_raw, rscale, in_w, out_w, slope, normed, mixed, spec, freqs):
    filters, lanes = mixed.shape[2], spec.shape[2]
    return pl.pallas_call(
        functools.partial(lower_kernel, freqs),
        in_specs=[VMEM] * 8,
        out_shape=shape((lanes, filters), F32),
        out_specs=VMEM,
        scratch_shapes=[pltpu.VMEM(normed.shape, F32)],
        compiler_params=params(20),
        cost_estimate=cost(1e9, 7e6),
    )(grad_raw, rscale, in_w, out_w, slope, normed, mixed, spec)


def up_to(rows, unit):
    return -(-rows // unit) * unit


class Layout:
    def __init__(self, lanes, filters, feats, width, embed, size, peers):
        self.size, self.peers = size, peers
        self.in_rows = feats // size // peers
        self.out_rows = width // size // peers
        self.mix_rows = lanes // peers
        self.top = up_to(self.in_rows, 16)
        self.strip = max(16, up_to(self.out_rows, 16))
        self.mix_blocks = -(-self.mix_rows // self.strip)
        self.rows = self.top + self.strip
        self.width = width
        assert embed == 128 and filters == 128 and (1 + self.mix_blocks) * 128 <= width

    def mix_parts(self):
        for block in range(self.mix_blocks):
            start = block * self.strip
            yield start, min(self.strip, self.mix_rows - start), slice(128 * (block + 1), 128 * (block + 2))


def weights_kernel(lay, columns, *refs):
    size, peers = lay.size, lay.peers
    pieces, raws, rest = refs[:size], refs[size : 2 * size], refs[2 * size :]
    out_w_ref, mix_ref, keep_ref, away_ref, g_in, g_out = rest
    deep, width, wide = columns
    share = width // size
    for i in range(size):
        raw = raws[i][...]
        grad_pre = pre_grads(raw, out_w_ref[...], pieces[i][:, deep : deep + width])
        term_in = mm_tn(pieces[i][:, :deep], grad_pre)
        term_out = mm_tn(pieces[i][:, deep + width :], raw)
        if i == 0:
            g_in[...] = term_in
            g_out[...] = term_out
        else:
            g_in[...] += term_in
            g_out[...] += term_out
    me = lax.axis_index("dp")
    first = 0 if wide == share else lax.axis_index("blk") * share
    keep_ref[:, lay.top :, :] = jnp.zeros((peers // 2, lay.strip, width), F32)
    away_ref[:, lay.top :, :] = jnp.zeros((peers // 2, lay.strip, width), BF16)
    if lay.top > lay.in_rows:
        keep_ref[:, : lay.top, :] = jnp.zeros((peers // 2, lay.top, width), F32)
        away_ref[:, : lay.top, :] = jnp.zeros((peers // 2, lay.top, width), BF16)
    for slot in range(peers):
        owner = me ^ slot
        target = away_ref if slot & 1 else keep_ref
        at = slot >> 1
        target[at, : lay.in_rows, :] = g_in[pl.ds(owner * lay.in_rows, lay.in_rows), :].astype(target.dtype)
        target[at, lay.top : lay.top + lay.out_rows, :128] = g_out[
            pl.ds(first + owner * lay.out_rows, lay.out_rows), :
        ].astype(target.dtype)
        for start, rows, cols in lay.mix_parts():
            target[at, lay.top : lay.top + rows, cols] = mix_ref[
                pl.ds(owner * lay.mix_rows + start, rows), :
            ].astype(target.dtype)


def weight_grads(lay, columns, pieces, raws, w_out, g_mix):
    deep, width, wide = columns
    block = (lay.peers // 2, lay.rows, lay.width)
    args = [*pieces, *raws, w_out, g_mix]
    return pl.pallas_call(
        functools.partial(weights_kernel, lay, columns),
        in_specs=[VMEM] * len(args),
        out_shape=[shape(block, F32), shape(block, BF16)],
        out_specs=[VMEM] * 2,
        scratch_shapes=[pltpu.VMEM((deep, width), F32), pltpu.VMEM((wide, 128), F32)],
        compiler_params=params(16),
        cost_estimate=cost(6e8, 4e6),
    )(*args)


HALVES = 2


def pair_kernel(keep_ref, got_ref, *out_refs):
    slots, _, width = keep_ref.shape
    part = width // HALVES
    for half in range(HALVES):
        cols = slice(half * part, (half + 1) * part)
        for i in range(slots):
            out_ref = out_refs[half * slots + i]
            total = keep_ref[i, :, cols] + got_ref[i, :, cols].astype(F32)
            out_ref[...] = total.astype(out_ref.dtype)


def pair_sum(keep, got):
    slots, rows, width = keep.shape
    part = (rows, width // HALVES)
    outs = [shape(part, F32)] + [shape(part, BF16)] * (slots - 1)
    sums = pl.pallas_call(
        pair_kernel,
        in_specs=[VMEM] * 2,
        out_shape=outs * HALVES,
        out_specs=[VMEM] * (slots * HALVES),
        compiler_params=params(8),
        cost_estimate=cost(1e6, 2e6),
    )(keep, got)
    return [sums[half * slots : (half + 1) * slots] for half in range(HALVES)]


def total_kernel(own_ref, *refs):
    total = own_ref[...]
    for each in refs[:-1]:
        total = total + each[...].astype(F32)
    refs[-1][...] = total.astype(BF16)


def total_sum(own, got):
    return pl.pallas_call(
        total_kernel,
        in_specs=[VMEM] * (1 + len(got)),
        out_shape=shape(own.shape, BF16),
        out_specs=VMEM,
        compiler_params=params(8),
        cost_estimate=cost(1e6, 1e6),
    )(own, *got)


def finish_kernel(lay, parts, done, fresh, closing, *refs):
    slots = lay.peers // 2
    part_cols = lay.width // HALVES
    part_refs, refs = dict(zip(parts, refs)), refs[len(parts) :]
    if done:
        refs = refs[2:]
    g_in_hbm, g_out_hbm, *refs = refs
    if closing:
        g_mix_hbm, *refs = refs
    stage, strip_stage, mix_stage, sems, strip_sems, mix_sems = refs
    me_blk, me_dp = lax.axis_index("blk"), lax.axis_index("dp")
    copies = []

    def send(kept, slot, target, sem):
        copy = pltpu.make_async_copy(kept.at[slot], target, sem.at[slot])
        copy.start()
        copies.append(copy)

    for n, (hop, core, half) in enumerate(fresh):
        source = part_refs[hop, core, half]
        cols = slice(half * part_cols, (half + 1) * part_cols)
        for z in range(slots):
            slot = n * slots + z
            at = z * lay.rows
            owner = (me_blk ^ hop) * lay.peers + (me_dp ^ (2 * z + core))
            stage[slot] = source[at : at + lay.in_rows, :].astype(F32)
            send(stage, slot, g_in_hbm.at[pl.ds(owner * lay.in_rows, lay.in_rows), cols], sems)
            if half == 0:
                strip = at + lay.top
                strip_stage[slot] = source[strip : strip + lay.out_rows, :128].astype(F32)
                send(
                    strip_stage,
                    slot,
                    g_out_hbm.at[pl.ds(owner * lay.out_rows, lay.out_rows), :],
                    strip_sems,
                )
    if closing:
        slot = 0
        for core in range(2):
            for z in range(slots):
                strip = z * lay.rows + lay.top
                owner = me_dp ^ (2 * z + core)
                for start, rows, cols in lay.mix_parts():
                    half, first = divmod(cols.start, part_cols)
                    terms = [
                        part_refs[hop, core, half][strip : strip + rows, first : first + 128].astype(F32)
                        for hop in range(lay.size)
                    ]
                    while len(terms) > 1:
                        terms = [terms[t] + terms[t + 1] for t in range(0, len(terms), 2)]
                    mix_stage[slot, :rows, :] = terms[0]
                    row = owner * lay.mix_rows + start
                    copy = pltpu.make_async_copy(
                        mix_stage.at[slot, :rows], g_mix_hbm.at[pl.ds(row, rows), :], mix_sems.at[slot]
                    )
                    copy.start()
                    copies.append(copy)
                    slot += 1
    for copy in copies:
        copy.wait()


def finish(lay, parts, done, fresh, closing, lanes, feats, width):
    slots = len(fresh) * lay.peers // 2
    outs = [shape((feats, width), F32), shape((width, 128), F32)]
    specs = [ANY, ANY]
    if closing:
        outs.append(shape((lanes, 128), F32))
        specs.append(ANY)
    blocks = lay.peers * lay.mix_blocks
    return pl.pallas_call(
        functools.partial(finish_kernel, lay, tuple(parts), bool(done), tuple(fresh), closing),
        in_specs=[VMEM] * len(parts) + [ANY] * len(done),
        out_shape=outs,
        out_specs=specs,
        scratch_shapes=[
            pltpu.VMEM((slots, lay.in_rows, lay.width // HALVES), F32),
            pltpu.VMEM((slots, lay.out_rows, 128), F32),
            pltpu.VMEM((blocks, lay.strip, 128), F32),
            pltpu.SemaphoreType.DMA((slots,)),
            pltpu.SemaphoreType.DMA((slots,)),
            pltpu.SemaphoreType.DMA((blocks,)),
        ],
        input_output_aliases={len(parts) + i: i for i in range(len(done))},
        compiler_params=params(24),
        cost_estimate=cost(1e6, 8e6),
    )(*parts.values(), *done)


def stack_kernel(*refs):
    rows = refs[0].shape[0]
    for i, each in enumerate(refs[:-1]):
        refs[-1][i * rows : (i + 1) * rows, :] = each[...]


def stack(blocks):
    rows, width = blocks[0].shape
    return pl.pallas_call(
        stack_kernel,
        in_specs=[VMEM] * len(blocks),
        out_shape=shape((len(blocks) * rows, width), blocks[0].dtype),
        out_specs=VMEM,
        compiler_params=params(8),
        cost_estimate=cost(1e3, 1e5),
    )(*blocks)


def swap(block, axis, bit):
    size = lax.axis_size(axis)
    return lax.ppermute(block, axis, [(src, src ^ bit) for src in range(size)])


def spread(block, axis, hops):
    return [block] + [swap(block, axis, hop) for hop in hops]


def on_device(patches, w_mix, w_in, w_out, partner_dev, partner_row):
    count, _, lanes = patches.shape
    filters = w_mix.shape[1]
    feats, width = w_in.shape
    embed = w_out.shape[1]
    freqs = feats // filters
    size, peers = lax.axis_size("blk"), lax.axis_size("dp")
    assert size & (size - 1) == 0 and peers & (peers - 1) == 0 and peers > 1
    across, along = range(1, size), range(2, peers, 2)
    single = [hop for hop in across if hop & (hop - 1) == 0]
    several = [hop for hop in across if hop & (hop - 1)]
    columns = piece_columns(feats, width, size)
    lay = Layout(lanes, filters, feats, width, embed, size, peers)

    *early, spec, mixed, normed, in_w, out_w, slope, units, unit32, norms, rscale = encode(
        patches, w_mix, w_in, w_out, size
    )
    other = swap(units, "dp", 1)
    pair = pair_up(units, other)
    got = stack(lax.optimization_barrier(cross(pair)))
    factors = {hop: swap(early[hop], "blk", hop) for hop in single}
    swapped = swap(got, "dp", 1)
    local, stats, loss, group, around = scores(
        partner_dev, partner_row, units, pair, got, swapped, size, peers
    )
    other = swap(stats, "dp", 1)
    pair = pair_up(stats, other)
    got = stack(lax.optimization_barrier(cross(pair)))
    factors.update({hop: swap(early[hop], "blk", hop) for hop in several})
    factors = [early[0]] + [factors[hop] for hop in across]
    swapped = swap(got, "dp", 1)
    grad_raw = upper(group, around, stats, pair, got, swapped, local, unit32, norms, size, peers)
    raws = spread(grad_raw, "blk", across)
    g_mix = lower(grad_raw, rscale, in_w, out_w, slope, normed, mixed, spec, freqs)
    keep, away = weight_grads(lay, columns, factors, raws, out_w, g_mix)
    got = swap(away, "dp", 1)
    planes = {}
    for half, (own, *sends) in enumerate(pair_sum(keep, got)):
        got = [swap(block, "dp", hop) for block, hop in zip(sends, along)]
        share = total_sum(own, got)
        shares = spread(share, "dp", along)
        planes[0, half] = stack(shares)
        for hop in single:
            planes[hop, half] = swap(planes[0, half], "blk", hop)
        for hop in several:
            bit = hop & -hop if half else 1 << (hop.bit_length() - 1)
            planes[hop, half] = swap(planes[hop ^ bit, half], "blk", bit)
    parts, done = {}, []
    stages = [[(0, 0), (0, 1)], [(hop, 0) for hop in single], [(hop, 1) for hop in single]]
    stages += [[(hop, half) for hop in several] for half in range(HALVES)]
    stages = [stage for stage in stages if stage]
    for order, stage in enumerate(stages):
        fresh = {}
        for hop, half in stage:
            fresh[hop, 0, half] = planes[hop, half]
            fresh[hop, 1, half] = swap(planes[hop, half], "dp", 1)
        parts.update(fresh)
        last = order == len(stages) - 1
        done = finish(
            lay, parts if last else fresh, done, fresh, last, lanes, feats, width
        )
    g_in, g_out, g_mix = done
    return (loss.reshape(count), g_mix, g_in, g_out)


def solution(mesh):
    placed = (P(("blk", "dp"), None, None), P(), P(), P(), P(("blk", "dp")), P(("blk", "dp")))
    return jax.shard_map(
        on_device,
        mesh=mesh,
        in_specs=placed,
        out_specs=(P(("blk", "dp")), P(), P(), P()),
        check_vma=False,
    )
```
